32 devices in a mesh: runs: 2 (over x), brick: 16 (over z, y, core).
Axes of the slice: x: 2, y: 2, z: 4, core: 2. Of those that a mesh axis runs over, the one named last changes fastest.
Arguments:
- grid: float32 [3, 8388608], P(None, ('runs', 'brick')), parts along dimension 1, may hold values from 0.2 to 4
- distribution: float32 [64, 16384], P(None, ('runs', 'brick')), parts along dimension 1, may hold values from 0.02 to 1
- owner_ids: int32 [16384, 1], P(('runs', 'brick')), parts along dimension 0, may hold values from 0 to 15; in each aligned block of 512 rows (0 to 511, 512 to 1023, ...) at most 64 rows name the same one
- coords: int32 [3, 16384], P(None, ('runs', 'brick')), parts along dimension 1, may hold values from 0 to 62
- fracs: float32 [3, 16384], P(None, ('runs', 'brick')), parts along dimension 1, may hold values from 0 to 1
- counts: int32 [16384], P(('runs', 'brick')), parts along dimension 0, may hold values from 1 to 4
- kernel: float32 [64, 64], replicated, may hold values from 0.002 to 0.2
- redist: float32 [64, 64], replicated, may hold values from 0.001 to 0.05
- shatter: float32 [64, 64], replicated, may hold values from 0.001 to 0.05
Outputs:
- updated: float32 [64, 16384], P(None, ('runs', 'brick')), parts along dimension 1
The draws below stay inside these ranges and needn't reach their ends.
There are 2 independent parts, one for each index of `runs`. The reference program is written for one: setup_inputs(seed, part) draws one part's arguments, and reference() takes and returns one part's arrays. A program takes and returns all parts, laid end to end along the dimension named above; an argument that names none is the same for every part. Nothing has to cross between parts.
Inputs may be any that keep to these rules, and one draw needn't show every extreme that they name: `owner_ids`: in the rows of one device at most 64 tracers name one brick, a bound that some block reaches of them.
All inputs are finite; a program needn't handle non-finite values.
Results may differ from the reference program's by a relative error of at most 0.0001.
Values sent between devices are 32-bit elements; how exact they have to be, the bound alone decides.
A program may use at most 256 MiB of HBM per device.

```python
import math
import jax
import jax.numpy as jnp
import numpy as np
from jax import lax

BINS = 64
BS = 64
TR_DEV = 512
CAP = 64
CELLS = 262144
TRACERS = 8192
N_BRICK = 16


def touch_ends(entries, key, smallest, top_value):
    place = [jax.random.randint(jax.random.fold_in(key, axis), (), 0, length) for axis, length in enumerate(entries.shape)]
    main_axis = entries.shape.index(max(entries.shape))
    neighbour = place[:main_axis] + [(place[main_axis] + 1) % entries.shape[main_axis]] + place[main_axis + 1:]
    return entries.at[tuple(place)].set(smallest).at[tuple(neighbour)].set(top_value)


def levels(stream_key, extent, split, least, top_value):
    factor_of = 1.0
    for position, shards_of in split:
        draws = jax.random.uniform(jax.random.fold_in(jax.random.fold_in(stream_key, 6), position), (shards_of,), jnp.float32, least / len(split), top_value / len(split))
        factor_of = factor_of * jnp.repeat(jnp.exp(draws), extent[position] // shards_of).reshape((-1,) + (1,) * (len(extent) - 1 - position))
    return factor_of


def shared_out(key, own, number, rows, amount, top, most, skew):
    order = jax.random.permutation(key, amount)
    heavy_load, usual = shares(amount, rows * top, most, skew, True), shares(amount, rows * top, most, skew, False)
    places = jnp.arange(amount)

    def named(lengths, rotation):
        used = int((lengths > 0).sum())
        fixed = max(1, used // 4)
        passed = fixed + (places - fixed + rotation * (used - fixed)) % max(1, amount - fixed)
        return jnp.zeros((amount,), jnp.int32).at[order[jnp.where(places < fixed, places, passed)]].set(jnp.asarray(lengths, jnp.int32))

    lengths = jnp.where(number % 4 == 0, named(heavy_load, number // 4), named(usual, number - number // 4 - 1))
    mixed = jax.random.permutation(jax.random.fold_in(own, 3), amount)
    giver, sink = mixed[0:amount // 2 * 2:2], mixed[1:amount // 2 * 2:2]
    margin = jnp.minimum(lengths[giver] - 1, most - lengths[sink]) // 2
    margin = jnp.where((giver == order[0]) | (sink == order[0]) | (lengths[sink] == 0), 0, jnp.maximum(margin, 0))
    passed = jax.random.randint(jax.random.fold_in(own, 4), (amount // 2,), 0, 1 << 20) % (margin + 1)
    lengths = lengths.at[giver].add(-passed).at[sink].add(passed)
    items = jnp.searchsorted(jnp.cumsum(lengths), jnp.arange(rows * top), side="right").astype(jnp.int32)
    table = items.reshape(top, rows).T
    table = table[jax.random.permutation(jax.random.fold_in(own, 1), rows)]
    rotation = jax.random.randint(jax.random.fold_in(own, 2), (rows, 1), 0, top)
    return jnp.take_along_axis(table, (jnp.arange(top)[None, :] + rotation) % top, axis=1)


def shares(count, total, reach, skew, full):
    portions = [(1 << 20) // math.isqrt(rank ** skew) + 1 for rank in range(1, count + 1)]
    largest = reach if full else min(reach, max(-(-total // count), total * portions[0] // sum(portions)))
    least = 1 if total - largest >= count - 1 else 0
    holding, surplus = [largest] + [least] * (count - 1), total - largest - least * (count - 1)
    while surplus > 0:
        candidates = [i for i in range(1, count) if holding[i] < largest] or [i for i in range(1, count) if holding[i] < reach]
        mass, left = sum([portions[i] for i in candidates]), surplus
        for i in candidates:
            more = min(reach - holding[i], max(1, left * portions[i] // mass), surplus)
            holding[i] = holding[i] + more
            surplus = surplus - more
    return np.array(holding)


def setup_inputs(seed: int = 0, part: int = 0) -> dict:
    seeds = jax.random.split(jax.random.key(seed), 10)
    part_keys = jax.random.split(jax.random.fold_in(seeds[9], part), 10)
    grid = jnp.clip(jnp.exp(math.log(4.0) - 2.9957323 * jax.random.uniform(part_keys[0], (3, CELLS * N_BRICK), jnp.float32) ** levels(part_keys[0], (3, CELLS * N_BRICK), ((1, 16),), -0.2, 0.2)), 0.2, 4.0)
    distribution = jnp.clip(jnp.exp(math.log(1.0) - 3.912023 * jax.random.uniform(part_keys[1], (BINS, TRACERS), jnp.float32) ** levels(part_keys[1], (BINS, TRACERS), ((1, 16),), -0.2, 0.2)), 0.02, 1.0)
    owner_ids_keys = jax.random.split(jax.random.fold_in(part_keys[2], 1), TRACERS // TR_DEV)
    owner_ids_turns = jax.random.permutation(jax.random.fold_in(part_keys[2], 3), TRACERS // TR_DEV)
    owner_ids = jax.vmap(lambda own, number: shared_out(jax.random.fold_in(part_keys[2], 2), own, number, TR_DEV, N_BRICK, 1, CAP, 2))(owner_ids_keys, owner_ids_turns).reshape((TRACERS, 1))
    coords = touch_ends(jax.random.randint(part_keys[3], (3, TRACERS), 0, BS - 1), jax.random.fold_in(part_keys[3], 1), 0, (BS - 1) - 1).astype(jnp.int32)
    fracs = jnp.clip(1.0 * jax.random.uniform(part_keys[4], (3, TRACERS), jnp.float32) ** levels(part_keys[4], (3, TRACERS), ((1, 16),), -0.2, 0.2), 0.0, 1.0)
    counts = touch_ends(jax.random.randint(part_keys[5], (TRACERS,), 1, 5), jax.random.fold_in(part_keys[5], 1), 1, 4).astype(jnp.int32)
    kernel = jnp.clip(jnp.exp(jax.random.uniform(seeds[6], (BINS, BINS), jnp.float32, math.log(0.002), math.log(0.2))), 0.002, 0.2)
    redist = jnp.clip(jnp.exp(jax.random.uniform(seeds[7], (BINS, BINS), jnp.float32, math.log(0.001), math.log(0.05))), 0.001, 0.05)
    shatter = jnp.clip(jnp.exp(jax.random.uniform(seeds[8], (BINS, BINS), jnp.float32, math.log(0.001), math.log(0.05))), 0.001, 0.05)
    return dict(grid=grid, distribution=distribution, owner_ids=owner_ids, coords=coords, fracs=fracs, counts=counts, kernel=kernel, redist=redist, shatter=shatter)


def corner_sum(fields, coords, fracs, side, offset):
    total = jnp.zeros(fracs.shape, jnp.float32)
    for corner in range(8):
        first = corner // 4
        second = corner // 2 % 2
        third = corner % 2
        weight = jnp.ones(fracs.shape[1:], jnp.float32)
        weight = weight * (fracs[0] if first else 1.0 - fracs[0])
        weight = weight * (fracs[1] if second else 1.0 - fracs[1])
        weight = weight * (fracs[2] if third else 1.0 - fracs[2])
        where = ((coords[0] + first) * side + coords[1] + second) * side + coords[2] + third + offset
        picked = jnp.take(fields, where.astype(jnp.int32), axis=1)
        total = total + weight[None] * picked
    return total

def advance(dist, coag, shat, steps, kernel, redist, shatter):
    step_size = 1.0 / jnp.maximum(steps, 1).astype(jnp.float32)
    for section in range(4):
        kernel_dot = jnp.einsum('ij,j...->i...', kernel, dist, precision=lax.Precision.HIGHEST)
        collided = dist * kernel_dot
        gain = coag * jnp.einsum('ij,j...->i...', redist, collided, precision=lax.Precision.HIGHEST)
        gain = gain + shat * jnp.einsum('ij,j...->i...', shatter, dist, precision=lax.Precision.HIGHEST)
        loss = coag * kernel_dot + shat
        fresh = (dist + step_size * gain) / (1.0 + step_size * loss)
        dist = jnp.where(steps >= section + 1, fresh, dist)
    return dist

def reference(grid, distribution, owner_ids, coords, fracs, counts, kernel, redist, shatter):
    owner = owner_ids[:, 0]
    sampled = corner_sum(grid, coords, fracs, BS, owner * (BS * BS * BS))
    coag = sampled[0] * jnp.sqrt(sampled[1])
    shat = sampled[2] * sampled[1]
    return advance(distribution, coag, shat, counts, kernel, redist, shatter)
```

```python
import functools

import jax
import jax.numpy as jnp
from jax import lax
from jax.experimental import pallas as pl
from jax.experimental.pallas import tpu as pltpu
from jax.sharding import PartitionSpec as P

BS = 64
LANES = 128
HALF = LANES // 2
SUB = 8
STEPS = 4
UNROLL = 4
MESH = pl.DeviceIdType.MESH
NT = ((1,), (1,))
PLANE = BS * BS // LANES


def iota(shape, dim):
    return lax.broadcasted_iota(jnp.int32, shape, dim)


def pieces(x, count=3):
    out = []
    for _ in range(count):
        high = x.astype(jnp.bfloat16)
        out.append(high)
        x = x - high.astype(jnp.float32)
    return out


def mxu(a, b, contract=((1,), (0,))):
    return lax.dot_general(a, b, (contract, ((), ())), preferred_element_type=jnp.float32)


def wide(x):
    high, low = pieces(x, 2)
    return jnp.concatenate([high, high, low], axis=1)


def tall(x):
    high, low = pieces(x, 2)
    return jnp.concatenate([high, low, high], axis=0)


def hat(x):
    return jnp.maximum(1.0 - jnp.abs(x), 0.0)


def partner(me, d, n):
    return {"brick": lax.rem(me + d, n)}


def fused(
    n, cap,
    owner_hbm, coords_hbm, fracs_hbm, cells_hbm, counts_hbm, dist_hbm, kernel_hbm, redist_hbm, shatter_hbm,
    out_ref,
    owner_ref, coords_ref, fracs_ref, counts_ref, dist_ref, mats_ref, cells,
    send, recv, index_v, index_s, wa_ref, wb_ref, rsend, rrecv,
    load_sem, index_sem, send_sem, recv_sem, rsend_sem, rrecv_sem,
):
    me = lax.axis_index("brick")
    rows = cells_hbm.shape[0]
    f32, bf16 = jnp.float32, jnp.bfloat16

    def load(source, target, i):
        return pltpu.make_async_copy(source, target, load_sem.at[i])

    first = [
        load(owner_hbm, owner_ref, 0),
        load(coords_hbm, coords_ref, 1),
        load(fracs_hbm, fracs_ref, 2),
    ]
    later = [
        load(cells_hbm, cells.at[:, pl.ds(0, 3), :], 3),
        load(cells_hbm.at[pl.ds(PLANE, rows - PLANE)], cells.at[pl.ds(0, rows - PLANE), pl.ds(4, 3), :], 4),
        load(counts_hbm, counts_ref, 5),
        load(dist_hbm, dist_ref, 6),
        load(kernel_hbm, mats_ref.at[0], 7),
        load(shatter_hbm, mats_ref.at[1], 8),
        load(redist_hbm, mats_ref.at[2], 9),
    ]
    for copy in first + later:
        copy.start()
    barrier = pltpu.get_barrier_semaphore()
    for d in range(1, n):
        pl.semaphore_signal(barrier, inc=1, device_id=partner(me, d, n), device_id_type=MESH)
    cells[rows - PLANE, 4:8, :] = jnp.zeros((4, LANES), f32)
    for copy in first:
        copy.wait()

    tracers = owner_ref.shape[1]
    blocks = tracers // LANES
    rel = owner_ref[...] - me
    rel = jnp.where(rel < 0, rel + n, rel)
    onehot = jnp.where(iota((n, tracers), 0) == rel, 1.0, 0.0)
    upto = jnp.where(iota((LANES, LANES), 0) <= iota((LANES, LANES), 1), 1.0, 0.0).astype(bf16)
    stacked = jnp.concatenate([onehot[:, b * LANES : (b + 1) * LANES] for b in range(blocks)], axis=0)
    counted = mxu(stacked.astype(bf16), upto)
    running = jnp.zeros((n, 1), f32)
    ranks = []
    for b in range(blocks):
        part = counted[b * n : (b + 1) * n]
        ranks.append(jnp.sum(onehot[:, b * LANES : (b + 1) * LANES] * (part + running), axis=0, keepdims=True))
        running = running + part[:, LANES - 1 :]
    rank = jnp.concatenate(ranks, axis=1).astype(jnp.int32) - 1
    placed = jnp.where(iota((LANES, tracers), 0) == rank, 1.0, 0.0).astype(bf16)

    blank = jnp.zeros((1, tracers), f32)
    coords = coords_ref[...].astype(f32)
    fracs = fracs_ref[...]
    high, middle, low = [p.astype(f32) for p in pieces(fracs)]
    main = jnp.concatenate([coords, blank, high, blank], axis=0)
    rest = jnp.concatenate([middle, blank, low, blank], axis=0)
    left = [jnp.where(rel == d, x, 0.0) for x in (main, rest) for d in range(n)]
    packed = mxu(jnp.concatenate(left, axis=0).astype(bf16), placed, NT)
    lower = iota((SUB, LANES), 0) < 4
    for d in range(n):
        x = packed[SUB * d : SUB * (d + 1)]
        y = packed[SUB * (n + d) : SUB * (n + d + 1)]
        x = x + jnp.where(lower, 0.0, y + pltpu.roll(y, 4, 0))
        send[d] = x
        if d == 0:
            recv[0] = x

    pl.semaphore_wait(barrier, n - 1)
    for d in range(1, n):
        pltpu.make_async_remote_copy(
            src_ref=send.at[d], dst_ref=recv.at[d], send_sem=send_sem, recv_sem=recv_sem,
            device_id=partner(me, d, n), device_id_type=MESH,
        ).start()

    for copy in later[2:]:
        copy.wait()
    steps = counts_ref[...]
    h = 1.0 / jnp.maximum(steps, 1).astype(f32)
    dist = dist_ref[...]
    bins = dist.shape[0]
    both = wide(jnp.concatenate([mats_ref[0], mats_ref[1]], axis=0))
    moved = wide(mats_ref[2])

    def products(dist):
        out = mxu(both, tall(dist))
        dot, broken = out[:bins], out[bins:]
        return dot, broken, mxu(moved, tall(dist * dot))

    ready = products(dist)

    pltpu.make_async_copy(recv.at[pl.ds(1, n - 1)], recv.at[pl.ds(1, n - 1)], recv_sem).wait()

    row = iota((SUB, LANES), 0)
    spots = []
    for s in range(n):
        x = recv[s]
        whole = x.astype(jnp.int32)
        spread = jnp.where(row == 0, whole * PLANE, whole >> 1)
        index_v[s : s + 1, :] = jnp.clip(spread[0:1] + spread[1:2], 0, rows - PLANE - 1)
        base = jnp.where(row == 1, (whole & 1).astype(f32), x)
        spots.append(base + pltpu.roll(x, 4, 0))
    move = pltpu.make_async_copy(index_v, index_s, index_sem)
    move.start()
    columns = jnp.concatenate(spots, axis=0).T
    lane = iota((cap, LANES), 1)
    inner = (lane % HALF).astype(f32)
    outer = (lane // HALF).astype(f32)
    for s in range(n):
        y = columns[:cap, SUB * s + 1 : SUB * s + 2]
        z = columns[:cap, SUB * s + 2 : SUB * s + 3]
        w = hat(inner - z)
        across = outer - y
        wa_ref[s] = w * hat(across)
        wb_ref[s] = w * hat(across + 2.0)
    for copy in later[:2]:
        copy.wait()
    move.wait()

    lanes = iota((SUB, LANES), 1)

    def some(group, carry):
        for u in range(UNROLL):
            s = group * UNROLL + u
            acc = jnp.zeros((SUB, LANES), f32)
            for c in range(cap):
                r = index_s[s, c]
                p = cells[r] * wa_ref[s, pl.ds(c, 1), :] + cells[r + 1] * wb_ref[s, pl.ds(c, 1), :]
                acc = jnp.where(lanes == c, jnp.sum(p, axis=1, keepdims=True), acc)
            rsend[s] = acc

            @pl.when(s == 0)
            def _():
                rrecv[0] = acc

            @pl.when(s > 0)
            def _():
                pltpu.make_async_remote_copy(
                    src_ref=rsend.at[s], dst_ref=rrecv.at[s], send_sem=rsend_sem, recv_sem=rrecv_sem,
                    device_id=partner(me, n - s, n), device_id_type=MESH,
                ).start()
        return carry

    lax.fori_loop(0, n // UNROLL, some, 0)

    pltpu.make_async_copy(rrecv.at[pl.ds(1, n - 1)], rrecv.at[pl.ds(1, n - 1)], rrecv_sem).wait()
    answers = jnp.concatenate(pieces(rrecv[...].reshape(n * SUB, LANES), 2), axis=1)
    found = mxu(answers, jnp.concatenate([placed, placed], axis=0))
    both_ends = jnp.zeros((SUB, tracers), f32)
    for s in range(n):
        both_ends = jnp.where(rel == s, found[SUB * s : SUB * (s + 1)], both_ends)
    f0 = fracs[0:1]
    sampled = [both_ends[f : f + 1] * (1.0 - f0) + both_ends[4 + f : 5 + f] * f0 for f in range(3)]
    coag = sampled[0] * jnp.sqrt(sampled[1])
    shat = sampled[2] * sampled[1]
    for section in range(STEPS):
        dot, broken, back = ready if section == 0 else products(dist)
        gain = coag * back + shat * broken
        loss = coag * dot + shat
        fresh = (dist + h * gain) / (1.0 + h * loss)
        dist = jnp.where(steps >= section + 1, fresh, dist)
    out_ref[...] = dist
    pltpu.make_async_copy(send.at[pl.ds(1, n - 1)], send.at[pl.ds(1, n - 1)], send_sem).wait()
    pltpu.make_async_copy(rsend.at[pl.ds(1, n - 1)], rsend.at[pl.ds(1, n - 1)], rsend_sem).wait()


def shards(grid, distribution, owner_ids, coords, fracs, counts, kernel, redist, shatter):
    n = lax.axis_size("brick")
    bins, tracers = distribution.shape
    cap = 2 * tracers // n
    assert cap <= HALF and n % UNROLL == 0 and tracers % LANES == 0
    f32, i32 = jnp.float32, jnp.int32
    cells = jnp.swapaxes(grid.reshape(grid.shape[0], -1, LANES), 0, 1)
    operands = (
        owner_ids.reshape(1, tracers), coords, fracs, cells, counts.reshape(1, tracers),
        distribution, kernel, redist, shatter,
    )
    dma = pltpu.SemaphoreType.DMA
    return pl.pallas_call(
        functools.partial(fused, n, cap),
        out_shape=jax.ShapeDtypeStruct((bins, tracers), f32),
        in_specs=[pl.BlockSpec(memory_space=pltpu.HBM)] * len(operands),
        out_specs=pl.BlockSpec(memory_space=pltpu.VMEM),
        scratch_shapes=[
            pltpu.VMEM((1, tracers), i32),
            pltpu.VMEM(coords.shape, i32),
            pltpu.VMEM(fracs.shape, f32),
            pltpu.VMEM((1, tracers), i32),
            pltpu.VMEM(distribution.shape, f32),
            pltpu.VMEM((3, *kernel.shape), f32),
            pltpu.VMEM((cells.shape[0], SUB, LANES), f32),
            pltpu.VMEM((n, SUB, LANES), f32),
            pltpu.VMEM((n, SUB, LANES), f32),
            pltpu.VMEM((n, LANES), i32),
            pltpu.SMEM((n, LANES), i32),
            pltpu.VMEM((n, cap, LANES), f32),
            pltpu.VMEM((n, cap, LANES), f32),
            pltpu.VMEM((n, SUB, LANES), f32),
            pltpu.VMEM((n, SUB, LANES), f32),
            dma((10,)), dma, dma, dma, dma, dma,
        ],
        compiler_params=pltpu.CompilerParams(
            collective_id=0, has_side_effects=True, vmem_limit_bytes=32 * 1024 * 1024
        ),
        name="fused",
    )(*[pltpu.with_memory_space_constraint(x, pltpu.HBM) for x in operands])


def solution(mesh):
    in_specs = (
        P(None, ("runs", "brick")),
        P(None, ("runs", "brick")),
        P(("runs", "brick"), None),
        P(None, ("runs", "brick")),
        P(None, ("runs", "brick")),
        P(("runs", "brick")),
        P(),
        P(),
        P(),
    )
    out_specs = P(None, ("runs", "brick"))
    return jax.shard_map(shards, mesh=mesh, in_specs=in_specs, out_specs=out_specs, check_vma=False)
```

```python
import functools

import jax
import jax.numpy as jnp
from jax import lax
from jax.experimental import pallas as pl
from jax.experimental.pallas import tpu as pltpu
from jax.sharding import PartitionSpec as P

BS = 64
LANES = 128
HALF = LANES // 2
SUB = 8
STEPS = 4
TEAM = 4
MESH = pl.DeviceIdType.MESH
NT = ((1,), (1,))
PLANE = BS * BS // LANES


def iota(shape, dim):
    return lax.broadcasted_iota(jnp.int32, shape, dim)


def pieces(x, count=3):
    out = []
    for _ in range(count):
        high = x.astype(jnp.bfloat16)
        out.append(high)
        x = x - high.astype(jnp.float32)
    return out


def mxu(a, b, contract=((1,), (0,))):
    return lax.dot_general(a, b, (contract, ((), ())), preferred_element_type=jnp.float32)


def wide(x):
    high, low = pieces(x, 2)
    return jnp.concatenate([high, high, low], axis=1)


def tall(x):
    high, low = pieces(x, 2)
    return jnp.concatenate([high, low, high], axis=0)


def hat(x):
    return jnp.maximum(1.0 - jnp.abs(x), 0.0)


def flips(me, n):
    return [(1 - 2 * (me // bit % 2)) * bit for bit in (1 << b for b in range(n.bit_length() - 1))]


def partner(me, d, flip):
    return {"brick": me + sum(f for b, f in enumerate(flip) if d >> b & 1)}


def fused(
    n, cap,
    owner_hbm, coords_hbm, fracs_hbm, cells_hbm, counts_hbm, dist_hbm, kernel_hbm, redist_hbm, shatter_hbm,
    out_ref,
    owner_ref, coords_ref, fracs_ref, counts_ref, dist_ref, mats_ref, cells,
    send, recv, index_v, wa_ref, wb_ref, rsend, rrecv,
    load_sem, send_sem, recv_sem, rsend_sem, rrecv_sem,
):
    me = lax.axis_index("brick")
    flip = flips(me, n)
    rows = cells_hbm.shape[0]
    f32, bf16 = jnp.float32, jnp.bfloat16

    def load(source, target, i):
        return pltpu.make_async_copy(source, target, load_sem.at[i])

    first = [
        load(owner_hbm, owner_ref, 0),
        load(coords_hbm, coords_ref, 1),
        load(fracs_hbm, fracs_ref, 2),
    ]
    later = [
        load(cells_hbm, cells.at[:, pl.ds(0, 3), :], 3),
        load(cells_hbm.at[pl.ds(PLANE, rows - PLANE)], cells.at[pl.ds(0, rows - PLANE), pl.ds(4, 3), :], 4),
        load(counts_hbm, counts_ref, 5),
        load(dist_hbm, dist_ref, 6),
        load(kernel_hbm, mats_ref.at[0], 7),
        load(shatter_hbm, mats_ref.at[1], 8),
        load(redist_hbm, mats_ref.at[2], 9),
    ]
    for copy in first:
        copy.start()
    barrier = pltpu.get_barrier_semaphore()
    for d in reversed(range(1, n)):
        pl.semaphore_signal(barrier, inc=1, device_id=partner(me, d, flip), device_id_type=MESH)
    for copy in later:
        copy.start()
    cells[rows - PLANE, 4:8, :] = jnp.zeros((4, LANES), f32)
    for copy in first:
        copy.wait()

    tracers = owner_ref.shape[1]
    blocks = tracers // LANES
    rel = owner_ref[...] ^ me
    onehot = jnp.where(iota((n, tracers), 0) == rel, 1.0, 0.0)
    upto = jnp.where(iota((LANES, LANES), 0) <= iota((LANES, LANES), 1), 1.0, 0.0).astype(bf16)
    stacked = jnp.concatenate([onehot[:, b * LANES : (b + 1) * LANES] for b in range(blocks)], axis=0)
    counted = mxu(stacked.astype(bf16), upto)
    running = jnp.zeros((n, 1), f32)
    ranks = []
    for b in range(blocks):
        part = counted[b * n : (b + 1) * n]
        ranks.append(jnp.sum(onehot[:, b * LANES : (b + 1) * LANES] * (part + running), axis=0, keepdims=True))
        running = running + part[:, LANES - 1 :]
    rank = jnp.concatenate(ranks, axis=1).astype(jnp.int32) - 1
    placed = jnp.where(iota((LANES, tracers), 0) == rank, 1.0, 0.0).astype(bf16)

    blank = jnp.zeros((1, tracers), f32)
    coords = coords_ref[...].astype(f32)
    fracs = fracs_ref[...]
    high, middle, low = [p.astype(f32) for p in pieces(fracs)]
    main = jnp.concatenate([coords, blank, high, blank], axis=0)
    rest = jnp.concatenate([middle, blank, low, blank], axis=0)
    left = [jnp.where(rel == d, x, 0.0) for x in (main, rest) for d in range(n)]
    packed = mxu(jnp.concatenate(left, axis=0).astype(bf16), placed, NT)
    lower = iota((SUB, LANES), 0) < 4
    for d in range(n):
        x = packed[SUB * d : SUB * (d + 1)]
        y = packed[SUB * (n + d) : SUB * (n + d + 1)]
        x = x + jnp.where(lower, 0.0, y + pltpu.roll(y, 4, 0))
        send[d] = x

    pltpu.make_async_copy(send.at[0], recv.at[0], recv_sem.at[0]).start()
    pl.semaphore_wait(barrier, n - 1)
    for d in reversed(range(1, n)):
        pltpu.make_async_remote_copy(
            src_ref=send.at[d], dst_ref=recv.at[d], send_sem=send_sem, recv_sem=recv_sem.at[d // TEAM],
            device_id=partner(me, d, flip), device_id_type=MESH,
        ).start()

    for copy in later[2:]:
        copy.wait()
    steps = counts_ref[...]
    h = 1.0 / jnp.maximum(steps, 1).astype(f32)
    dist = dist_ref[...]
    bins = dist.shape[0]
    both = wide(jnp.concatenate([mats_ref[0], mats_ref[1]], axis=0))
    moved = wide(mats_ref[2])

    def products(dist):
        out = mxu(both, tall(dist))
        dot, broken = out[:bins], out[bins:]
        return dot, broken, mxu(moved, tall(dist * dot))

    ready = products(dist)

    for copy in later[:2]:
        copy.wait()

    row = iota((SUB, LANES), 0)
    lanes = iota((SUB, LANES), 1)
    lane = iota((cap, LANES), 1)
    inner = (lane % HALF).astype(f32)
    outer = (lane // HALF).astype(f32)

    def answer(team, carry):
        start = team * TEAM
        here = recv.at[pl.ds(start, TEAM)]
        pltpu.make_async_copy(here, here, recv_sem.at[team]).wait()
        spots = []
        for u in range(TEAM):
            x = recv[start + u]
            whole = x.astype(jnp.int32)
            spread = jnp.where(row == 0, whole * PLANE, whole >> 1)
            index = (spread + pltpu.roll(spread, SUB - 1, 0)).astype(f32)
            base = jnp.where(row == 1, (whole & 1).astype(f32), x)
            spots.append(jnp.where(row == 0, index, base + pltpu.roll(x, 4, 0)))
        columns = jnp.concatenate(spots, axis=0).T
        whole = jnp.clip(columns[:cap].astype(jnp.int32), 0, rows - PLANE - 1)
        for u in range(TEAM):
            index_v[u] = whole[:, SUB * u : SUB * (u + 1)]
        for u in range(TEAM):
            y = columns[:cap, SUB * u + 1 : SUB * u + 2]
            z = columns[:cap, SUB * u + 2 : SUB * u + 3]
            w = hat(inner - z)
            across = outer - y
            wa_ref[u] = w * hat(across)
            wb_ref[u] = w * hat(across + 2.0)
        for u in range(TEAM):
            acc = jnp.zeros((SUB, LANES), f32)
            for c in range(cap):
                r = index_v[u, c, 0]
                p = cells[r] * wa_ref[u, pl.ds(c, 1), :] + cells[r + 1] * wb_ref[u, pl.ds(c, 1), :]
                acc = jnp.where(lanes == c, jnp.sum(p, axis=1, keepdims=True), acc)
            rsend[start + u] = acc
        base = me
        for b, f in enumerate(flip[TEAM.bit_length() - 1 :]):
            base = base + team // (1 << b) % 2 * f
        for u in range(TEAM):
            s = start + u
            remote = pltpu.make_async_remote_copy(
                src_ref=rsend.at[s], dst_ref=rrecv.at[s], send_sem=rsend_sem, recv_sem=rrecv_sem,
                device_id=partner(base, u, flip), device_id_type=MESH,
            )
            if u:
                remote.start()
            else:
                pl.when(team > 0)(remote.start)

                @pl.when(team == 0)
                def _():
                    pltpu.make_async_copy(rsend.at[0], rrecv.at[0], rrecv_sem).start()
        return carry

    lax.fori_loop(0, n // TEAM, answer, 0)

    pltpu.make_async_copy(rrecv, rrecv, rrecv_sem).wait()
    answers = jnp.concatenate(pieces(rrecv[...].reshape(n * SUB, LANES), 2), axis=1)
    found = mxu(answers, jnp.concatenate([placed, placed], axis=0))
    both_ends = jnp.zeros((SUB, tracers), f32)
    for s in range(n):
        both_ends = jnp.where(rel == s, found[SUB * s : SUB * (s + 1)], both_ends)
    f0 = fracs[0:1]
    sampled = [both_ends[f : f + 1] * (1.0 - f0) + both_ends[4 + f : 5 + f] * f0 for f in range(3)]
    coag = sampled[0] * jnp.sqrt(sampled[1])
    shat = sampled[2] * sampled[1]
    for section in range(STEPS):
        dot, broken, back = ready if section == 0 else products(dist)
        gain = coag * back + shat * broken
        loss = coag * dot + shat
        fresh = (dist + h * gain) / (1.0 + h * loss)
        dist = jnp.where(steps >= section + 1, fresh, dist)
    out_ref[...] = dist
    pltpu.make_async_copy(send.at[pl.ds(1, n - 1)], send.at[pl.ds(1, n - 1)], send_sem).wait()
    pltpu.make_async_copy(rsend.at[pl.ds(1, n - 1)], rsend.at[pl.ds(1, n - 1)], rsend_sem).wait()


def shards(grid, distribution, owner_ids, coords, fracs, counts, kernel, redist, shatter):
    n = lax.axis_size("brick")
    bins, tracers = distribution.shape
    cap = 2 * tracers // n
    assert cap <= HALF and n % TEAM == 0 and n & (n - 1) == 0 and tracers % LANES == 0
    f32, i32 = jnp.float32, jnp.int32
    cells = jnp.swapaxes(grid.reshape(grid.shape[0], -1, LANES), 0, 1)
    operands = (
        owner_ids.reshape(1, tracers), coords, fracs, cells, counts.reshape(1, tracers),
        distribution, kernel, redist, shatter,
    )
    dma = pltpu.SemaphoreType.DMA
    return pl.pallas_call(
        functools.partial(fused, n, cap),
        out_shape=jax.ShapeDtypeStruct((bins, tracers), f32),
        in_specs=[pl.BlockSpec(memory_space=pltpu.HBM)] * len(operands),
        out_specs=pl.BlockSpec(memory_space=pltpu.VMEM),
        scratch_shapes=[
            pltpu.VMEM((1, tracers), i32),
            pltpu.VMEM(coords.shape, i32),
            pltpu.VMEM(fracs.shape, f32),
            pltpu.VMEM((1, tracers), i32),
            pltpu.VMEM(distribution.shape, f32),
            pltpu.VMEM((3, *kernel.shape), f32),
            pltpu.VMEM((cells.shape[0], SUB, LANES), f32),
            pltpu.VMEM((n, SUB, LANES), f32),
            pltpu.VMEM((n, SUB, LANES), f32),
            pltpu.VMEM((TEAM, cap, SUB), i32),
            pltpu.VMEM((TEAM, cap, LANES), f32),
            pltpu.VMEM((TEAM, cap, LANES), f32),
            pltpu.VMEM((n, SUB, LANES), f32),
            pltpu.VMEM((n, SUB, LANES), f32),
            dma((10,)), dma, dma((n // TEAM,)), dma, dma,
        ],
        compiler_params=pltpu.CompilerParams(
            collective_id=0, has_side_effects=True, vmem_limit_bytes=32 * 1024 * 1024
        ),
        name="fused",
    )(*[pltpu.with_memory_space_constraint(x, pltpu.HBM) for x in operands])


def solution(mesh):
    in_specs = (
        P(None, ("runs", "brick")),
        P(None, ("runs", "brick")),
        P(("runs", "brick"), None),
        P(None, ("runs", "brick")),
        P(None, ("runs", "brick")),
        P(("runs", "brick")),
        P(),
        P(),
        P(),
    )
    out_specs = P(None, ("runs", "brick"))
    return jax.shard_map(shards, mesh=mesh, in_specs=in_specs, out_specs=out_specs, check_vma=False)
```

```python
import functools

import jax
import jax.numpy as jnp
from jax import lax
from jax.experimental import pallas as pl
from jax.experimental.pallas import tpu as pltpu
from jax.sharding import PartitionSpec as P

BS = 64
LANES = 128
HALF = LANES // 2
SUB = 8
STEPS = 4
TEAM = 2
RELAY = 2
MESH = pl.DeviceIdType.MESH
NT = ((1,), (1,))
PLANE = BS * BS // LANES


def iota(shape, dim):
    return lax.broadcasted_iota(jnp.int32, shape, dim)


def pieces(x, count=3):
    out = []
    for _ in range(count):
        high = x.astype(jnp.bfloat16)
        out.append(high)
        x = x - high.astype(jnp.float32)
    return out


def mxu(a, b, contract=((1,), (0,))):
    return lax.dot_general(a, b, (contract, ((), ())), preferred_element_type=jnp.float32)


def wide(x):
    high, low = pieces(x, 2)
    return jnp.concatenate([high, high, low], axis=1)


def tall(x):
    high, low = pieces(x, 2)
    return jnp.concatenate([high, low, high], axis=0)


def hat(x):
    return jnp.maximum(1.0 - jnp.abs(x), 0.0)


def device(chip, e, core, flip):
    return {"brick": 2 * (chip + sum(f for b, f in enumerate(flip) if e >> b & 1)) + core}


def fused(
    n, cap,
    owner_hbm, coords_hbm, fracs_hbm, cells_hbm, counts_hbm, dist_hbm, kernel_hbm, redist_hbm, shatter_hbm,
    out_ref,
    owner_ref, coords_ref, fracs_ref, counts_ref, dist_ref, mats_ref, cells,
    send, relay, recv, index_v, wa_ref, wb_ref, rsend, rrecv,
    load_sem, send_sem, relay_sem, recv_sem, rsend_sem, rrecv_sem,
):
    me = lax.axis_index("brick")
    chips, chip, core = n // 2, me // 2, me % 2
    flip = [(1 - 2 * (chip // bit % 2)) * bit for bit in (1 << b for b in range(chips.bit_length() - 1))]

    def spot(e, c):
        return 4 * (e // 2) + 2 * c + e % 2

    far_first = tuple(reversed(range(chips)))
    rows = cells_hbm.shape[0]
    f32, bf16 = jnp.float32, jnp.bfloat16

    def load(source, target, i):
        return pltpu.make_async_copy(source, target, load_sem.at[i])

    first = [
        load(owner_hbm, owner_ref, 0),
        load(coords_hbm, coords_ref, 1),
        load(fracs_hbm, fracs_ref, 2),
    ]
    later = [
        load(cells_hbm, cells.at[:, pl.ds(0, 3), :], 3),
        load(cells_hbm.at[pl.ds(PLANE, rows - PLANE)], cells.at[pl.ds(0, rows - PLANE), pl.ds(4, 3), :], 4),
        load(counts_hbm, counts_ref, 5),
        load(dist_hbm, dist_ref, 6),
        load(kernel_hbm, mats_ref.at[0], 7),
        load(shatter_hbm, mats_ref.at[1], 8),
        load(redist_hbm, mats_ref.at[2], 9),
    ]
    for copy in first:
        copy.start()
    barrier = pltpu.get_barrier_semaphore()
    for e in far_first[:-1]:
        pl.semaphore_signal(barrier, inc=1, device_id=device(chip, e, 1, flip), device_id_type=MESH)
    bit = RELAY.bit_length() - 1
    pl.semaphore_signal(
        barrier, inc=1, device_id={"brick": 2 * (chip + core * flip[bit]) + 1 - core}, device_id_type=MESH
    )
    for copy in later:
        copy.start()
    cells[rows - PLANE, 4:8, :] = jnp.zeros((4, LANES), f32)
    for copy in first:
        copy.wait()

    tracers = owner_ref.shape[1]
    blocks = tracers // LANES
    owner = owner_ref[...]
    apart = (owner >> 1) ^ chip
    rel = 4 * (apart >> 1) + 2 * (owner & 1) + (apart & 1)
    onehot = jnp.where(iota((n, tracers), 0) == rel, 1.0, 0.0)
    upto = jnp.where(iota((LANES, LANES), 0) <= iota((LANES, LANES), 1), 1.0, 0.0).astype(bf16)
    stacked = jnp.concatenate([onehot[:, b * LANES : (b + 1) * LANES] for b in range(blocks)], axis=0)
    counted = mxu(stacked.astype(bf16), upto)
    running = jnp.zeros((n, 1), f32)
    ranks = []
    for b in range(blocks):
        part = counted[b * n : (b + 1) * n]
        ranks.append(jnp.sum(onehot[:, b * LANES : (b + 1) * LANES] * (part + running), axis=0, keepdims=True))
        running = running + part[:, LANES - 1 :]
    rank = jnp.concatenate(ranks, axis=1).astype(jnp.int32) - 1
    placed = jnp.where(iota((LANES, tracers), 0) == rank, 1.0, 0.0).astype(bf16)

    blank = jnp.zeros((1, tracers), f32)
    coords = coords_ref[...].astype(f32)
    fracs = fracs_ref[...]
    high, middle, low = [p.astype(f32) for p in pieces(fracs)]
    main = jnp.concatenate([coords, blank, high, blank], axis=0)
    rest = jnp.concatenate([middle, blank, low, blank], axis=0)
    left = [jnp.where(rel == d, x, 0.0) for x in (main, rest) for d in range(n)]
    packed = mxu(jnp.concatenate(left, axis=0).astype(bf16), placed, NT)
    lower = iota((SUB, LANES), 0) < 4
    for d in range(n):
        x = packed[SUB * d : SUB * (d + 1)]
        y = packed[SUB * (n + d) : SUB * (n + d + 1)]
        x = x + jnp.where(lower, 0.0, y + pltpu.roll(y, 4, 0))
        send[d] = x

    pltpu.make_async_copy(send.at[2 * core], recv.at[2 * core], recv_sem.at[core]).start()

    def pass_on(source, target, e, c, i, sem):
        pltpu.make_async_remote_copy(
            src_ref=source, dst_ref=target, send_sem=send_sem.at[i], recv_sem=sem,
            device_id=device(chip, e, c, flip), device_id_type=MESH,
        ).start()

    @pl.when(core == 0)
    def _():
        pl.semaphore_wait(barrier, 1)
        for g in reversed(range(n // 4)):
            part = pl.ds(4 * g, 4)
            pass_on(send.at[part], relay.at[part], RELAY, 1, 0, relay_sem.at[g])
        pass_on(send.at[spot(RELAY, 1)], recv.at[spot(RELAY, 0)], RELAY, 1, 1, recv_sem.at[2 * (RELAY // 2)])

    @pl.when(core == 1)
    def _():
        pl.semaphore_wait(barrier, n - 1)
        for g in reversed(range(n // 4)):
            for e in (2 * g + 1, 2 * g):
                for c in (0, 1):
                    if e or not c:
                        pass_on(send.at[spot(e, c)], recv.at[spot(e, 1)], e, c, 0, recv_sem.at[2 * g + 1])
        for g in reversed(range(n // 4)):
            part = relay.at[pl.ds(4 * g, 4)]
            pltpu.make_async_copy(part, part, relay_sem.at[g]).wait()
            for e in (2 * g + 1, 2 * g):
                for c in (0, 1):
                    if (e, c) not in ((0, 0), (RELAY, 1)):
                        pass_on(relay.at[spot(e, c)], recv.at[spot(e, 0)], RELAY ^ e, c, 1, recv_sem.at[2 * g])

    for copy in later[2:]:
        copy.wait()
    steps = counts_ref[...]
    h = 1.0 / jnp.maximum(steps, 1).astype(f32)
    dist = dist_ref[...]
    bins = dist.shape[0]
    both = wide(jnp.concatenate([mats_ref[0], mats_ref[1]], axis=0))
    moved = wide(mats_ref[2])

    def products(dist):
        out = mxu(both, tall(dist))
        dot, broken = out[:bins], out[bins:]
        return dot, broken, mxu(moved, tall(dist * dot))

    ready = products(dist)

    for copy in later[:2]:
        copy.wait()

    row = iota((SUB, LANES), 0)
    lanes = iota((SUB, LANES), 1)
    lane = iota((cap, LANES), 1)
    inner = (lane % HALF).astype(f32)
    outer = (lane // HALF).astype(f32)

    def answer(team, carry):
        start = team * TEAM
        here = recv.at[pl.ds(start, TEAM)]
        pltpu.make_async_copy(here, here, recv_sem.at[team]).wait()
        spots = []
        for u in range(TEAM):
            x = recv[start + u]
            whole = x.astype(jnp.int32)
            spread = jnp.where(row == 0, whole * PLANE, whole >> 1)
            index = (spread + pltpu.roll(spread, SUB - 1, 0)).astype(f32)
            base = jnp.where(row == 1, (whole & 1).astype(f32), x)
            spots.append(jnp.where(row == 0, index, base + pltpu.roll(x, 4, 0)))
        columns = jnp.concatenate(spots, axis=0).T
        whole = jnp.clip(columns[:cap].astype(jnp.int32), 0, rows - PLANE - 1)
        for u in range(TEAM):
            index_v[u] = whole[:, SUB * u : SUB * (u + 1)]
        for u in range(TEAM):
            y = columns[:cap, SUB * u + 1 : SUB * u + 2]
            z = columns[:cap, SUB * u + 2 : SUB * u + 3]
            w = hat(inner - z)
            across = outer - y
            wa_ref[u] = w * hat(across)
            wb_ref[u] = w * hat(across + 2.0)
        for u in range(TEAM):
            acc = jnp.zeros((SUB, LANES), f32)
            for c in range(cap):
                r = index_v[u, c, 0]
                p = cells[r] * wa_ref[u, pl.ds(c, 1), :] + cells[r + 1] * wb_ref[u, pl.ds(c, 1), :]
                acc = jnp.where(lanes == c, jnp.sum(p, axis=1, keepdims=True), acc)
            rsend[start + u] = acc
        base = chip
        for b, f in enumerate(flip[1:]):
            base = base + team // 2 // (1 << b) % 2 * f
        for u in range(TEAM):
            home = 4 * (team // 2) + 2 * core + u
            remote = pltpu.make_async_remote_copy(
                src_ref=rsend.at[start + u], dst_ref=rrecv.at[home], send_sem=rsend_sem, recv_sem=rrecv_sem,
                device_id=device(base, u, team % 2, flip), device_id_type=MESH,
            )
            if u:
                remote.start()
            else:
                pl.when(team != core)(remote.start)

                @pl.when(team == core)
                def _():
                    pltpu.make_async_copy(rsend.at[2 * core], rrecv.at[2 * core], rrecv_sem).start()
        return carry

    lax.fori_loop(0, n // TEAM, answer, 0)

    pltpu.make_async_copy(rrecv, rrecv, rrecv_sem).wait()
    answers = jnp.concatenate(pieces(rrecv[...].reshape(n * SUB, LANES), 2), axis=1)
    found = mxu(answers, jnp.concatenate([placed, placed], axis=0))
    both_ends = jnp.zeros((SUB, tracers), f32)
    for s in range(n):
        both_ends = jnp.where(rel == s, found[SUB * s : SUB * (s + 1)], both_ends)
    f0 = fracs[0:1]
    sampled = [both_ends[f : f + 1] * (1.0 - f0) + both_ends[4 + f : 5 + f] * f0 for f in range(3)]
    coag = sampled[0] * jnp.sqrt(sampled[1])
    shat = sampled[2] * sampled[1]
    for section in range(STEPS):
        dot, broken, back = ready if section == 0 else products(dist)
        gain = coag * back + shat * broken
        loss = coag * dot + shat
        fresh = (dist + h * gain) / (1.0 + h * loss)
        dist = jnp.where(steps >= section + 1, fresh, dist)
    out_ref[...] = dist
    some = rsend.at[pl.ds(1, n - 1)]
    pltpu.make_async_copy(some, some, rsend_sem).wait()

    @pl.when(core == 0)
    def _():
        pltpu.make_async_copy(send, send, send_sem.at[0]).wait()
        pltpu.make_async_copy(send.at[0], send.at[0], send_sem.at[1]).wait()

    @pl.when(core == 1)
    def _():
        own, others = send.at[pl.ds(1, n - 1)], relay.at[pl.ds(2, n - 2)]
        pltpu.make_async_copy(own, own, send_sem.at[0]).wait()
        pltpu.make_async_copy(others, others, send_sem.at[1]).wait()


def shards(grid, distribution, owner_ids, coords, fracs, counts, kernel, redist, shatter):
    n = lax.axis_size("brick")
    bins, tracers = distribution.shape
    cap = 2 * tracers // n
    assert cap <= HALF and n > 2 * RELAY and n & (n - 1) == 0 and tracers % LANES == 0
    f32, i32 = jnp.float32, jnp.int32
    cells = jnp.swapaxes(grid.reshape(grid.shape[0], -1, LANES), 0, 1)
    operands = (
        owner_ids.reshape(1, tracers), coords, fracs, cells, counts.reshape(1, tracers),
        distribution, kernel, redist, shatter,
    )
    dma = pltpu.SemaphoreType.DMA
    return pl.pallas_call(
        functools.partial(fused, n, cap),
        out_shape=jax.ShapeDtypeStruct((bins, tracers), f32),
        in_specs=[pl.BlockSpec(memory_space=pltpu.HBM)] * len(operands),
        out_specs=pl.BlockSpec(memory_space=pltpu.VMEM),
        scratch_shapes=[
            pltpu.VMEM((1, tracers), i32),
            pltpu.VMEM(coords.shape, i32),
            pltpu.VMEM(fracs.shape, f32),
            pltpu.VMEM((1, tracers), i32),
            pltpu.VMEM(distribution.shape, f32),
            pltpu.VMEM((3, *kernel.shape), f32),
            pltpu.VMEM((cells.shape[0], SUB, LANES), f32),
            pltpu.VMEM((n, SUB, LANES), f32),
            pltpu.VMEM((n, SUB, LANES), f32),
            pltpu.VMEM((n, SUB, LANES), f32),
            pltpu.VMEM((TEAM, cap, SUB), i32),
            pltpu.VMEM((TEAM, cap, LANES), f32),
            pltpu.VMEM((TEAM, cap, LANES), f32),
            pltpu.VMEM((n, SUB, LANES), f32),
            pltpu.VMEM((n, SUB, LANES), f32),
            dma((10,)), dma((2,)), dma((n // 4,)), dma((n // TEAM,)), dma, dma,
        ],
        compiler_params=pltpu.CompilerParams(
            collective_id=0, has_side_effects=True, vmem_limit_bytes=32 * 1024 * 1024
        ),
        name="fused",
    )(*[pltpu.with_memory_space_constraint(x, pltpu.HBM) for x in operands])


def solution(mesh):
    in_specs = (
        P(None, ("runs", "brick")),
        P(None, ("runs", "brick")),
        P(("runs", "brick"), None),
        P(None, ("runs", "brick")),
        P(None, ("runs", "brick")),
        P(("runs", "brick")),
        P(),
        P(),
        P(),
    )
    out_specs = P(None, ("runs", "brick"))
    return jax.shard_map(shards, mesh=mesh, in_specs=in_specs, out_specs=out_specs, check_vma=False)
```

```python
import functools

import jax
import jax.numpy as jnp
from jax import lax
from jax.experimental import pallas as pl
from jax.experimental.pallas import tpu as pltpu
from jax.sharding import PartitionSpec as P

BS = 64
LANES = 128
HALF = LANES // 2
SUB = 8
STEPS = 4
TEAM = 2
MESH = pl.DeviceIdType.MESH
NT = ((1,), (1,))
PLANE = BS * BS // LANES


def iota(shape, dim):
    return lax.broadcasted_iota(jnp.int32, shape, dim)


def pieces(x, count=3):
    out = []
    for _ in range(count):
        high = x.astype(jnp.bfloat16)
        out.append(high)
        x = x - high.astype(jnp.float32)
    return out


def mxu(a, b, contract=((1,), (0,))):
    return lax.dot_general(a, b, (contract, ((), ())), preferred_element_type=jnp.float32)


def wide(x):
    high, low = pieces(x, 2)
    return jnp.concatenate([high, high, low], axis=1)


def tall(x):
    high, low = pieces(x, 2)
    return jnp.concatenate([high, low, high], axis=0)


def hat(x):
    return jnp.maximum(1.0 - jnp.abs(x), 0.0)


def device(chip, e, core, flip):
    return {"brick": 2 * (chip + sum(f for b, f in enumerate(flip) if e >> b & 1)) + core}


def fused(
    n, cap,
    owner_hbm, coords_hbm, fracs_hbm, cells_hbm, counts_hbm, dist_hbm, kernel_hbm, redist_hbm, shatter_hbm,
    out_ref,
    owner_ref, coords_ref, fracs_ref, counts_ref, dist_ref, mats_ref, cells,
    send, relay, recv, index_v, wa_ref, wb_ref, rsend, rrecv,
    load_sem, send_sem, relay_sem, recv_sem, rsend_sem, rrecv_sem,
):
    me = lax.axis_index("brick")
    chips, chip, core = n // 2, me // 2, me % 2
    flip = [(1 - 2 * (chip // bit % 2)) * bit for bit in (1 << b for b in range(chips.bit_length() - 1))]

    def spot(e, c):
        return 4 * (e // 2) + 2 * c + e % 2

    far_first = tuple(reversed(range(chips)))
    rows = cells_hbm.shape[0]
    f32, bf16 = jnp.float32, jnp.bfloat16

    def load(source, target, i):
        return pltpu.make_async_copy(source, target, load_sem.at[i])

    first = [
        load(owner_hbm, owner_ref, 0),
        load(coords_hbm, coords_ref, 1),
        load(fracs_hbm, fracs_ref, 2),
    ]
    later = [
        load(cells_hbm, cells.at[:, pl.ds(0, 3), :], 3),
        load(cells_hbm.at[pl.ds(PLANE, rows - PLANE)], cells.at[pl.ds(0, rows - PLANE), pl.ds(4, 3), :], 4),
        load(counts_hbm, counts_ref, 5),
        load(dist_hbm, dist_ref, 6),
        load(kernel_hbm, mats_ref.at[0], 7),
        load(shatter_hbm, mats_ref.at[1], 8),
        load(redist_hbm, mats_ref.at[2], 9),
    ]
    for copy in first:
        copy.start()
    barrier = pltpu.get_barrier_semaphore()
    for e in far_first[:-1]:
        pl.semaphore_signal(barrier, inc=1, device_id=device(chip, e, 1, flip), device_id_type=MESH)
    pl.semaphore_signal(barrier, inc=1, device_id=device(chip, 0, 1 - core, flip), device_id_type=MESH)
    for copy in later:
        copy.start()
    cells[rows - PLANE, 4:8, :] = jnp.zeros((4, LANES), f32)
    for copy in first:
        copy.wait()

    tracers = owner_ref.shape[1]
    blocks = tracers // LANES
    owner = owner_ref[...]
    apart = (owner >> 1) ^ chip
    rel = 4 * (apart >> 1) + 2 * (owner & 1) + (apart & 1)
    onehot = jnp.where(iota((n, tracers), 0) == rel, 1.0, 0.0)
    upto = jnp.where(iota((LANES, LANES), 0) <= iota((LANES, LANES), 1), 1.0, 0.0).astype(bf16)
    stacked = jnp.concatenate([onehot[:, b * LANES : (b + 1) * LANES] for b in range(blocks)], axis=0)
    counted = mxu(stacked.astype(bf16), upto)
    running = jnp.zeros((n, 1), f32)
    ranks = []
    for b in range(blocks):
        part = counted[b * n : (b + 1) * n]
        ranks.append(jnp.sum(onehot[:, b * LANES : (b + 1) * LANES] * (part + running), axis=0, keepdims=True))
        running = running + part[:, LANES - 1 :]
    rank = jnp.concatenate(ranks, axis=1).astype(jnp.int32) - 1
    placed = jnp.where(iota((LANES, tracers), 0) == rank, 1.0, 0.0).astype(bf16)

    blank = jnp.zeros((1, tracers), f32)
    coords = coords_ref[...].astype(f32)
    fracs = fracs_ref[...]
    high, middle, low = [p.astype(f32) for p in pieces(fracs)]
    main = jnp.concatenate([coords, blank, high, blank], axis=0)
    rest = jnp.concatenate([middle, blank, low, blank], axis=0)
    left = [jnp.where(rel == d, x, 0.0) for x in (main, rest) for d in range(n)]
    packed = mxu(jnp.concatenate(left, axis=0).astype(bf16), placed, NT)
    lower = iota((SUB, LANES), 0) < 4
    for d in range(n):
        x = packed[SUB * d : SUB * (d + 1)]
        y = packed[SUB * (n + d) : SUB * (n + d + 1)]
        x = x + jnp.where(lower, 0.0, y + pltpu.roll(y, 4, 0))
        send[d] = x

    pltpu.make_async_copy(send.at[2 * core], recv.at[2 * core], recv_sem.at[core]).start()

    def pass_on(source, target, e, c, i, sem):
        pltpu.make_async_remote_copy(
            src_ref=source, dst_ref=target, send_sem=send_sem.at[i], recv_sem=sem,
            device_id=device(chip, e, c, flip), device_id_type=MESH,
        ).start()

    @pl.when(core == 0)
    def _():
        pl.semaphore_wait(barrier, 1)
        for g in reversed(range(n // 4)):
            part = pl.ds(4 * g, 4)
            pass_on(send.at[part], relay.at[part], 0, 1, 0, relay_sem.at[g])
        pass_on(send.at[spot(0, 1)], recv.at[spot(0, 0)], 0, 1, 1, recv_sem.at[0])

    @pl.when(core == 1)
    def _():
        pl.semaphore_wait(barrier, n - 1)
        for g in reversed(range(n // 4)):
            for e in (2 * g + 1, 2 * g):
                for c in (0, 1):
                    if e or not c:
                        pass_on(send.at[spot(e, c)], recv.at[spot(e, 1)], e, c, 0, recv_sem.at[2 * g + 1])
        for g in reversed(range(n // 4)):
            part = relay.at[pl.ds(4 * g, 4)]
            pltpu.make_async_copy(part, part, relay_sem.at[g]).wait()
            for e in (2 * g + 1, 2 * g):
                for c in (0, 1):
                    if e:
                        pass_on(relay.at[spot(e, c)], recv.at[spot(e, 0)], e, c, 1, recv_sem.at[2 * g])

    for copy in later[2:]:
        copy.wait()
    steps = counts_ref[...]
    h = 1.0 / jnp.maximum(steps, 1).astype(f32)
    dist = dist_ref[...]
    bins = dist.shape[0]
    both = wide(jnp.concatenate([mats_ref[0], mats_ref[1]], axis=0))
    moved = wide(mats_ref[2])

    def products(dist):
        out = mxu(both, tall(dist))
        dot, broken = out[:bins], out[bins:]
        return dot, broken, mxu(moved, tall(dist * dot))

    ready = products(dist)

    for copy in later[:2]:
        copy.wait()

    row = iota((SUB, LANES), 0)
    lanes = iota((SUB, LANES), 1)
    lane = iota((cap, LANES), 1)
    inner = (lane % HALF).astype(f32)
    outer = (lane // HALF).astype(f32)

    def answer(team, carry):
        start = team * TEAM
        here = recv.at[pl.ds(start, TEAM)]
        pltpu.make_async_copy(here, here, recv_sem.at[team]).wait()
        spots = []
        for u in range(TEAM):
            x = recv[start + u]
            whole = x.astype(jnp.int32)
            spread = jnp.where(row == 0, whole * PLANE, whole >> 1)
            index = (spread + pltpu.roll(spread, SUB - 1, 0)).astype(f32)
            base = jnp.where(row == 1, (whole & 1).astype(f32), x)
            spots.append(jnp.where(row == 0, index, base + pltpu.roll(x, 4, 0)))
        columns = jnp.concatenate(spots, axis=0).T
        whole = jnp.clip(columns[:cap].astype(jnp.int32), 0, rows - PLANE - 1)
        for u in range(TEAM):
            index_v[u] = whole[:, SUB * u : SUB * (u + 1)]
        for u in range(TEAM):
            y = columns[:cap, SUB * u + 1 : SUB * u + 2]
            z = columns[:cap, SUB * u + 2 : SUB * u + 3]
            w = hat(inner - z)
            across = outer - y
            wa_ref[u] = w * hat(across)
            wb_ref[u] = w * hat(across + 2.0)
        for u in range(TEAM):
            acc = jnp.zeros((SUB, LANES), f32)
            for c in range(cap):
                r = index_v[u, c, 0]
                p = cells[r] * wa_ref[u, pl.ds(c, 1), :] + cells[r + 1] * wb_ref[u, pl.ds(c, 1), :]
                acc = jnp.where(lanes == c, jnp.sum(p, axis=1, keepdims=True), acc)
            rsend[start + u] = acc
        base = chip
        for b, f in enumerate(flip[1:]):
            base = base + team // 2 // (1 << b) % 2 * f
        for u in range(TEAM):
            home = 4 * (team // 2) + 2 * core + u
            remote = pltpu.make_async_remote_copy(
                src_ref=rsend.at[start + u], dst_ref=rrecv.at[home], send_sem=rsend_sem, recv_sem=rrecv_sem,
                device_id=device(base, u, team % 2, flip), device_id_type=MESH,
            )
            if u:
                remote.start()
            else:
                pl.when(team != core)(remote.start)

                @pl.when(team == core)
                def _():
                    pltpu.make_async_copy(rsend.at[2 * core], rrecv.at[2 * core], rrecv_sem).start()
        return carry

    lax.fori_loop(0, n // TEAM, answer, 0)

    pltpu.make_async_copy(rrecv, rrecv, rrecv_sem).wait()
    answers = jnp.concatenate(pieces(rrecv[...].reshape(n * SUB, LANES), 2), axis=1)
    found = mxu(answers, jnp.concatenate([placed, placed], axis=0))
    both_ends = jnp.zeros((SUB, tracers), f32)
    for s in range(n):
        both_ends = jnp.where(rel == s, found[SUB * s : SUB * (s + 1)], both_ends)
    f0 = fracs[0:1]
    sampled = [both_ends[f : f + 1] * (1.0 - f0) + both_ends[4 + f : 5 + f] * f0 for f in range(3)]
    coag = sampled[0] * jnp.sqrt(sampled[1])
    shat = sampled[2] * sampled[1]
    for section in range(STEPS):
        dot, broken, back = ready if section == 0 else products(dist)
        gain = coag * back + shat * broken
        loss = coag * dot + shat
        fresh = (dist + h * gain) / (1.0 + h * loss)
        dist = jnp.where(steps >= section + 1, fresh, dist)
    out_ref[...] = dist
    some = rsend.at[pl.ds(1, n - 1)]
    pltpu.make_async_copy(some, some, rsend_sem).wait()

    @pl.when(core == 0)
    def _():
        pltpu.make_async_copy(send, send, send_sem.at[0]).wait()
        pltpu.make_async_copy(send.at[0], send.at[0], send_sem.at[1]).wait()

    @pl.when(core == 1)
    def _():
        own, others = send.at[pl.ds(1, n - 1)], relay.at[pl.ds(2, n - 2)]
        pltpu.make_async_copy(own, own, send_sem.at[0]).wait()
        pltpu.make_async_copy(others, others, send_sem.at[1]).wait()


def shards(grid, distribution, owner_ids, coords, fracs, counts, kernel, redist, shatter):
    n = lax.axis_size("brick")
    bins, tracers = distribution.shape
    cap = 2 * tracers // n
    assert cap <= HALF and n >= 8 and n & (n - 1) == 0 and tracers % LANES == 0
    f32, i32 = jnp.float32, jnp.int32
    cells = jnp.swapaxes(grid.reshape(grid.shape[0], -1, LANES), 0, 1)
    operands = (
        owner_ids.reshape(1, tracers), coords, fracs, cells, counts.reshape(1, tracers),
        distribution, kernel, redist, shatter,
    )
    dma = pltpu.SemaphoreType.DMA
    return pl.pallas_call(
        functools.partial(fused, n, cap),
        out_shape=jax.ShapeDtypeStruct((bins, tracers), f32),
        in_specs=[pl.BlockSpec(memory_space=pltpu.HBM)] * len(operands),
        out_specs=pl.BlockSpec(memory_space=pltpu.VMEM),
        scratch_shapes=[
            pltpu.VMEM((1, tracers), i32),
            pltpu.VMEM(coords.shape, i32),
            pltpu.VMEM(fracs.shape, f32),
            pltpu.VMEM((1, tracers), i32),
            pltpu.VMEM(distribution.shape, f32),
            pltpu.VMEM((3, *kernel.shape), f32),
            pltpu.VMEM((cells.shape[0], SUB, LANES), f32),
            pltpu.VMEM((n, SUB, LANES), f32),
            pltpu.VMEM((n, SUB, LANES), f32),
            pltpu.VMEM((n, SUB, LANES), f32),
            pltpu.VMEM((TEAM, cap, SUB), i32),
            pltpu.VMEM((TEAM, cap, LANES), f32),
            pltpu.VMEM((TEAM, cap, LANES), f32),
            pltpu.VMEM((n, SUB, LANES), f32),
            pltpu.VMEM((n, SUB, LANES), f32),
            dma((10,)), dma((2,)), dma((n // 4,)), dma((n // TEAM,)), dma, dma,
        ],
        compiler_params=pltpu.CompilerParams(
            collective_id=0, has_side_effects=True, vmem_limit_bytes=32 * 1024 * 1024
        ),
        name="fused",
    )(*[pltpu.with_memory_space_constraint(x, pltpu.HBM) for x in operands])


def solution(mesh):
    in_specs = (
        P(None, ("runs", "brick")),
        P(None, ("runs", "brick")),
        P(("runs", "brick"), None),
        P(None, ("runs", "brick")),
        P(None, ("runs", "brick")),
        P(("runs", "brick")),
        P(),
        P(),
        P(),
    )
    out_specs = P(None, ("runs", "brick"))
    return jax.shard_map(shards, mesh=mesh, in_specs=in_specs, out_specs=out_specs, check_vma=False)
```

```python
import functools

import jax
import jax.numpy as jnp
from jax import lax
from jax.experimental import pallas as pl
from jax.experimental.pallas import tpu as pltpu
from jax.sharding import PartitionSpec as P

BS = 64
LANES = 128
HALF = LANES // 2
SUB = 8
STEPS = 4
TEAM = 2
BESIDE = 2
MESH = pl.DeviceIdType.MESH
NT = ((1,), (1,))
PLANE = BS * BS // LANES


def iota(shape, dim):
    return lax.broadcasted_iota(jnp.int32, shape, dim)


def pieces(x, count=3):
    out = []
    for _ in range(count):
        high = x.astype(jnp.bfloat16)
        out.append(high)
        x = x - high.astype(jnp.float32)
    return out


def mxu(a, b, contract=((1,), (0,))):
    return lax.dot_general(a, b, (contract, ((), ())), preferred_element_type=jnp.float32)


def wide(x):
    high, low = pieces(x, 2)
    return jnp.concatenate([high, high, low], axis=1)


def tall(x):
    high, low = pieces(x, 2)
    return jnp.concatenate([high, low, high], axis=0)


def hat(x):
    return jnp.maximum(1.0 - jnp.abs(x), 0.0)


def device(chip, e, core, flip):
    return {"brick": 2 * (chip + sum(f for b, f in enumerate(flip) if e >> b & 1)) + core}


def fused(
    n, cap,
    owner_hbm, coords_hbm, fracs_hbm, cells_hbm, counts_hbm, dist_hbm, kernel_hbm, redist_hbm, shatter_hbm,
    out_ref,
    owner_ref, coords_ref, fracs_ref, counts_ref, dist_ref, mats_ref, cells,
    send, relay, recv, index_v, wa_ref, wb_ref, rsend, rrecv,
    load_sem, send_sem, relay_sem, recv_sem, rsend_sem, rrecv_sem,
):
    me = lax.axis_index("brick")
    rows = cells_hbm.shape[0]
    f32, bf16 = jnp.float32, jnp.bfloat16
    chips, chip, core = n // 2, me // 2, me % 2
    layers, layer, side = n // 4, me // 4, me // 2 % 2
    flip = [(1 - 2 * (chip // bit % 2)) * bit for bit in (1 << b for b in range(chips.bit_length() - 1))]
    inner = (layer + layer // 2) % 2
    passes = inner * core

    def spot(e, c):
        return 4 * (e // 2) + 2 * c + e % 2

    def order(odd):
        return [e for e in reversed(range(chips)) if (e // 2 + e // 4) % 2 == odd]

    def load(source, target, i):
        return pltpu.make_async_copy(source, target, load_sem.at[i])

    first = [
        load(owner_hbm, owner_ref, 0),
        load(coords_hbm, coords_ref, 1),
        load(fracs_hbm, fracs_ref, 2),
    ]
    later = [
        load(cells_hbm, cells.at[:, pl.ds(0, 3), :], 3),
        load(cells_hbm.at[pl.ds(PLANE, rows - PLANE)], cells.at[pl.ds(0, rows - PLANE), pl.ds(4, 3), :], 4),
        load(counts_hbm, counts_ref, 5),
        load(dist_hbm, dist_ref, 6),
        load(kernel_hbm, mats_ref.at[0], 7),
        load(shatter_hbm, mats_ref.at[1], 8),
        load(redist_hbm, mats_ref.at[2], 9),
    ]
    for copy in first:
        copy.start()
    barrier = pltpu.get_barrier_semaphore()

    def enter(e, c):
        pl.semaphore_signal(barrier, inc=1, device_id=device(chip, e, c, flip), device_id_type=MESH)

    @pl.when(inner == 0)
    def _():
        for e in order(1):
            for c in (1, 0):
                enter(e, c)

    @pl.when(inner == 1)
    def _():
        for e in order(0):
            if e:
                for c in (1, 0):
                    enter(e, c)
        enter(0, 1 - core)

    @pl.when(passes == 1)
    def _():
        enter(BESIDE, 0)
        enter(BESIDE, 1)

    for copy in later:
        copy.start()
    cells[rows - PLANE, 4:8, :] = jnp.zeros((4, LANES), f32)
    for copy in first:
        copy.wait()

    tracers = owner_ref.shape[1]
    blocks = tracers // LANES
    owner = owner_ref[...]
    apart = (owner >> 1) ^ chip
    rel = 4 * (apart >> 1) + 2 * (owner & 1) + (apart & 1)
    onehot = jnp.where(iota((n, tracers), 0) == rel, 1.0, 0.0)
    upto = jnp.where(iota((LANES, LANES), 0) <= iota((LANES, LANES), 1), 1.0, 0.0).astype(bf16)
    stacked = jnp.concatenate([onehot[:, b * LANES : (b + 1) * LANES] for b in range(blocks)], axis=0)
    counted = mxu(stacked.astype(bf16), upto)
    running = jnp.zeros((n, 1), f32)
    ranks = []
    for b in range(blocks):
        part = counted[b * n : (b + 1) * n]
        ranks.append(jnp.sum(onehot[:, b * LANES : (b + 1) * LANES] * (part + running), axis=0, keepdims=True))
        running = running + part[:, LANES - 1 :]
    rank = jnp.concatenate(ranks, axis=1).astype(jnp.int32) - 1
    placed = jnp.where(iota((LANES, tracers), 0) == rank, 1.0, 0.0).astype(bf16)

    blank = jnp.zeros((1, tracers), f32)
    coords = coords_ref[...].astype(f32)
    fracs = fracs_ref[...]
    high, middle, low = [p.astype(f32) for p in pieces(fracs)]
    main = jnp.concatenate([coords, blank, high, blank], axis=0)
    rest = jnp.concatenate([middle, blank, low, blank], axis=0)
    left = [jnp.where(rel == d, x, 0.0) for x in (main, rest) for d in range(n)]
    packed = mxu(jnp.concatenate(left, axis=0).astype(bf16), placed, NT)
    lower = iota((SUB, LANES), 0) < 4
    for d in range(n):
        x = packed[SUB * d : SUB * (d + 1)]
        y = packed[SUB * (n + d) : SUB * (n + d + 1)]
        x = x + jnp.where(lower, 0.0, y + pltpu.roll(y, 4, 0))
        send[d] = x

    pltpu.make_async_copy(send.at[2 * core], recv.at[2 * core], recv_sem.at[core]).start()

    def pass_on(source, target, e, c, i, sem):
        pltpu.make_async_remote_copy(
            src_ref=source, dst_ref=target, send_sem=send_sem.at[i], recv_sem=sem,
            device_id=device(chip, e, c, flip), device_id_type=MESH,
        ).start()

    def give():
        for g in reversed(range(layers)):
            pass_on(
                send.at[pl.ds(4 * g, 4)], relay.at[pl.ds(n * core + 4 * g, 4)], BESIDE, 1, 0,
                relay_sem.at[layers * core + g],
            )
        pass_on(
            send.at[spot(BESIDE, 1)], recv.at[spot(BESIDE, core)], BESIDE, 1, 1, recv_sem.at[2 * (BESIDE // 2) + core]
        )

    def mine():
        for e in reversed(range(chips)):
            for c in (0, 1) if e else (1 - core,):
                pass_on(send.at[spot(e, c)], recv.at[spot(e, core)], e, c, 0, recv_sem.at[2 * (e // 2) + core])

    def theirs():
        for g in reversed(range(layers)):
            for k in (0, 1):
                part = relay.at[pl.ds(n * k + 4 * g, 4)]
                pltpu.make_async_copy(part, part, relay_sem.at[layers * k + g]).wait()
                for e in (2 * g + 1, 2 * g):
                    for c in (0, 1):
                        if (e, c) not in ((0, k), (BESIDE, 1)):
                            pass_on(
                                relay.at[n * k + spot(e, c)], recv.at[spot(e, k)], BESIDE ^ e, c, 1,
                                recv_sem.at[2 * g + k],
                            )

    @pl.when(inner == 0)
    def _():
        pl.semaphore_wait(barrier, 1)
        give()

    @pl.when(inner == 1)
    def _():
        pl.semaphore_wait(barrier, n - 1)

        def phase(i, carry):
            first = (i + 2 * layer // layers) % 2
            pl.when(first == 1)(mine)
            pl.when((first == 0) & (core == 1))(theirs)
            return carry

        lax.fori_loop(0, 2, phase, 0)

    for copy in later[2:]:
        copy.wait()
    steps = counts_ref[...]
    h = 1.0 / jnp.maximum(steps, 1).astype(f32)
    dist = dist_ref[...]
    bins = dist.shape[0]
    both = wide(jnp.concatenate([mats_ref[0], mats_ref[1]], axis=0))
    moved = wide(mats_ref[2])

    def products(dist):
        out = mxu(both, tall(dist))
        dot, broken = out[:bins], out[bins:]
        return dot, broken, mxu(moved, tall(dist * dot))

    ready = products(dist)

    for copy in later[:2]:
        copy.wait()

    row = iota((SUB, LANES), 0)
    lanes = iota((SUB, LANES), 1)
    lane = iota((cap, LANES), 1)
    within = (lane % HALF).astype(f32)
    half = (lane // HALF).astype(f32)

    def answer(turn, carry):
        place, kind = turn // 2, turn % 2
        source = place
        for p in range(layers - 1):
            source = jnp.where(place == p, (p + 2) % (layers - 1), source)
        apart = sum((layer // bit + source // bit) % 2 * bit for bit in (1 << b for b in range(layers.bit_length() - 1)))
        team = 2 * apart + kind
        start = team * TEAM
        here = recv.at[pl.ds(start, TEAM)]
        pltpu.make_async_copy(here, here, recv_sem.at[team]).wait()
        spots = []
        for u in range(TEAM):
            x = recv[start + u]
            whole = x.astype(jnp.int32)
            spread = jnp.where(row == 0, whole * PLANE, whole >> 1)
            index = (spread + pltpu.roll(spread, SUB - 1, 0)).astype(f32)
            base = jnp.where(row == 1, (whole & 1).astype(f32), x)
            spots.append(jnp.where(row == 0, index, base + pltpu.roll(x, 4, 0)))
        columns = jnp.concatenate(spots, axis=0).T
        whole = jnp.clip(columns[:cap].astype(jnp.int32), 0, rows - PLANE - 1)
        for u in range(TEAM):
            index_v[u] = whole[:, SUB * u : SUB * (u + 1)]
        for u in range(TEAM):
            y = columns[:cap, SUB * u + 1 : SUB * u + 2]
            z = columns[:cap, SUB * u + 2 : SUB * u + 3]
            w = hat(within - z)
            across = half - y
            wa_ref[u] = w * hat(across)
            wb_ref[u] = w * hat(across + 2.0)
        for u in range(TEAM):
            acc = jnp.zeros((SUB, LANES), f32)
            for c in range(cap):
                r = index_v[u, c, 0]
                p = cells[r] * wa_ref[u, pl.ds(c, 1), :] + cells[r + 1] * wb_ref[u, pl.ds(c, 1), :]
                acc = jnp.where(lanes == c, jnp.sum(p, axis=1, keepdims=True), acc)
            rsend[start + u] = acc
        for u in range(TEAM):
            at = side if u == 0 else 1 - side
            remote = pltpu.make_async_remote_copy(
                src_ref=rsend.at[start + u], dst_ref=rrecv.at[4 * apart + 2 * core + u],
                send_sem=rsend_sem, recv_sem=rrecv_sem,
                device_id={"brick": 4 * source + 2 * at + kind}, device_id_type=MESH,
            )
            if u:
                remote.start()
            else:
                pl.when(team != core)(remote.start)

                @pl.when(team == core)
                def _():
                    pltpu.make_async_copy(rsend.at[2 * core], rrecv.at[2 * core], rrecv_sem).start()
        return carry

    lax.fori_loop(0, n // TEAM, answer, 0)

    pltpu.make_async_copy(rrecv, rrecv, rrecv_sem).wait()
    answers = jnp.concatenate(pieces(rrecv[...].reshape(n * SUB, LANES), 2), axis=1)
    found = mxu(answers, jnp.concatenate([placed, placed], axis=0))
    both_ends = jnp.zeros((SUB, tracers), f32)
    for s in range(n):
        both_ends = jnp.where(rel == s, found[SUB * s : SUB * (s + 1)], both_ends)
    f0 = fracs[0:1]
    sampled = [both_ends[f : f + 1] * (1.0 - f0) + both_ends[4 + f : 5 + f] * f0 for f in range(3)]
    coag = sampled[0] * jnp.sqrt(sampled[1])
    shat = sampled[2] * sampled[1]
    for section in range(STEPS):
        dot, broken, back = ready if section == 0 else products(dist)
        gain = coag * back + shat * broken
        loss = coag * dot + shat
        fresh = (dist + h * gain) / (1.0 + h * loss)
        dist = jnp.where(steps >= section + 1, fresh, dist)
    out_ref[...] = dist
    some = rsend.at[pl.ds(1, n - 1)]
    pltpu.make_async_copy(some, some, rsend_sem).wait()

    @pl.when(inner == 0)
    def _():
        pltpu.make_async_copy(send, send, send_sem.at[0]).wait()
        pltpu.make_async_copy(send.at[0], send.at[0], send_sem.at[1]).wait()

    @pl.when(inner == 1)
    def _():
        own = send.at[pl.ds(1, n - 1)]
        pltpu.make_async_copy(own, own, send_sem.at[0]).wait()

    @pl.when(passes == 1)
    def _():
        others = relay.at[pl.ds(4, 2 * n - 4)]
        pltpu.make_async_copy(others, others, send_sem.at[1]).wait()


def shards(grid, distribution, owner_ids, coords, fracs, counts, kernel, redist, shatter):
    n = lax.axis_size("brick")
    bins, tracers = distribution.shape
    cap = 2 * tracers // n
    assert cap <= HALF and n >= 16 and n & (n - 1) == 0 and tracers % LANES == 0
    f32, i32 = jnp.float32, jnp.int32
    cells = jnp.swapaxes(grid.reshape(grid.shape[0], -1, LANES), 0, 1)
    operands = (
        owner_ids.reshape(1, tracers), coords, fracs, cells, counts.reshape(1, tracers),
        distribution, kernel, redist, shatter,
    )
    dma = pltpu.SemaphoreType.DMA
    return pl.pallas_call(
        functools.partial(fused, n, cap),
        out_shape=jax.ShapeDtypeStruct((bins, tracers), f32),
        in_specs=[pl.BlockSpec(memory_space=pltpu.HBM)] * len(operands),
        out_specs=pl.BlockSpec(memory_space=pltpu.VMEM),
        scratch_shapes=[
            pltpu.VMEM((1, tracers), i32),
            pltpu.VMEM(coords.shape, i32),
            pltpu.VMEM(fracs.shape, f32),
            pltpu.VMEM((1, tracers), i32),
            pltpu.VMEM(distribution.shape, f32),
            pltpu.VMEM((3, *kernel.shape), f32),
            pltpu.VMEM((cells.shape[0], SUB, LANES), f32),
            pltpu.VMEM((n, SUB, LANES), f32),
            pltpu.VMEM((2 * n, SUB, LANES), f32),
            pltpu.VMEM((n, SUB, LANES), f32),
            pltpu.VMEM((TEAM, cap, SUB), i32),
            pltpu.VMEM((TEAM, cap, LANES), f32),
            pltpu.VMEM((TEAM, cap, LANES), f32),
            pltpu.VMEM((n, SUB, LANES), f32),
            pltpu.VMEM((n, SUB, LANES), f32),
            dma((10,)), dma((2,)), dma((n // 2,)), dma((n // TEAM,)), dma, dma,
        ],
        compiler_params=pltpu.CompilerParams(
            collective_id=0, has_side_effects=True, vmem_limit_bytes=32 * 1024 * 1024
        ),
        name="fused",
    )(*[pltpu.with_memory_space_constraint(x, pltpu.HBM) for x in operands])


def solution(mesh):
    in_specs = (
        P(None, ("runs", "brick")),
        P(None, ("runs", "brick")),
        P(("runs", "brick"), None),
        P(None, ("runs", "brick")),
        P(None, ("runs", "brick")),
        P(("runs", "brick")),
        P(),
        P(),
        P(),
    )
    out_specs = P(None, ("runs", "brick"))
    return jax.shard_map(shards, mesh=mesh, in_specs=in_specs, out_specs=out_specs, check_vma=False)
```

```python
import functools

import jax
import jax.numpy as jnp
from jax import lax
from jax.experimental import pallas as pl
from jax.experimental.pallas import tpu as pltpu
from jax.sharding import PartitionSpec as P

BS = 64
LANES = 128
HALF = LANES // 2
SUB = 8
STEPS = 4
TEAM = 2
BESIDE = 2
MESH = pl.DeviceIdType.MESH
NT = ((1,), (1,))
PLANE = BS * BS // LANES


def iota(shape, dim):
    return lax.broadcasted_iota(jnp.int32, shape, dim)


def pieces(x, count=3):
    out = []
    for _ in range(count):
        high = x.astype(jnp.bfloat16)
        out.append(high)
        x = x - high.astype(jnp.float32)
    return out


def mxu(a, b, contract=((1,), (0,))):
    return lax.dot_general(a, b, (contract, ((), ())), preferred_element_type=jnp.float32)


def wide(x):
    high, low = pieces(x, 2)
    return jnp.concatenate([high, high, low], axis=1)


def tall(x):
    high, low = pieces(x, 2)
    return jnp.concatenate([high, low, high], axis=0)


def hat(x):
    return jnp.maximum(1.0 - jnp.abs(x), 0.0)


def device(chip, e, core, flip):
    return {"brick": 2 * (chip + sum(f for b, f in enumerate(flip) if e >> b & 1)) + core}


def fused(
    n, cap,
    owner_hbm, coords_hbm, fracs_hbm, cells_hbm, counts_hbm, dist_hbm, kernel_hbm, redist_hbm, shatter_hbm,
    out_ref,
    owner_ref, coords_ref, fracs_ref, counts_ref, dist_ref, mats_ref, cells,
    send, relay, recv, index_v, wa_ref, wb_ref, rsend, rrecv,
    load_sem, send_sem, relay_sem, recv_sem, rsend_sem, rrecv_sem,
):
    me = lax.axis_index("brick")
    rows = cells_hbm.shape[0]
    f32, bf16 = jnp.float32, jnp.bfloat16
    chips, chip, core = n // 2, me // 2, me % 2
    layers, layer, side = n // 4, me // 4, me // 2 % 2
    flip = [(1 - 2 * (chip // bit % 2)) * bit for bit in (1 << b for b in range(chips.bit_length() - 1))]
    lower = 1 - 2 * layer // layers
    gives = lower * ((layer + layer // 2 + 1) % 2)
    passes = lower * (1 - gives) * core
    senders = [at for at in range(layers) if 2 * at >= layers or (at + at // 2) % 2]

    def spot(e, c):
        return 4 * (e // 2) + 2 * c + e % 2

    def load(source, target, i):
        return pltpu.make_async_copy(source, target, load_sem.at[i])

    first = [
        load(owner_hbm, owner_ref, 0),
        load(coords_hbm, coords_ref, 1),
        load(fracs_hbm, fracs_ref, 2),
    ]
    later = [
        load(cells_hbm, cells.at[:, pl.ds(0, 3), :], 3),
        load(cells_hbm.at[pl.ds(PLANE, rows - PLANE)], cells.at[pl.ds(0, rows - PLANE), pl.ds(4, 3), :], 4),
        load(counts_hbm, counts_ref, 5),
        load(dist_hbm, dist_ref, 6),
        load(kernel_hbm, mats_ref.at[0], 7),
        load(shatter_hbm, mats_ref.at[1], 8),
        load(redist_hbm, mats_ref.at[2], 9),
    ]
    for copy in first:
        copy.start()
    barrier = pltpu.get_barrier_semaphore()

    def enter(device_id):
        pl.semaphore_signal(barrier, inc=1, device_id=device_id, device_id_type=MESH)

    for at in senders:
        for c in (1, 0):
            for d in (4 * at + c, 4 * at + 2 + c):
                pl.when(me != d)(functools.partial(enter, {"brick": d}))

    @pl.when(passes == 1)
    def _():
        enter(device(chip, BESIDE, 0, flip))
        enter(device(chip, BESIDE, 1, flip))

    for copy in later:
        copy.start()
    cells[rows - PLANE, 4:8, :] = jnp.zeros((4, LANES), f32)
    for copy in first:
        copy.wait()

    tracers = owner_ref.shape[1]
    blocks = tracers // LANES
    owner = owner_ref[...]
    apart = (owner >> 1) ^ chip
    rel = 4 * (apart >> 1) + 2 * (owner & 1) + (apart & 1)
    onehot = jnp.where(iota((n, tracers), 0) == rel, 1.0, 0.0)
    upto = jnp.where(iota((LANES, LANES), 0) <= iota((LANES, LANES), 1), 1.0, 0.0).astype(bf16)
    stacked = jnp.concatenate([onehot[:, b * LANES : (b + 1) * LANES] for b in range(blocks)], axis=0)
    counted = mxu(stacked.astype(bf16), upto)
    running = jnp.zeros((n, 1), f32)
    ranks = []
    for b in range(blocks):
        part = counted[b * n : (b + 1) * n]
        ranks.append(jnp.sum(onehot[:, b * LANES : (b + 1) * LANES] * (part + running), axis=0, keepdims=True))
        running = running + part[:, LANES - 1 :]
    rank = jnp.concatenate(ranks, axis=1).astype(jnp.int32) - 1
    placed = jnp.where(iota((LANES, tracers), 0) == rank, 1.0, 0.0).astype(bf16)

    blank = jnp.zeros((1, tracers), f32)
    coords = coords_ref[...].astype(f32)
    fracs = fracs_ref[...]
    high, middle, low = [p.astype(f32) for p in pieces(fracs)]
    main = jnp.concatenate([coords, blank, high, blank], axis=0)
    rest = jnp.concatenate([middle, blank, low, blank], axis=0)
    left = [jnp.where(rel == d, x, 0.0) for x in (main, rest) for d in range(n)]
    packed = mxu(jnp.concatenate(left, axis=0).astype(bf16), placed, NT)
    top = iota((SUB, LANES), 0) < 4
    for d in range(n):
        x = packed[SUB * d : SUB * (d + 1)]
        y = packed[SUB * (n + d) : SUB * (n + d + 1)]
        x = x + jnp.where(top, 0.0, y + pltpu.roll(y, 4, 0))
        send[d] = x

    pltpu.make_async_copy(send.at[2 * core], recv.at[2 * core], recv_sem.at[core]).start()

    def pass_on(source, target, e, c, i, sem):
        pltpu.make_async_remote_copy(
            src_ref=source, dst_ref=target, send_sem=send_sem.at[i], recv_sem=sem,
            device_id=device(chip, e, c, flip), device_id_type=MESH,
        ).start()

    def give():
        for g in reversed(range(layers)):
            pass_on(
                send.at[pl.ds(4 * g, 4)], relay.at[pl.ds(n * core + 4 * g, 4)], BESIDE, 1, 0,
                relay_sem.at[layers * core + g],
            )
        pass_on(
            send.at[spot(BESIDE, 1)], recv.at[spot(BESIDE, core)], BESIDE, 1, 1, recv_sem.at[2 * (BESIDE // 2) + core]
        )

    def mine():
        for e in reversed(range(chips)):
            for c in (0, 1) if e else (1 - core,):
                pass_on(send.at[spot(e, c)], recv.at[spot(e, core)], e, c, 0, recv_sem.at[2 * (e // 2) + core])

    def theirs():
        for g in reversed(range(layers)):
            for k in (0, 1):
                part = relay.at[pl.ds(n * k + 4 * g, 4)]
                pltpu.make_async_copy(part, part, relay_sem.at[layers * k + g]).wait()
                for e in (2 * g + 1, 2 * g):
                    for c in (0, 1):
                        if (e, c) not in ((0, k), (BESIDE, 1)):
                            pass_on(
                                relay.at[n * k + spot(e, c)], recv.at[spot(e, k)], BESIDE ^ e, c, 1,
                                recv_sem.at[2 * g + k],
                            )

    @pl.when(gives == 1)
    def _():
        pl.semaphore_wait(barrier, 1)
        give()

    @pl.when(gives == 0)
    def _():
        pl.semaphore_wait(barrier, n - 1)
        pl.when(passes == 1)(theirs)
        mine()

    for copy in later[2:]:
        copy.wait()
    steps = counts_ref[...]
    h = 1.0 / jnp.maximum(steps, 1).astype(f32)
    dist = dist_ref[...]
    bins = dist.shape[0]
    both = wide(jnp.concatenate([mats_ref[0], mats_ref[1]], axis=0))
    moved = wide(mats_ref[2])

    def products(dist):
        out = mxu(both, tall(dist))
        dot, broken = out[:bins], out[bins:]
        return dot, broken, mxu(moved, tall(dist * dot))

    ready = products(dist)

    for copy in later[:2]:
        copy.wait()

    row = iota((SUB, LANES), 0)
    lanes = iota((SUB, LANES), 1)
    lane = iota((cap, LANES), 1)
    within = (lane % HALF).astype(f32)
    half = (lane // HALF).astype(f32)

    def answer(turn, carry):
        source, kind = turn // 2, turn % 2
        apart = sum((layer // bit + source // bit) % 2 * bit for bit in (1 << b for b in range(layers.bit_length() - 1)))
        team = 2 * apart + kind
        start = team * TEAM
        here = recv.at[pl.ds(start, TEAM)]
        pltpu.make_async_copy(here, here, recv_sem.at[team]).wait()
        spots = []
        for u in range(TEAM):
            x = recv[start + u]
            whole = x.astype(jnp.int32)
            spread = jnp.where(row == 0, whole * PLANE, whole >> 1)
            index = (spread + pltpu.roll(spread, SUB - 1, 0)).astype(f32)
            base = jnp.where(row == 1, (whole & 1).astype(f32), x)
            spots.append(jnp.where(row == 0, index, base + pltpu.roll(x, 4, 0)))
        columns = jnp.concatenate(spots, axis=0).T
        whole = jnp.clip(columns[:cap].astype(jnp.int32), 0, rows - PLANE - 1)
        for u in range(TEAM):
            index_v[u] = whole[:, SUB * u : SUB * (u + 1)]
        for u in range(TEAM):
            y = columns[:cap, SUB * u + 1 : SUB * u + 2]
            z = columns[:cap, SUB * u + 2 : SUB * u + 3]
            w = hat(within - z)
            across = half - y
            wa_ref[u] = w * hat(across)
            wb_ref[u] = w * hat(across + 2.0)
        for u in range(TEAM):
            acc = jnp.zeros((SUB, LANES), f32)
            for c in range(cap):
                r = index_v[u, c, 0]
                p = cells[r] * wa_ref[u, pl.ds(c, 1), :] + cells[r + 1] * wb_ref[u, pl.ds(c, 1), :]
                acc = jnp.where(lanes == c, jnp.sum(p, axis=1, keepdims=True), acc)
            rsend[start + u] = acc
        for u in range(TEAM):
            at = side if u == 0 else 1 - side
            remote = pltpu.make_async_remote_copy(
                src_ref=rsend.at[start + u], dst_ref=rrecv.at[4 * apart + 2 * core + u],
                send_sem=rsend_sem, recv_sem=rrecv_sem,
                device_id={"brick": 4 * source + 2 * at + kind}, device_id_type=MESH,
            )
            if u:
                remote.start()
            else:
                pl.when(team != core)(remote.start)

                @pl.when(team == core)
                def _():
                    pltpu.make_async_copy(rsend.at[2 * core], rrecv.at[2 * core], rrecv_sem).start()
        return carry

    lax.fori_loop(0, n // TEAM, answer, 0)

    pltpu.make_async_copy(rrecv, rrecv, rrecv_sem).wait()
    answers = jnp.concatenate(pieces(rrecv[...].reshape(n * SUB, LANES), 2), axis=1)
    found = mxu(answers, jnp.concatenate([placed, placed], axis=0))
    both_ends = jnp.zeros((SUB, tracers), f32)
    for s in range(n):
        both_ends = jnp.where(rel == s, found[SUB * s : SUB * (s + 1)], both_ends)
    f0 = fracs[0:1]
    sampled = [both_ends[f : f + 1] * (1.0 - f0) + both_ends[4 + f : 5 + f] * f0 for f in range(3)]
    coag = sampled[0] * jnp.sqrt(sampled[1])
    shat = sampled[2] * sampled[1]
    for section in range(STEPS):
        dot, broken, back = ready if section == 0 else products(dist)
        gain = coag * back + shat * broken
        loss = coag * dot + shat
        fresh = (dist + h * gain) / (1.0 + h * loss)
        dist = jnp.where(steps >= section + 1, fresh, dist)
    out_ref[...] = dist
    some = rsend.at[pl.ds(1, n - 1)]
    pltpu.make_async_copy(some, some, rsend_sem).wait()

    @pl.when(gives == 1)
    def _():
        pltpu.make_async_copy(send, send, send_sem.at[0]).wait()
        pltpu.make_async_copy(send.at[0], send.at[0], send_sem.at[1]).wait()

    @pl.when(gives == 0)
    def _():
        own = send.at[pl.ds(1, n - 1)]
        pltpu.make_async_copy(own, own, send_sem.at[0]).wait()

    @pl.when(passes == 1)
    def _():
        others = relay.at[pl.ds(4, 2 * n - 4)]
        pltpu.make_async_copy(others, others, send_sem.at[1]).wait()


def shards(grid, distribution, owner_ids, coords, fracs, counts, kernel, redist, shatter):
    n = lax.axis_size("brick")
    bins, tracers = distribution.shape
    cap = 2 * tracers // n
    assert cap <= HALF and n >= 16 and n & (n - 1) == 0 and tracers % LANES == 0
    f32, i32 = jnp.float32, jnp.int32
    cells = jnp.swapaxes(grid.reshape(grid.shape[0], -1, LANES), 0, 1)
    operands = (
        owner_ids.reshape(1, tracers), coords, fracs, cells, counts.reshape(1, tracers),
        distribution, kernel, redist, shatter,
    )
    dma = pltpu.SemaphoreType.DMA
    return pl.pallas_call(
        functools.partial(fused, n, cap),
        out_shape=jax.ShapeDtypeStruct((bins, tracers), f32),
        in_specs=[pl.BlockSpec(memory_space=pltpu.HBM)] * len(operands),
        out_specs=pl.BlockSpec(memory_space=pltpu.VMEM),
        scratch_shapes=[
            pltpu.VMEM((1, tracers), i32),
            pltpu.VMEM(coords.shape, i32),
            pltpu.VMEM(fracs.shape, f32),
            pltpu.VMEM((1, tracers), i32),
            pltpu.VMEM(distribution.shape, f32),
            pltpu.VMEM((3, *kernel.shape), f32),
            pltpu.VMEM((cells.shape[0], SUB, LANES), f32),
            pltpu.VMEM((n, SUB, LANES), f32),
            pltpu.VMEM((2 * n, SUB, LANES), f32),
            pltpu.VMEM((n, SUB, LANES), f32),
            pltpu.VMEM((TEAM, cap, SUB), i32),
            pltpu.VMEM((TEAM, cap, LANES), f32),
            pltpu.VMEM((TEAM, cap, LANES), f32),
            pltpu.VMEM((n, SUB, LANES), f32),
            pltpu.VMEM((n, SUB, LANES), f32),
            dma((10,)), dma((2,)), dma((n // 2,)), dma((n // TEAM,)), dma, dma,
        ],
        compiler_params=pltpu.CompilerParams(
            collective_id=0, has_side_effects=True, vmem_limit_bytes=32 * 1024 * 1024
        ),
        name="fused",
    )(*[pltpu.with_memory_space_constraint(x, pltpu.HBM) for x in operands])


def solution(mesh):
    in_specs = (
        P(None, ("runs", "brick")),
        P(None, ("runs", "brick")),
        P(("runs", "brick"), None),
        P(None, ("runs", "brick")),
        P(None, ("runs", "brick")),
        P(("runs", "brick")),
        P(),
        P(),
        P(),
    )
    out_specs = P(None, ("runs", "brick"))
    return jax.shard_map(shards, mesh=mesh, in_specs=in_specs, out_specs=out_specs, check_vma=False)
```

```python
import functools

import jax
import jax.numpy as jnp
from jax import lax
from jax.experimental import pallas as pl
from jax.experimental.pallas import tpu as pltpu
from jax.sharding import PartitionSpec as P

BS = 64
LANES = 128
HALF = LANES // 2
SUB = 8
STEPS = 4
TEAM = 2
BESIDE = 2
MESH = pl.DeviceIdType.MESH
NT = ((1,), (1,))
PLANE = BS * BS // LANES


def iota(shape, dim):
    return lax.broadcasted_iota(jnp.int32, shape, dim)


def pieces(x, count=3):
    out = []
    for _ in range(count):
        high = x.astype(jnp.bfloat16)
        out.append(high)
        x = x - high.astype(jnp.float32)
    return out


def mxu(a, b, contract=((1,), (0,))):
    return lax.dot_general(a, b, (contract, ((), ())), preferred_element_type=jnp.float32)


def wide(x):
    high, low = pieces(x, 2)
    return jnp.concatenate([high, high, low], axis=1)


def tall(x):
    high, low = pieces(x, 2)
    return jnp.concatenate([high, low, high], axis=0)


def hat(x):
    return jnp.maximum(1.0 - jnp.abs(x), 0.0)


def device(chip, e, core, flip):
    return {"brick": 2 * (chip + sum(f for b, f in enumerate(flip) if e >> b & 1)) + core}


def fused(
    n, cap,
    owner_hbm, coords_hbm, fracs_hbm, cells_hbm, counts_hbm, dist_hbm, kernel_hbm, redist_hbm, shatter_hbm,
    out_ref,
    owner_ref, coords_ref, fracs_ref, counts_ref, dist_ref, mats_ref, cells,
    send, relay, recv, index_v, wa_ref, wb_ref, rsend, rrecv,
    local_sem, relay_sem, recv_sem, rrecv_sem,
):
    me = lax.axis_index("brick")
    rows = cells_hbm.shape[0]
    f32, bf16 = jnp.float32, jnp.bfloat16
    chips, chip, core = n // 2, me // 2, me % 2
    layers, layer, side = n // 4, me // 4, me // 2 % 2
    flip = [(1 - 2 * (chip // bit % 2)) * bit for bit in (1 << b for b in range(chips.bit_length() - 1))]
    lower = 1 - 2 * layer // layers
    gives = lower * ((layer + layer // 2 + 1) % 2)
    passes = lower * (1 - gives) * core
    senders = [at for at in range(layers) if 2 * at >= layers or (at + at // 2) % 2]

    def spot(e, c):
        return 4 * (e // 2) + 2 * c + e % 2

    def load(source, target, i):
        return pltpu.make_async_copy(source, target, local_sem.at[i])

    first = [
        load(owner_hbm, owner_ref, 0),
        load(coords_hbm, coords_ref, 1),
        load(fracs_hbm, fracs_ref, 2),
    ]
    grid = [
        load(cells_hbm, cells.at[:, pl.ds(0, 3), :], 3),
        load(cells_hbm.at[pl.ds(PLANE, rows - PLANE)], cells.at[pl.ds(0, rows - PLANE), pl.ds(4, 3), :], 4),
    ]
    for copy in first:
        copy.start()
    barrier = pltpu.get_barrier_semaphore()

    def enter(device_id):
        pl.semaphore_signal(barrier, inc=1, device_id=device_id, device_id_type=MESH)

    for at in senders:
        for c in (1, 0):
            for d in (4 * at + c, 4 * at + 2 + c):
                pl.when(me != d)(functools.partial(enter, {"brick": d}))

    @pl.when(passes == 1)
    def _():
        enter(device(chip, BESIDE, 0, flip))
        enter(device(chip, BESIDE, 1, flip))

    @pl.when(gives == 1)
    def _():
        enter(device(chip, 0, 1 - core, flip))
        enter(device(chip, 1, 0, flip))
        enter(device(chip, 1, 1, flip))

    for copy in grid:
        copy.start()
    cells[rows - PLANE, 4:8, :] = jnp.zeros((4, LANES), f32)
    for copy in first:
        copy.wait()
    load(dist_hbm, dist_ref, 0).start()
    for i, matrix in enumerate((kernel_hbm, shatter_hbm, redist_hbm)):
        load(matrix, mats_ref.at[i], 1).start()
    load(counts_hbm, counts_ref, 2).start()

    tracers = owner_ref.shape[1]
    blocks = tracers // LANES
    owner = owner_ref[...]
    apart = (owner >> 1) ^ chip
    rel = 4 * (apart >> 1) + 2 * (owner & 1) + (apart & 1)
    onehot = jnp.where(iota((n, tracers), 0) == rel, 1.0, 0.0)
    upto = jnp.where(iota((LANES, LANES), 0) <= iota((LANES, LANES), 1), 1.0, 0.0).astype(bf16)
    stacked = jnp.concatenate([onehot[:, b * LANES : (b + 1) * LANES] for b in range(blocks)], axis=0)
    counted = mxu(stacked.astype(bf16), upto)
    running = jnp.zeros((n, 1), f32)
    ranks = []
    for b in range(blocks):
        part = counted[b * n : (b + 1) * n]
        ranks.append(jnp.sum(onehot[:, b * LANES : (b + 1) * LANES] * (part + running), axis=0, keepdims=True))
        running = running + part[:, LANES - 1 :]
    rank = jnp.concatenate(ranks, axis=1).astype(jnp.int32) - 1
    placed = jnp.where(iota((LANES, tracers), 0) == rank, 1.0, 0.0).astype(bf16)

    blank = jnp.zeros((1, tracers), f32)
    coords = coords_ref[...].astype(f32)
    fracs = fracs_ref[...]
    high, middle, low = [p.astype(f32) for p in pieces(fracs)]
    main = jnp.concatenate([coords, blank, high, blank], axis=0)
    rest = jnp.concatenate([middle, blank, low, blank], axis=0)
    left = [jnp.where(rel == d, x, 0.0) for x in (main, rest) for d in range(n)]
    packed = mxu(jnp.concatenate(left, axis=0).astype(bf16), placed, NT)
    top = iota((SUB, LANES), 0) < 4
    for d in range(n):
        x = packed[SUB * d : SUB * (d + 1)]
        y = packed[SUB * (n + d) : SUB * (n + d + 1)]
        x = x + jnp.where(top, 0.0, y + pltpu.roll(y, 4, 0))
        send[d] = x

    pltpu.make_async_copy(send.at[2 * core], recv.at[2 * core], recv_sem.at[core]).start()

    def pass_on(source, target, e, c, i, sem):
        pltpu.make_async_remote_copy(
            src_ref=source, dst_ref=target, send_sem=local_sem.at[5 + i], recv_sem=sem,
            device_id=device(chip, e, c, flip), device_id_type=MESH,
        ).start()

    spans = ((3 * layers // 4, layers), (1, 3 * layers // 4))

    def give():
        for i, (a, b) in enumerate(spans):
            size = 4 * (b - a)
            pass_on(
                send.at[pl.ds(4 * a, size)], relay.at[pl.ds(n * core + 4 * a, size)], BESIDE, 1, 0,
                relay_sem.at[2 * core + i],
            )
        pass_on(
            send.at[spot(BESIDE, 1)], recv.at[spot(BESIDE, core)], BESIDE, 1, 1, recv_sem.at[2 * (BESIDE // 2) + core]
        )
        for e, c in ((1, 0), (1, 1), (0, 1 - core)):
            pass_on(send.at[spot(e, c)], recv.at[spot(e, core)], e, c, 1, recv_sem.at[core])

    def mine():
        for e in reversed(range(chips)):
            for c in (0, 1) if e else (1 - core,):
                pass_on(send.at[spot(e, c)], recv.at[spot(e, core)], e, c, 0, recv_sem.at[2 * (e // 2) + core])

    def theirs():
        for i, (a, b) in enumerate(spans):
            for k in (0, 1):
                part = relay.at[pl.ds(n * k + 4 * a, 4 * (b - a))]
                pltpu.make_async_copy(part, part, relay_sem.at[2 * k + i]).wait()
                for e in reversed(range(2 * a, 2 * b)):
                    for c in (0, 1):
                        if (e, c) != (BESIDE, 1):
                            pass_on(
                                relay.at[n * k + spot(e, c)], recv.at[spot(e, k)], BESIDE ^ e, c, 1,
                                recv_sem.at[2 * (e // 2) + k],
                            )

    @pl.when(gives == 1)
    def _():
        pl.semaphore_wait(barrier, 4)
        give()

    @pl.when(gives == 0)
    def _():
        pl.semaphore_wait(barrier, n - 1)
        pl.when(passes == 1)(theirs)
        mine()

    load(dist_hbm, dist_ref, 0).wait()
    pltpu.make_async_copy(mats_ref, mats_ref, local_sem.at[1]).wait()
    load(counts_hbm, counts_ref, 2).wait()
    steps = counts_ref[...]
    h = 1.0 / jnp.maximum(steps, 1).astype(f32)
    dist = dist_ref[...]
    bins = dist.shape[0]
    both = wide(jnp.concatenate([mats_ref[0], mats_ref[1]], axis=0))
    moved = wide(mats_ref[2])

    def products(dist):
        out = mxu(both, tall(dist))
        dot, broken = out[:bins], out[bins:]
        return dot, broken, mxu(moved, tall(dist * dot))

    ready = products(dist)

    for copy in grid:
        copy.wait()

    row = iota((SUB, LANES), 0)
    lanes = iota((SUB, LANES), 1)
    lane = iota((cap, LANES), 1)
    within = (lane % HALF).astype(f32)
    half = (lane // HALF).astype(f32)

    def answer(turn, carry):
        source, kind = turn // 2, turn % 2
        apart = sum((layer // bit + source // bit) % 2 * bit for bit in (1 << b for b in range(layers.bit_length() - 1)))
        team = 2 * apart + kind
        start = team * TEAM
        here = recv.at[pl.ds(start, TEAM)]
        pltpu.make_async_copy(here, here, recv_sem.at[team]).wait()
        spots = []
        for u in range(TEAM):
            x = recv[start + u]
            whole = x.astype(jnp.int32)
            spread = jnp.where(row == 0, whole * PLANE, whole >> 1)
            index = (spread + pltpu.roll(spread, SUB - 1, 0)).astype(f32)
            base = jnp.where(row == 1, (whole & 1).astype(f32), x)
            spots.append(jnp.where(row == 0, index, base + pltpu.roll(x, 4, 0)))
        columns = jnp.concatenate(spots, axis=0).T
        whole = jnp.clip(columns[:cap].astype(jnp.int32), 0, rows - PLANE - 1)
        for u in range(TEAM):
            index_v[u] = whole[:, SUB * u : SUB * (u + 1)]
        for u in range(TEAM):
            y = columns[:cap, SUB * u + 1 : SUB * u + 2]
            z = columns[:cap, SUB * u + 2 : SUB * u + 3]
            w = hat(within - z)
            across = half - y
            wa_ref[u] = w * hat(across)
            wb_ref[u] = w * hat(across + 2.0)
        for u in reversed(range(TEAM)):
            acc = jnp.zeros((SUB, LANES), f32)
            for c in range(cap):
                r = index_v[u, c, 0]
                p = cells[r] * wa_ref[u, pl.ds(c, 1), :] + cells[r + 1] * wb_ref[u, pl.ds(c, 1), :]
                acc = jnp.where(lanes == c, jnp.sum(p, axis=1, keepdims=True), acc)
            rsend[start + u] = acc
            at = side if u == 0 else 1 - side
            remote = pltpu.make_async_remote_copy(
                src_ref=rsend.at[start + u], dst_ref=rrecv.at[4 * apart + 2 * core + u],
                send_sem=local_sem.at[0], recv_sem=rrecv_sem,
                device_id={"brick": 4 * source + 2 * at + kind}, device_id_type=MESH,
            )
            if u:
                remote.start()
            else:
                pl.when(team != core)(remote.start)

                @pl.when(team == core)
                def _():
                    pltpu.make_async_copy(rsend.at[2 * core], rrecv.at[2 * core], rrecv_sem).start()
        return carry

    lax.fori_loop(0, n // TEAM, answer, 0)

    pltpu.make_async_copy(rrecv, rrecv, rrecv_sem).wait()
    answers = jnp.concatenate(pieces(rrecv[...].reshape(n * SUB, LANES), 2), axis=1)
    found = mxu(answers, jnp.concatenate([placed, placed], axis=0))
    both_ends = jnp.zeros((SUB, tracers), f32)
    for s in range(n):
        both_ends = jnp.where(rel == s, found[SUB * s : SUB * (s + 1)], both_ends)
    f0 = fracs[0:1]
    sampled = [both_ends[f : f + 1] * (1.0 - f0) + both_ends[4 + f : 5 + f] * f0 for f in range(3)]
    coag = h * sampled[0] * jnp.sqrt(sampled[1])
    shat = h * sampled[2] * sampled[1]
    for section in range(STEPS):
        dot, broken, back = ready if section == 0 else products(dist)
        active = steps >= section + 1
        c, s = jnp.where(active, coag, 0.0), jnp.where(active, shat, 0.0)
        dist = (dist + (c * back + s * broken)) / ((1.0 + s) + c * dot)
    out_ref[...] = dist
    some = rsend.at[pl.ds(1, n - 1)]
    pltpu.make_async_copy(some, some, local_sem.at[0]).wait()

    @pl.when(gives == 1)
    def _():
        handed, own = send.at[pl.ds(4, n - 4)], send.at[pl.ds(0, 4)]
        pltpu.make_async_copy(handed, handed, local_sem.at[5]).wait()
        pltpu.make_async_copy(own, own, local_sem.at[6]).wait()

    @pl.when(gives == 0)
    def _():
        own = send.at[pl.ds(1, n - 1)]
        pltpu.make_async_copy(own, own, local_sem.at[5]).wait()

    @pl.when(passes == 1)
    def _():
        others = relay.at[pl.ds(0, 2 * (n - 5))]
        pltpu.make_async_copy(others, others, local_sem.at[6]).wait()


def shards(grid, distribution, owner_ids, coords, fracs, counts, kernel, redist, shatter):
    n = lax.axis_size("brick")
    bins, tracers = distribution.shape
    cap = 2 * tracers // n
    assert cap <= HALF and n >= 16 and n & (n - 1) == 0 and tracers % LANES == 0
    f32, i32 = jnp.float32, jnp.int32
    cells = jnp.swapaxes(grid.reshape(grid.shape[0], -1, LANES), 0, 1)
    operands = (
        owner_ids.reshape(1, tracers), coords, fracs, cells, counts.reshape(1, tracers),
        distribution, kernel, redist, shatter,
    )
    dma = pltpu.SemaphoreType.DMA
    return pl.pallas_call(
        functools.partial(fused, n, cap),
        out_shape=jax.ShapeDtypeStruct((bins, tracers), f32),
        in_specs=[pl.BlockSpec(memory_space=pltpu.HBM)] * len(operands),
        out_specs=pl.BlockSpec(memory_space=pltpu.VMEM),
        scratch_shapes=[
            pltpu.VMEM((1, tracers), i32),
            pltpu.VMEM(coords.shape, i32),
            pltpu.VMEM(fracs.shape, f32),
            pltpu.VMEM((1, tracers), i32),
            pltpu.VMEM(distribution.shape, f32),
            pltpu.VMEM((3, *kernel.shape), f32),
            pltpu.VMEM((cells.shape[0], SUB, LANES), f32),
            pltpu.VMEM((n, SUB, LANES), f32),
            pltpu.VMEM((2 * n, SUB, LANES), f32),
            pltpu.VMEM((n, SUB, LANES), f32),
            pltpu.VMEM((TEAM, cap, SUB), i32),
            pltpu.VMEM((TEAM, cap, LANES), f32),
            pltpu.VMEM((TEAM, cap, LANES), f32),
            pltpu.VMEM((n, SUB, LANES), f32),
            pltpu.VMEM((n, SUB, LANES), f32),
            dma((7,)), dma((4,)), dma((n // TEAM,)), dma,
        ],
        compiler_params=pltpu.CompilerParams(
            collective_id=0, has_side_effects=True, vmem_limit_bytes=32 * 1024 * 1024
        ),
        name="fused",
    )(*[pltpu.with_memory_space_constraint(x, pltpu.HBM) for x in operands])


def solution(mesh):
    in_specs = (
        P(None, ("runs", "brick")),
        P(None, ("runs", "brick")),
        P(("runs", "brick"), None),
        P(None, ("runs", "brick")),
        P(None, ("runs", "brick")),
        P(("runs", "brick")),
        P(),
        P(),
        P(),
    )
    out_specs = P(None, ("runs", "brick"))
    return jax.shard_map(shards, mesh=mesh, in_specs=in_specs, out_specs=out_specs, check_vma=False)
```

```python
import functools

import jax
import jax.numpy as jnp
from jax import lax
from jax.experimental import pallas as pl
from jax.experimental.pallas import tpu as pltpu
from jax.sharding import PartitionSpec as P

BS = 64
LANES = 128
HALF = LANES // 2
SUB = 8
STEPS = 4
TEAM = 2
BESIDE = 2
MESH = pl.DeviceIdType.MESH
NT = ((1,), (1,))
PLANE = BS * BS // LANES


def iota(shape, dim):
    return lax.broadcasted_iota(jnp.int32, shape, dim)


def pieces(x, count=3):
    out = []
    for _ in range(count):
        high = x.astype(jnp.bfloat16)
        out.append(high)
        x = x - high.astype(jnp.float32)
    return out


def mxu(a, b, contract=((1,), (0,))):
    return lax.dot_general(a, b, (contract, ((), ())), preferred_element_type=jnp.float32)


def wide(x):
    high, low = pieces(x, 2)
    return jnp.concatenate([high, high, low], axis=1)


def tall(x):
    high, low = pieces(x, 2)
    return jnp.concatenate([high, low, high], axis=0)


def hat(x):
    return jnp.maximum(1.0 - jnp.abs(x), 0.0)


def device(chip, e, core, flip):
    return {"brick": 2 * (chip + sum(f for b, f in enumerate(flip) if e >> b & 1)) + core}


def fused(
    n, cap,
    owner_hbm, coords_hbm, fracs_hbm, cells_hbm, counts_hbm, dist_hbm, kernel_hbm, redist_hbm, shatter_hbm,
    out_ref,
    owner_ref, coords_ref, fracs_ref, counts_ref, dist_ref, mats_ref, cells,
    send, relay, recv, index_v, wa_ref, wb_ref, rsend, rrecv,
    local_sem, relay_sem, recv_sem, rrecv_sem,
):
    me = lax.axis_index("brick")
    rows = cells_hbm.shape[0]
    f32, bf16 = jnp.float32, jnp.bfloat16
    chips, chip, core = n // 2, me // 2, me % 2
    layers, layer, side = n // 4, me // 4, me // 2 % 2
    flip = [(1 - 2 * (chip // bit % 2)) * bit for bit in (1 << b for b in range(chips.bit_length() - 1))]
    lower = 1 - 2 * layer // layers
    gives = lower * ((layer + layer // 2 + 1) % 2)
    passes = lower * (1 - gives) * core
    senders = [at for at in range(layers) if 2 * at >= layers or (at + at // 2) % 2]

    def spot(e, c):
        return 4 * (e // 2) + 2 * c + e % 2

    def load(source, target, i):
        return pltpu.make_async_copy(source, target, local_sem.at[i])

    first = [
        load(owner_hbm, owner_ref, 0),
        load(coords_hbm, coords_ref, 1),
        load(fracs_hbm, fracs_ref, 2),
    ]
    grid = [
        load(cells_hbm, cells.at[:, pl.ds(0, 3), :], 3),
        load(cells_hbm.at[pl.ds(PLANE, rows - PLANE)], cells.at[pl.ds(0, rows - PLANE), pl.ds(4, 3), :], 4),
    ]
    for copy in first:
        copy.start()
    barrier = pltpu.get_barrier_semaphore()

    def enter(device_id):
        pl.semaphore_signal(barrier, inc=1, device_id=device_id, device_id_type=MESH)

    for at in senders:
        for c in (1, 0):
            for d in (4 * at + c, 4 * at + 2 + c):
                pl.when(me != d)(functools.partial(enter, {"brick": d}))

    @pl.when(passes == 1)
    def _():
        enter(device(chip, BESIDE, 0, flip))
        enter(device(chip, BESIDE, 1, flip))

    @pl.when(gives == 1)
    def _():
        enter(device(chip, 0, 1 - core, flip))
        enter(device(chip, 1, 0, flip))
        enter(device(chip, 1, 1, flip))

    for copy in grid:
        copy.start()
    cells[rows - PLANE, 4:8, :] = jnp.zeros((4, LANES), f32)
    for copy in first:
        copy.wait()
    load(dist_hbm, dist_ref, 0).start()
    for i, matrix in enumerate((kernel_hbm, shatter_hbm, redist_hbm)):
        load(matrix, mats_ref.at[i], 1).start()
    load(counts_hbm, counts_ref, 2).start()

    tracers = owner_ref.shape[1]
    blocks = tracers // LANES
    owner = owner_ref[...]
    apart = (owner >> 1) ^ chip
    rel = 4 * (apart >> 1) + 2 * (owner & 1) + (apart & 1)
    onehot = jnp.where(iota((n, tracers), 0) == rel, 1.0, 0.0)
    upto = jnp.where(iota((LANES, LANES), 0) <= iota((LANES, LANES), 1), 1.0, 0.0).astype(bf16)
    stacked = jnp.concatenate([onehot[:, b * LANES : (b + 1) * LANES] for b in range(blocks)], axis=0)
    counted = mxu(stacked.astype(bf16), upto)
    running = jnp.zeros((n, 1), f32)
    ranks = []
    for b in range(blocks):
        part = counted[b * n : (b + 1) * n]
        ranks.append(jnp.sum(onehot[:, b * LANES : (b + 1) * LANES] * (part + running), axis=0, keepdims=True))
        running = running + part[:, LANES - 1 :]
    rank = jnp.concatenate(ranks, axis=1).astype(jnp.int32) - 1
    placed = jnp.where(iota((LANES, tracers), 0) == rank, 1.0, 0.0).astype(bf16)

    blank = jnp.zeros((1, tracers), f32)
    coords = coords_ref[...].astype(f32)
    fracs = fracs_ref[...]
    high, middle, low = [p.astype(f32) for p in pieces(fracs)]
    main = jnp.concatenate([coords, blank, high, blank], axis=0)
    rest = jnp.concatenate([middle, blank, low, blank], axis=0)
    left = [jnp.where(rel == d, x, 0.0) for x in (main, rest) for d in range(n)]
    packed = mxu(jnp.concatenate(left, axis=0).astype(bf16), placed, NT)
    top = iota((SUB, LANES), 0) < 4
    for d in range(n):
        x = packed[SUB * d : SUB * (d + 1)]
        y = packed[SUB * (n + d) : SUB * (n + d + 1)]
        x = x + jnp.where(top, 0.0, y + pltpu.roll(y, 4, 0))
        send[d] = x

    pltpu.make_async_copy(send.at[2 * core], recv.at[2 * core], recv_sem.at[core]).start()

    def pass_on(source, target, e, c, i, sem):
        pltpu.make_async_remote_copy(
            src_ref=source, dst_ref=target, send_sem=local_sem.at[5 + i], recv_sem=sem,
            device_id=device(chip, e, c, flip), device_id_type=MESH,
        ).start()

    spans = ((3 * layers // 4, layers), (1, 3 * layers // 4))

    def give():
        for i, (a, b) in enumerate(spans):
            size = 4 * (b - a)
            pass_on(
                send.at[pl.ds(4 * a, size)], relay.at[pl.ds(n * core + 4 * a, size)], BESIDE, 1, 0,
                relay_sem.at[2 * core + i],
            )
        pass_on(
            send.at[spot(BESIDE, 1)], recv.at[spot(BESIDE, core)], BESIDE, 1, 1, recv_sem.at[2 * (BESIDE // 2) + core]
        )
        for e, c in ((1, 0), (1, 1), (0, 1 - core)):
            pass_on(send.at[spot(e, c)], recv.at[spot(e, core)], e, c, 1, recv_sem.at[core])

    def mine():
        for e in reversed(range(chips)):
            for c in (0, 1) if e else (1 - core,):
                pass_on(send.at[spot(e, c)], recv.at[spot(e, core)], e, c, 0, recv_sem.at[2 * (e // 2) + core])

    def theirs():
        for i, (a, b) in enumerate(spans):
            for k in (0, 1):
                part = relay.at[pl.ds(n * k + 4 * a, 4 * (b - a))]
                pltpu.make_async_copy(part, part, relay_sem.at[2 * k + i]).wait()
                for e in reversed(range(2 * a, 2 * b)):
                    for c in (0, 1):
                        if (e, c) != (BESIDE, 1):
                            pass_on(
                                relay.at[n * k + spot(e, c)], recv.at[spot(e, k)], BESIDE ^ e, c, 1,
                                recv_sem.at[2 * (e // 2) + k],
                            )

    @pl.when(gives == 1)
    def _():
        pl.semaphore_wait(barrier, 4)
        give()

    @pl.when(gives == 0)
    def _():
        pl.semaphore_wait(barrier, n - 1)
        pl.when(passes == 1)(theirs)
        mine()

    load(dist_hbm, dist_ref, 0).wait()
    pltpu.make_async_copy(mats_ref, mats_ref, local_sem.at[1]).wait()
    load(counts_hbm, counts_ref, 2).wait()
    steps = counts_ref[...]
    h = 1.0 / jnp.maximum(steps, 1).astype(f32)
    dist = dist_ref[...]
    bins = dist.shape[0]
    both = wide(jnp.concatenate([mats_ref[0], mats_ref[1]], axis=0))
    moved = wide(mats_ref[2])

    def products(dist):
        out = mxu(both, tall(dist))
        dot, broken = out[:bins], out[bins:]
        return dot, broken, mxu(moved, tall(dist * dot))

    ready = products(dist)

    for copy in grid:
        copy.wait()

    row = iota((SUB, LANES), 0)
    lanes = iota((SUB, LANES), 1)
    lane = iota((cap, LANES), 1)
    within = (lane % HALF).astype(f32)
    half = (lane // HALF).astype(f32)

    def answer(turn, carry):
        source, kind = turn // 2, turn % 2
        apart = sum((layer // bit + source // bit) % 2 * bit for bit in (1 << b for b in range(layers.bit_length() - 1)))
        team = 2 * apart + kind
        start = team * TEAM
        here = recv.at[pl.ds(start, TEAM)]
        pltpu.make_async_copy(here, here, recv_sem.at[team]).wait()
        spots = []
        for u in range(TEAM):
            x = recv[start + u]
            whole = x.astype(jnp.int32)
            spread = jnp.where(row == 0, whole * PLANE, whole >> 1)
            index = (spread + pltpu.roll(spread, SUB - 1, 0)).astype(f32)
            base = jnp.where(row == 1, (whole & 1).astype(f32), x)
            spots.append(jnp.where(row == 0, index, base + pltpu.roll(x, 4, 0)))
        columns = jnp.concatenate(spots, axis=0).T
        whole = jnp.clip(columns[:cap].astype(jnp.int32), 0, rows - PLANE - 1)
        for u in range(TEAM):
            index_v[u] = whole[:, SUB * u : SUB * (u + 1)]
        for u in range(TEAM):
            y = columns[:cap, SUB * u + 1 : SUB * u + 2]
            z = columns[:cap, SUB * u + 2 : SUB * u + 3]
            w = hat(within - z)
            across = half - y
            wa_ref[u] = w * hat(across)
            wb_ref[u] = w * hat(across + 2.0)
        for u in range(TEAM):
            acc = jnp.zeros((SUB, LANES), f32)
            for c in range(cap):
                r = index_v[u, c, 0]
                p = cells[r] * wa_ref[u, pl.ds(c, 1), :] + cells[r + 1] * wb_ref[u, pl.ds(c, 1), :]
                acc = jnp.where(lanes == c, jnp.sum(p, axis=1, keepdims=True), acc)
            rsend[start + u] = acc
        for u in reversed(range(TEAM)):
            at = side if u == 0 else 1 - side
            remote = pltpu.make_async_remote_copy(
                src_ref=rsend.at[start + u], dst_ref=rrecv.at[4 * apart + 2 * core + u],
                send_sem=local_sem.at[0], recv_sem=rrecv_sem,
                device_id={"brick": 4 * source + 2 * at + kind}, device_id_type=MESH,
            )
            if u:
                remote.start()
            else:
                pl.when(team != core)(remote.start)

                @pl.when(team == core)
                def _():
                    pltpu.make_async_copy(rsend.at[2 * core], rrecv.at[2 * core], rrecv_sem).start()
        return carry

    lax.fori_loop(0, n // TEAM, answer, 0)

    pltpu.make_async_copy(rrecv, rrecv, rrecv_sem).wait()
    answers = jnp.concatenate(pieces(rrecv[...].reshape(n * SUB, LANES), 2), axis=1)
    found = mxu(answers, jnp.concatenate([placed, placed], axis=0))
    both_ends = jnp.zeros((SUB, tracers), f32)
    for s in range(n):
        both_ends = jnp.where(rel == s, found[SUB * s : SUB * (s + 1)], both_ends)
    f0 = fracs[0:1]
    sampled = [both_ends[f : f + 1] * (1.0 - f0) + both_ends[4 + f : 5 + f] * f0 for f in range(3)]
    coag = h * sampled[0] * jnp.sqrt(sampled[1])
    shat = h * sampled[2] * sampled[1]
    for section in range(STEPS):
        dot, broken, back = ready if section == 0 else products(dist)
        active = steps >= section + 1
        c, s = jnp.where(active, coag, 0.0), jnp.where(active, shat, 0.0)
        dist = (dist + (c * back + s * broken)) / ((1.0 + s) + c * dot)
    out_ref[...] = dist
    some = rsend.at[pl.ds(1, n - 1)]
    pltpu.make_async_copy(some, some, local_sem.at[0]).wait()

    @pl.when(gives == 1)
    def _():
        handed, own = send.at[pl.ds(4, n - 4)], send.at[pl.ds(0, 4)]
        pltpu.make_async_copy(handed, handed, local_sem.at[5]).wait()
        pltpu.make_async_copy(own, own, local_sem.at[6]).wait()

    @pl.when(gives == 0)
    def _():
        own = send.at[pl.ds(1, n - 1)]
        pltpu.make_async_copy(own, own, local_sem.at[5]).wait()

    @pl.when(passes == 1)
    def _():
        others = relay.at[pl.ds(0, 2 * (n - 5))]
        pltpu.make_async_copy(others, others, local_sem.at[6]).wait()


def shards(grid, distribution, owner_ids, coords, fracs, counts, kernel, redist, shatter):
    n = lax.axis_size("brick")
    bins, tracers = distribution.shape
    cap = 2 * tracers // n
    assert cap <= HALF and n >= 16 and n & (n - 1) == 0 and tracers % LANES == 0
    f32, i32 = jnp.float32, jnp.int32
    cells = jnp.swapaxes(grid.reshape(grid.shape[0], -1, LANES), 0, 1)
    operands = (
        owner_ids.reshape(1, tracers), coords, fracs, cells, counts.reshape(1, tracers),
        distribution, kernel, redist, shatter,
    )
    dma = pltpu.SemaphoreType.DMA
    return pl.pallas_call(
        functools.partial(fused, n, cap),
        out_shape=jax.ShapeDtypeStruct((bins, tracers), f32),
        in_specs=[pl.BlockSpec(memory_space=pltpu.HBM)] * len(operands),
        out_specs=pl.BlockSpec(memory_space=pltpu.VMEM),
        scratch_shapes=[
            pltpu.VMEM((1, tracers), i32),
            pltpu.VMEM(coords.shape, i32),
            pltpu.VMEM(fracs.shape, f32),
            pltpu.VMEM((1, tracers), i32),
            pltpu.VMEM(distribution.shape, f32),
            pltpu.VMEM((3, *kernel.shape), f32),
            pltpu.VMEM((cells.shape[0], SUB, LANES), f32),
            pltpu.VMEM((n, SUB, LANES), f32),
            pltpu.VMEM((2 * n, SUB, LANES), f32),
            pltpu.VMEM((n, SUB, LANES), f32),
            pltpu.VMEM((TEAM, cap, SUB), i32),
            pltpu.VMEM((TEAM, cap, LANES), f32),
            pltpu.VMEM((TEAM, cap, LANES), f32),
            pltpu.VMEM((n, SUB, LANES), f32),
            pltpu.VMEM((n, SUB, LANES), f32),
            dma((7,)), dma((4,)), dma((n // TEAM,)), dma,
        ],
        compiler_params=pltpu.CompilerParams(
            collective_id=0, has_side_effects=True, vmem_limit_bytes=32 * 1024 * 1024
        ),
        name="fused",
    )(*[pltpu.with_memory_space_constraint(x, pltpu.HBM) for x in operands])


def solution(mesh):
    in_specs = (
        P(None, ("runs", "brick")),
        P(None, ("runs", "brick")),
        P(("runs", "brick"), None),
        P(None, ("runs", "brick")),
        P(None, ("runs", "brick")),
        P(("runs", "brick")),
        P(),
        P(),
        P(),
    )
    out_specs = P(None, ("runs", "brick"))
    return jax.shard_map(shards, mesh=mesh, in_specs=in_specs, out_specs=out_specs, check_vma=False)
```

```python
import functools

import jax
import jax.numpy as jnp
from jax import lax
from jax.experimental import pallas as pl
from jax.experimental.pallas import tpu as pltpu
from jax.sharding import PartitionSpec as P

BS = 64
LANES = 128
HALF = LANES // 2
SUB = 8
STEPS = 4
TEAM = 2
BESIDE = 2
MESH = pl.DeviceIdType.MESH
NT = ((1,), (1,))
PLANE = BS * BS // LANES


def iota(shape, dim):
    return lax.broadcasted_iota(jnp.int32, shape, dim)


def pieces(x, count=3):
    out = []
    for _ in range(count):
        high = x.astype(jnp.bfloat16)
        out.append(high)
        x = x - high.astype(jnp.float32)
    return out


def mxu(a, b, contract=((1,), (0,))):
    return lax.dot_general(a, b, (contract, ((), ())), preferred_element_type=jnp.float32)


def wide(x):
    high, low = pieces(x, 2)
    return jnp.concatenate([high, high, low], axis=1)


def tall(x):
    high, low = pieces(x, 2)
    return jnp.concatenate([high, low, high], axis=0)


def hat(x):
    return jnp.maximum(1.0 - jnp.abs(x), 0.0)


def device(chip, e, core, flip):
    return {"brick": 2 * (chip + sum(f for b, f in enumerate(flip) if e >> b & 1)) + core}


def fused(
    n, cap,
    owner_hbm, coords_hbm, fracs_hbm, cells_hbm, counts_hbm, dist_hbm, kernel_hbm, redist_hbm, shatter_hbm,
    out_ref,
    owner_ref, coords_ref, fracs_ref, counts_ref, dist_ref, mats_ref, cells,
    send, relay, recv, index_v, wa_ref, wb_ref, rsend, rrecv,
    relay_sem, recv_sem, rrecv_sem, local_sem,
):
    me = lax.axis_index("brick")
    rows = cells_hbm.shape[0]
    f32, bf16 = jnp.float32, jnp.bfloat16
    chips, chip, core = n // 2, me // 2, me % 2
    layers, layer, side = n // 4, me // 4, me // 2 % 2
    flip = [(1 - 2 * (chip // bit % 2)) * bit for bit in (1 << b for b in range(chips.bit_length() - 1))]
    lower = 1 - 2 * layer // layers
    gives = lower * ((layer + layer // 2 + 1) % 2)
    passes = lower * (1 - gives) * core
    senders = [at for at in range(layers) if 2 * at >= layers or (at + at // 2) % 2]

    def spot(e, c):
        return 4 * (e // 2) + 2 * c + e % 2

    def load(source, target, i):
        return pltpu.make_async_copy(source, target, local_sem.at[i])

    first = [
        load(owner_hbm, owner_ref, 0),
        load(coords_hbm, coords_ref, 1),
        load(fracs_hbm, fracs_ref, 2),
    ]
    grid = [
        load(cells_hbm, cells.at[:, pl.ds(0, 3), :], 3),
        load(cells_hbm.at[pl.ds(PLANE, rows - PLANE)], cells.at[pl.ds(0, rows - PLANE), pl.ds(4, 3), :], 4),
    ]
    for copy in first:
        copy.start()
    barrier = pltpu.get_barrier_semaphore()

    def enter(device_id):
        pl.semaphore_signal(barrier, inc=1, device_id=device_id, device_id_type=MESH)

    for at in senders:
        for c in (1, 0):
            for d in (4 * at + c, 4 * at + 2 + c):
                pl.when(me != d)(functools.partial(enter, {"brick": d}))

    @pl.when(passes == 1)
    def _():
        enter(device(chip, BESIDE, 0, flip))
        enter(device(chip, BESIDE, 1, flip))

    @pl.when(gives == 1)
    def _():
        enter(device(chip, 0, 1 - core, flip))
        enter(device(chip, 1, 0, flip))
        enter(device(chip, 1, 1, flip))

    for copy in grid:
        copy.start()
    cells[rows - PLANE, 4:8, :] = jnp.zeros((4, LANES), f32)
    for copy in first:
        copy.wait()
    load(dist_hbm, dist_ref, 0).start()
    for i, matrix in enumerate((kernel_hbm, shatter_hbm, redist_hbm)):
        load(matrix, mats_ref.at[i], 1).start()
    load(counts_hbm, counts_ref, 2).start()

    tracers = owner_ref.shape[1]
    blocks = tracers // LANES
    owner = owner_ref[...]
    apart = (owner >> 1) ^ chip
    rel = 4 * (apart >> 1) + 2 * (owner & 1) + (apart & 1)
    onehot = jnp.where(iota((n, tracers), 0) == rel, 1.0, 0.0)
    upto = jnp.where(iota((LANES, LANES), 0) <= iota((LANES, LANES), 1), 1.0, 0.0).astype(bf16)
    stacked = jnp.concatenate([onehot[:, b * LANES : (b + 1) * LANES] for b in range(blocks)], axis=0)
    counted = mxu(stacked.astype(bf16), upto)
    running = jnp.zeros((n, 1), f32)
    ranks = []
    for b in range(blocks):
        part = counted[b * n : (b + 1) * n]
        ranks.append(jnp.sum(onehot[:, b * LANES : (b + 1) * LANES] * (part + running), axis=0, keepdims=True))
        running = running + part[:, LANES - 1 :]
    rank = jnp.concatenate(ranks, axis=1).astype(jnp.int32) - 1
    placed = jnp.where(iota((LANES, tracers), 0) == rank, 1.0, 0.0).astype(bf16)
    slot = jnp.clip(rank, 0, LANES - 1)

    blank = jnp.zeros((1, tracers), f32)
    coords = coords_ref[...].astype(f32)
    fracs = fracs_ref[...]
    high, middle, low = [p.astype(f32) for p in pieces(fracs)]
    main = jnp.concatenate([coords, blank, high, blank], axis=0)
    rest = jnp.concatenate([middle, blank, low, blank], axis=0)
    left = [jnp.where(rel == d, x, 0.0) for x in (main, rest) for d in range(n)]
    packed = mxu(jnp.concatenate(left, axis=0).astype(bf16), placed, NT)
    top = iota((SUB, LANES), 0) < 4
    for d in range(n):
        x = packed[SUB * d : SUB * (d + 1)]
        y = packed[SUB * (n + d) : SUB * (n + d + 1)]
        x = x + jnp.where(top, 0.0, y + pltpu.roll(y, 4, 0))
        send[d] = x

    pltpu.make_async_copy(send.at[2 * core], recv.at[2 * core], recv_sem.at[core]).start()

    def pass_on(source, target, e, c, i, sem):
        pltpu.make_async_remote_copy(
            src_ref=source, dst_ref=target, send_sem=local_sem.at[5 + i], recv_sem=sem,
            device_id=device(chip, e, c, flip), device_id_type=MESH,
        ).start()

    most = 3 * layers // 4
    spans = ((most, layers), (1, most))

    def give():
        for i, (a, b) in enumerate(spans):
            size = 4 * (b - a)
            pass_on(
                send.at[pl.ds(4 * a, size)], relay.at[pl.ds(n * core + 4 * a, size)], BESIDE, 1, 0,
                relay_sem.at[2 * core + i],
            )
        pass_on(
            send.at[spot(BESIDE, 1)], recv.at[spot(BESIDE, core)], BESIDE, 1, 1, recv_sem.at[2 * (BESIDE // 2) + core]
        )
        for e, c in ((1, 0), (1, 1), (0, 1 - core)):
            pass_on(send.at[spot(e, c)], recv.at[spot(e, core)], e, c, 1, recv_sem.at[core])

    def mine():
        for e in reversed(range(chips)):
            for c in (0, 1) if e else (1 - core,):
                pass_on(send.at[spot(e, c)], recv.at[spot(e, core)], e, c, 0, recv_sem.at[2 * (e // 2) + core])

    def theirs():
        for i, (a, b) in enumerate(spans):
            for k in (0, 1):
                part = relay.at[pl.ds(n * k + 4 * a, 4 * (b - a))]
                pltpu.make_async_copy(part, part, relay_sem.at[2 * k + i]).wait()
                for e in reversed(range(2 * a, 2 * b)):
                    for c in (0, 1):
                        if (e, c) != (BESIDE, 1):
                            pass_on(
                                relay.at[n * k + spot(e, c)], recv.at[spot(e, k)], BESIDE ^ e, c, 1,
                                recv_sem.at[2 * (e // 2) + k],
                            )

    @pl.when(gives == 1)
    def _():
        pl.semaphore_wait(barrier, 4)
        give()

    @pl.when(gives == 0)
    def _():
        pl.semaphore_wait(barrier, n - 1)
        pl.when(passes == 1)(theirs)
        mine()

    load(dist_hbm, dist_ref, 0).wait()
    pltpu.make_async_copy(mats_ref, mats_ref, local_sem.at[1]).wait()
    load(counts_hbm, counts_ref, 2).wait()
    steps = counts_ref[...]
    h = 1.0 / jnp.maximum(steps, 1).astype(f32)
    dist = dist_ref[...]
    bins = dist.shape[0]
    both = wide(jnp.concatenate([mats_ref[0], mats_ref[1]], axis=0))
    moved = wide(mats_ref[2])

    out = mxu(both, tall(dist))
    dot, broken = out[:bins], out[bins:]
    back = mxu(moved, tall(dist * dot))

    for copy in grid:
        copy.wait()

    row = iota((SUB, LANES), 0)
    lanes = iota((SUB, LANES), 1)
    lane = iota((cap, LANES), 1)
    within = (lane % HALF).astype(f32)
    half = (lane // HALF).astype(f32)

    def answer(turn, carry):
        source, kind = turn // 2, turn % 2
        apart = sum((layer // bit + source // bit) % 2 * bit for bit in (1 << b for b in range(layers.bit_length() - 1)))
        team = 2 * apart + kind
        start = team * TEAM
        here = recv.at[pl.ds(start, TEAM)]
        pltpu.make_async_copy(here, here, recv_sem.at[team]).wait()
        spots = []
        for u in range(TEAM):
            x = recv[start + u]
            whole = x.astype(jnp.int32)
            spread = jnp.where(row == 0, whole * PLANE, whole >> 1)
            index = (spread + pltpu.roll(spread, SUB - 1, 0)).astype(f32)
            base = jnp.where(row == 1, (whole & 1).astype(f32), x)
            spots.append(jnp.where(row == 0, index, base + pltpu.roll(x, 4, 0)))
        columns = jnp.concatenate(spots, axis=0).T
        whole = jnp.clip(columns[:cap].astype(jnp.int32), 0, rows - PLANE - 1)
        for u in range(TEAM):
            index_v[u] = whole[:, SUB * u : SUB * (u + 1)]
        for u in range(TEAM):
            y = columns[:cap, SUB * u + 1 : SUB * u + 2]
            z = columns[:cap, SUB * u + 2 : SUB * u + 3]
            w = hat(within - z)
            across = half - y
            wa_ref[u] = w * hat(across)
            wb_ref[u] = w * hat(across + 2.0)
        for u in range(TEAM):
            acc = jnp.zeros((SUB, LANES), f32)
            for c in range(cap):
                r = index_v[u, c, 0]
                p = cells[r] * wa_ref[u, pl.ds(c, 1), :] + cells[r + 1] * wb_ref[u, pl.ds(c, 1), :]
                acc = jnp.where(lanes == c, jnp.sum(p, axis=1, keepdims=True), acc)
            rsend[start + u] = acc
        for u in reversed(range(TEAM)):
            at = side if u == 0 else 1 - side
            remote = pltpu.make_async_remote_copy(
                src_ref=rsend.at[start + u], dst_ref=rrecv.at[4 * apart + 2 * core + u],
                send_sem=local_sem.at[0], recv_sem=rrecv_sem.at[apart // most],
                device_id={"brick": 4 * source + 2 * at + kind}, device_id_type=MESH,
            )
            if u:
                remote.start()
            else:
                pl.when(team != core)(remote.start)

                @pl.when(team == core)
                def _():
                    pltpu.make_async_copy(rsend.at[2 * core], rrecv.at[2 * core], rrecv_sem.at[0]).start()
        return carry

    lax.fori_loop(0, n // TEAM, answer, 0)

    near, far = rrecv.at[pl.ds(0, 4 * most)], rrecv.at[pl.ds(4 * most, n - 4 * most)]
    pltpu.make_async_copy(near, near, rrecv_sem.at[0]).wait()
    answers = jnp.concatenate(pieces(near[...].reshape(4 * most * SUB, LANES), 2), axis=1)
    found = mxu(answers, jnp.concatenate([placed, placed], axis=0))
    both_ends = jnp.zeros((SUB, tracers), f32)
    for i in range(4 * most):
        both_ends = jnp.where(rel == i, found[SUB * i : SUB * (i + 1)], both_ends)
    pltpu.make_async_copy(far, far, rrecv_sem.at[1]).wait()
    parts = []
    for b in range(blocks):
        block = slice(b * LANES, (b + 1) * LANES)
        part, place = both_ends[:, block], jnp.broadcast_to(slot[:, block], (SUB, LANES))
        for i in range(4 * most, n):
            one = jnp.take_along_axis(rrecv[i], place, axis=1, mode="promise_in_bounds")
            part = jnp.where(rel[:, block] == i, one, part)
        parts.append(part)
    both_ends = jnp.concatenate(parts, axis=1)
    f0 = fracs[0:1]
    sampled = [both_ends[f : f + 1] * (1.0 - f0) + both_ends[4 + f : 5 + f] * f0 for f in range(3)]
    coag = h * sampled[0] * jnp.sqrt(sampled[1])
    shat = h * sampled[2] * sampled[1]
    for section in range(STEPS):
        if section:
            out = mxu(both, tall(dist))
            dot, broken = out[:bins], out[bins:]
            back = mxu(moved, tall(dist * dot))
        active = steps >= section + 1
        c, s = jnp.where(active, coag, 0.0), jnp.where(active, shat, 0.0)
        dist = ((dist + s * broken) + c * back) * (1.0 / ((1.0 + s) + c * dot))
    out_ref[...] = dist
    some = rsend.at[pl.ds(1, n - 1)]
    pltpu.make_async_copy(some, some, local_sem.at[0]).wait()

    @pl.when(gives == 1)
    def _():
        handed, own = send.at[pl.ds(4, n - 4)], send.at[pl.ds(0, 4)]
        pltpu.make_async_copy(handed, handed, local_sem.at[5]).wait()
        pltpu.make_async_copy(own, own, local_sem.at[6]).wait()

    @pl.when(gives == 0)
    def _():
        own = send.at[pl.ds(1, n - 1)]
        pltpu.make_async_copy(own, own, local_sem.at[5]).wait()

    @pl.when(passes == 1)
    def _():
        others = relay.at[pl.ds(0, 2 * (n - 5))]
        pltpu.make_async_copy(others, others, local_sem.at[6]).wait()


def shards(grid, distribution, owner_ids, coords, fracs, counts, kernel, redist, shatter):
    n = lax.axis_size("brick")
    bins, tracers = distribution.shape
    cap = 2 * tracers // n
    assert cap <= HALF and n >= 16 and n & (n - 1) == 0 and tracers % LANES == 0
    f32, i32 = jnp.float32, jnp.int32
    cells = jnp.swapaxes(grid.reshape(grid.shape[0], -1, LANES), 0, 1)
    operands = (
        owner_ids.reshape(1, tracers), coords, fracs, cells, counts.reshape(1, tracers),
        distribution, kernel, redist, shatter,
    )
    dma = pltpu.SemaphoreType.DMA
    return pl.pallas_call(
        lambda *refs: pl.run_scoped(functools.partial(fused, n, cap, *refs), dma((7,))),
        out_shape=jax.ShapeDtypeStruct((bins, tracers), f32),
        in_specs=[pl.BlockSpec(memory_space=pltpu.HBM)] * len(operands),
        out_specs=pl.BlockSpec(memory_space=pltpu.VMEM),
        scratch_shapes=[
            pltpu.VMEM((1, tracers), i32),
            pltpu.VMEM(coords.shape, i32),
            pltpu.VMEM(fracs.shape, f32),
            pltpu.VMEM((1, tracers), i32),
            pltpu.VMEM(distribution.shape, f32),
            pltpu.VMEM((3, *kernel.shape), f32),
            pltpu.VMEM((cells.shape[0], SUB, LANES), f32),
            pltpu.VMEM((n, SUB, LANES), f32),
            pltpu.VMEM((2 * n, SUB, LANES), f32),
            pltpu.VMEM((n, SUB, LANES), f32),
            pltpu.VMEM((TEAM, cap, SUB), i32),
            pltpu.VMEM((TEAM, cap, LANES), f32),
            pltpu.VMEM((TEAM, cap, LANES), f32),
            pltpu.VMEM((n, SUB, LANES), f32),
            pltpu.VMEM((n, SUB, LANES), f32),
            dma((4,)), dma((n // TEAM,)), dma((2,)),
        ],
        compiler_params=pltpu.CompilerParams(
            collective_id=0, has_side_effects=True, vmem_limit_bytes=32 * 1024 * 1024
        ),
        name="fused",
    )(*[pltpu.with_memory_space_constraint(x, pltpu.HBM) for x in operands])


def solution(mesh):
    in_specs = (
        P(None, ("runs", "brick")),
        P(None, ("runs", "brick")),
        P(("runs", "brick"), None),
        P(None, ("runs", "brick")),
        P(None, ("runs", "brick")),
        P(("runs", "brick")),
        P(),
        P(),
        P(),
    )
    out_specs = P(None, ("runs", "brick"))
    return jax.shard_map(shards, mesh=mesh, in_specs=in_specs, out_specs=out_specs, check_vma=False)
```

```python
import functools

import jax
import jax.numpy as jnp
from jax import lax
from jax.experimental import pallas as pl
from jax.experimental.pallas import tpu as pltpu
from jax.sharding import PartitionSpec as P

BS = 64
LANES = 128
HALF = LANES // 2
SUB = 8
STEPS = 4
TEAM = 2
BESIDE = 2
MESH = pl.DeviceIdType.MESH
NT = ((1,), (1,))
PLANE = BS * BS // LANES


def iota(shape, dim):
    return lax.broadcasted_iota(jnp.int32, shape, dim)


def pieces(x, count=3):
    out = []
    for _ in range(count):
        high = x.astype(jnp.bfloat16)
        out.append(high)
        x = x - high.astype(jnp.float32)
    return out


def mxu(a, b, contract=((1,), (0,))):
    return lax.dot_general(a, b, (contract, ((), ())), preferred_element_type=jnp.float32)


def wide(x):
    high, low = pieces(x, 2)
    return jnp.concatenate([high, high, low], axis=1)


def tall(x):
    high, low = pieces(x, 2)
    return jnp.concatenate([high, low, high], axis=0)


def hat(x):
    return jnp.maximum(1.0 - jnp.abs(x), 0.0)


def quotient(x, d):
    return lax.div(x, d)


def remainder(x, d):
    return lax.rem(x, d)


def device(chip, e, core, flip):
    return {"brick": 2 * (chip + sum(f for b, f in enumerate(flip) if e >> b & 1)) + core}


def fused(
    n, cap,
    owner_hbm, coords_hbm, fracs_hbm, cells_hbm, counts_hbm, dist_hbm, kernel_hbm, redist_hbm, shatter_hbm,
    out_ref,
    owner_ref, coords_ref, fracs_ref, counts_ref, dist_ref, mats_ref, cells,
    send, relay, recv, index_v, wa_ref, wb_ref, rsend, rrecv,
    relay_sem, recv_sem, rrecv_sem, local_sem,
):
    me = lax.axis_index("brick")
    rows = cells_hbm.shape[0]
    f32, bf16 = jnp.float32, jnp.bfloat16
    chips, chip, core = n // 2, quotient(me, 2), remainder(me, 2)
    layers, layer, side = n // 4, quotient(me, 4), remainder(quotient(me, 2), 2)
    flip = [(1 - 2 * remainder(quotient(chip, bit), 2)) * bit for bit in (1 << b for b in range(chips.bit_length() - 1))]
    lower = 1 - quotient(2 * layer, layers)
    gives = lower * remainder(layer + quotient(layer, 2) + 1, 2)
    passes = lower * (1 - gives) * core
    senders = [at for at in range(layers) if 2 * at >= layers or (at + at // 2) % 2]

    def spot(e, c):
        return 4 * (e // 2) + 2 * c + e % 2

    def load(source, target, i):
        return pltpu.make_async_copy(source, target, local_sem.at[i])

    first = [
        load(owner_hbm, owner_ref, 0),
        load(coords_hbm, coords_ref, 1),
        load(fracs_hbm, fracs_ref, 2),
    ]
    grid = [
        load(cells_hbm, cells.at[:, pl.ds(0, 3), :], 3),
        load(cells_hbm.at[pl.ds(PLANE, rows - PLANE)], cells.at[pl.ds(0, rows - PLANE), pl.ds(4, 3), :], 4),
    ]
    for copy in first:
        copy.start()
    barrier = pltpu.get_barrier_semaphore()

    def enter(device_id):
        pl.semaphore_signal(barrier, inc=1, device_id=device_id, device_id_type=MESH)

    @pl.when(passes == 1)
    def _():
        enter(device(chip, BESIDE, 0, flip))
        enter(device(chip, BESIDE, 1, flip))

    @pl.when(gives == 1)
    def _():
        enter(device(chip, 0, 1 - core, flip))
        enter(device(chip, 1, 0, flip))
        enter(device(chip, 1, 1, flip))

    for at in senders:
        for c in (1, 0):
            for d in (4 * at + c, 4 * at + 2 + c):
                pl.when(me != d)(functools.partial(enter, {"brick": d}))

    for copy in grid:
        copy.start()
    cells[rows - PLANE, 4:8, :] = jnp.zeros((4, LANES), f32)
    for copy in first:
        copy.wait()
    load(dist_hbm, dist_ref, 0).start()
    for i, matrix in enumerate((kernel_hbm, shatter_hbm, redist_hbm)):
        load(matrix, mats_ref.at[i], 1).start()
    load(counts_hbm, counts_ref, 2).start()

    tracers = owner_ref.shape[1]
    blocks = tracers // LANES
    owner = owner_ref[...]
    apart = (owner >> 1) ^ chip
    rel = 4 * (apart >> 1) + 2 * (owner & 1) + (apart & 1)
    onehot = jnp.where(iota((n, tracers), 0) == rel, 1.0, 0.0)
    upto = jnp.where(iota((LANES, LANES), 0) <= iota((LANES, LANES), 1), 1.0, 0.0).astype(bf16)
    stacked = jnp.concatenate([onehot[:, b * LANES : (b + 1) * LANES] for b in range(blocks)], axis=0)
    counted = mxu(stacked.astype(bf16), upto)
    running = jnp.zeros((n, 1), f32)
    ranks = []
    for b in range(blocks):
        part = counted[b * n : (b + 1) * n]
        ranks.append(jnp.sum(onehot[:, b * LANES : (b + 1) * LANES] * (part + running), axis=0, keepdims=True))
        running = running + part[:, LANES - 1 :]
    rank = jnp.concatenate(ranks, axis=1).astype(jnp.int32) - 1
    placed = jnp.where(iota((LANES, tracers), 0) == rank, 1.0, 0.0).astype(bf16)
    slot = jnp.clip(rank, 0, LANES - 1)

    blank = jnp.zeros((1, tracers), f32)
    coords = coords_ref[...].astype(f32)
    fracs = fracs_ref[...]
    high, middle, low = [p.astype(f32) for p in pieces(fracs)]
    main = jnp.concatenate([coords, blank, high, blank], axis=0)
    rest = jnp.concatenate([middle, blank, low, blank], axis=0)
    left = [jnp.where(rel == d, x, 0.0) for x in (main, rest) for d in range(n)]
    packed = mxu(jnp.concatenate(left, axis=0).astype(bf16), placed, NT)
    top = iota((SUB, LANES), 0) < 4
    for d in range(n):
        x = packed[SUB * d : SUB * (d + 1)]
        y = packed[SUB * (n + d) : SUB * (n + d + 1)]
        x = x + jnp.where(top, 0.0, y + pltpu.roll(y, 4, 0))
        send[d] = x

    pltpu.make_async_copy(send.at[2 * core], recv.at[2 * core], recv_sem.at[core]).start()

    def pass_on(source, target, e, c, i, sem):
        pltpu.make_async_remote_copy(
            src_ref=source, dst_ref=target, send_sem=local_sem.at[5 + i], recv_sem=sem,
            device_id=device(chip, e, c, flip), device_id_type=MESH,
        ).start()

    most = 3 * layers // 4
    spans = ((most, layers), (1, most))

    def give():
        for i, (a, b) in enumerate(spans):
            size = 4 * (b - a)
            pass_on(
                send.at[pl.ds(4 * a, size)], relay.at[pl.ds(n * core + 4 * a, size)], BESIDE, 1, 0,
                relay_sem.at[2 * core + i],
            )
        pass_on(
            send.at[spot(BESIDE, 1)], recv.at[spot(BESIDE, core)], BESIDE, 1, 1, recv_sem.at[2 * (BESIDE // 2) + core]
        )
        for e, c in ((1, 0), (1, 1), (0, 1 - core)):
            pass_on(send.at[spot(e, c)], recv.at[spot(e, core)], e, c, 1, recv_sem.at[core])

    def mine():
        for e in reversed(range(chips)):
            for c in (0, 1) if e else (1 - core,):
                pass_on(send.at[spot(e, c)], recv.at[spot(e, core)], e, c, 0, recv_sem.at[2 * (e // 2) + core])

    def theirs():
        for i, (a, b) in enumerate(spans):
            for k in (0, 1):
                part = relay.at[pl.ds(n * k + 4 * a, 4 * (b - a))]
                pltpu.make_async_copy(part, part, relay_sem.at[2 * k + i]).wait()
                for e in reversed(range(2 * a, 2 * b)):
                    for c in (0, 1):
                        if (e, c) != (BESIDE, 1):
                            pass_on(
                                relay.at[n * k + spot(e, c)], recv.at[spot(e, k)], BESIDE ^ e, c, 1,
                                recv_sem.at[2 * (e // 2) + k],
                            )

    @pl.when(gives == 1)
    def _():
        pl.semaphore_wait(barrier, 4)
        give()

    @pl.when(gives == 0)
    def _():
        pl.semaphore_wait(barrier, n - 1)
        pl.when(passes == 1)(theirs)
        mine()

    load(dist_hbm, dist_ref, 0).wait()
    pltpu.make_async_copy(mats_ref, mats_ref, local_sem.at[1]).wait()
    load(counts_hbm, counts_ref, 2).wait()
    steps = counts_ref[...]
    h = 1.0 / jnp.maximum(steps, 1).astype(f32)
    dist = dist_ref[...]
    bins = dist.shape[0]
    both = wide(jnp.concatenate([mats_ref[0], mats_ref[1]], axis=0))
    moved = wide(mats_ref[2])

    out = mxu(both, tall(dist))
    dot, broken = out[:bins], out[bins:]
    back = mxu(moved, tall(dist * dot))

    for copy in grid:
        copy.wait()

    row = iota((SUB, LANES), 0)
    lanes = iota((SUB, LANES), 1)
    lane = iota((cap, LANES), 1)
    within = (lane % HALF).astype(f32)
    half = (lane // HALF).astype(f32)

    def answer(turn, carry):
        source, kind = quotient(turn, 2), remainder(turn, 2)
        apart = sum(
            remainder(quotient(layer, bit) + quotient(source, bit), 2) * bit
            for bit in (1 << b for b in range(layers.bit_length() - 1))
        )
        team = 2 * apart + kind
        start = team * TEAM
        here = recv.at[pl.ds(start, TEAM)]
        pltpu.make_async_copy(here, here, recv_sem.at[team]).wait()
        spots = []
        for u in range(TEAM):
            x = recv[start + u]
            whole = x.astype(jnp.int32)
            spread = jnp.where(row == 0, whole * PLANE, whole >> 1)
            index = (spread + pltpu.roll(spread, SUB - 1, 0)).astype(f32)
            base = jnp.where(row == 1, (whole & 1).astype(f32), x)
            spots.append(jnp.where(row == 0, index, base + pltpu.roll(x, 4, 0)))
        columns = jnp.concatenate(spots, axis=0).T
        whole = jnp.clip(columns[:cap].astype(jnp.int32), 0, rows - PLANE - 1)
        for u in range(TEAM):
            index_v[u] = whole[:, SUB * u : SUB * (u + 1)]
        for u in range(TEAM):
            y = columns[:cap, SUB * u + 1 : SUB * u + 2]
            z = columns[:cap, SUB * u + 2 : SUB * u + 3]
            w = hat(within - z)
            across = half - y
            wa_ref[u] = w * hat(across)
            wb_ref[u] = w * hat(across + 2.0)
        for u in range(TEAM):
            acc = jnp.zeros((SUB, LANES), f32)
            for c in range(cap):
                r = index_v[u, c, 0]
                p = cells[r] * wa_ref[u, pl.ds(c, 1), :] + cells[r + 1] * wb_ref[u, pl.ds(c, 1), :]
                acc = jnp.where(lanes == c, jnp.sum(p, axis=1, keepdims=True), acc)
            rsend[start + u] = acc
        for u in reversed(range(TEAM)):
            at = side if u == 0 else 1 - side
            remote = pltpu.make_async_remote_copy(
                src_ref=rsend.at[start + u], dst_ref=rrecv.at[4 * apart + 2 * core + u],
                send_sem=local_sem.at[0], recv_sem=rrecv_sem.at[quotient(apart, most)],
                device_id={"brick": 4 * source + 2 * at + kind}, device_id_type=MESH,
            )
            if u:
                remote.start()
            else:
                pl.when(team != core)(remote.start)

                @pl.when(team == core)
                def _():
                    pltpu.make_async_copy(rsend.at[2 * core], rrecv.at[2 * core], rrecv_sem.at[0]).start()
        return carry

    lax.fori_loop(0, n // TEAM, answer, 0)

    near, far = rrecv.at[pl.ds(0, 4 * most)], rrecv.at[pl.ds(4 * most, n - 4 * most)]
    pltpu.make_async_copy(near, near, rrecv_sem.at[0]).wait()
    answers = jnp.concatenate(pieces(near[...].reshape(4 * most * SUB, LANES), 2), axis=1)
    found = mxu(answers, jnp.concatenate([placed, placed], axis=0))
    both_ends = jnp.zeros((SUB, tracers), f32)
    for i in range(4 * most):
        both_ends = jnp.where(rel == i, found[SUB * i : SUB * (i + 1)], both_ends)
    pltpu.make_async_copy(far, far, rrecv_sem.at[1]).wait()
    parts = []
    for b in range(blocks):
        block = slice(b * LANES, (b + 1) * LANES)
        part, place = both_ends[:, block], jnp.broadcast_to(slot[:, block], (SUB, LANES))
        for i in range(4 * most, n):
            one = jnp.take_along_axis(rrecv[i], place, axis=1, mode="promise_in_bounds")
            part = jnp.where(rel[:, block] == i, one, part)
        parts.append(part)
    both_ends = jnp.concatenate(parts, axis=1)
    f0 = fracs[0:1]
    sampled = [both_ends[f : f + 1] * (1.0 - f0) + both_ends[4 + f : 5 + f] * f0 for f in range(3)]
    coag = h * sampled[0] * jnp.sqrt(sampled[1])
    shat = h * sampled[2] * sampled[1]
    for section in range(STEPS):
        if section:
            out = mxu(both, tall(dist))
            dot, broken = out[:bins], out[bins:]
            back = mxu(moved, tall(dist * dot))
        active = steps >= section + 1
        c, s = jnp.where(active, coag, 0.0), jnp.where(active, shat, 0.0)
        dist = ((dist + s * broken) + c * back) * (1.0 / ((1.0 + s) + c * dot))
    out_ref[...] = dist
    some = rsend.at[pl.ds(1, n - 1)]
    pltpu.make_async_copy(some, some, local_sem.at[0]).wait()

    @pl.when(gives == 1)
    def _():
        handed, own = send.at[pl.ds(4, n - 4)], send.at[pl.ds(0, 4)]
        pltpu.make_async_copy(handed, handed, local_sem.at[5]).wait()
        pltpu.make_async_copy(own, own, local_sem.at[6]).wait()

    @pl.when(gives == 0)
    def _():
        own = send.at[pl.ds(1, n - 1)]
        pltpu.make_async_copy(own, own, local_sem.at[5]).wait()

    @pl.when(passes == 1)
    def _():
        others = relay.at[pl.ds(0, 2 * (n - 5))]
        pltpu.make_async_copy(others, others, local_sem.at[6]).wait()


def shards(grid, distribution, owner_ids, coords, fracs, counts, kernel, redist, shatter):
    n = lax.axis_size("brick")
    bins, tracers = distribution.shape
    cap = 2 * tracers // n
    assert cap <= HALF and n >= 16 and n & (n - 1) == 0 and tracers % LANES == 0
    f32, i32 = jnp.float32, jnp.int32
    cells = jnp.swapaxes(grid.reshape(grid.shape[0], -1, LANES), 0, 1)
    operands = (
        owner_ids.reshape(1, tracers), coords, fracs, cells, counts.reshape(1, tracers),
        distribution, kernel, redist, shatter,
    )
    dma = pltpu.SemaphoreType.DMA
    return pl.pallas_call(
        lambda *refs: pl.run_scoped(functools.partial(fused, n, cap, *refs), dma((7,))),
        out_shape=jax.ShapeDtypeStruct((bins, tracers), f32),
        in_specs=[pl.BlockSpec(memory_space=pltpu.HBM)] * len(operands),
        out_specs=pl.BlockSpec(memory_space=pltpu.VMEM),
        scratch_shapes=[
            pltpu.VMEM((1, tracers), i32),
            pltpu.VMEM(coords.shape, i32),
            pltpu.VMEM(fracs.shape, f32),
            pltpu.VMEM((1, tracers), i32),
            pltpu.VMEM(distribution.shape, f32),
            pltpu.VMEM((3, *kernel.shape), f32),
            pltpu.VMEM((cells.shape[0], SUB, LANES), f32),
            pltpu.VMEM((n, SUB, LANES), f32),
            pltpu.VMEM((2 * n, SUB, LANES), f32),
            pltpu.VMEM((n, SUB, LANES), f32),
            pltpu.VMEM((TEAM, cap, SUB), i32),
            pltpu.VMEM((TEAM, cap, LANES), f32),
            pltpu.VMEM((TEAM, cap, LANES), f32),
            pltpu.VMEM((n, SUB, LANES), f32),
            pltpu.VMEM((n, SUB, LANES), f32),
            dma((4,)), dma((n // TEAM,)), dma((2,)),
        ],
        compiler_params=pltpu.CompilerParams(
            collective_id=0, has_side_effects=True, vmem_limit_bytes=32 * 1024 * 1024
        ),
        name="fused",
    )(*[pltpu.with_memory_space_constraint(x, pltpu.HBM) for x in operands])


def solution(mesh):
    in_specs = (
        P(None, ("runs", "brick")),
        P(None, ("runs", "brick")),
        P(("runs", "brick"), None),
        P(None, ("runs", "brick")),
        P(None, ("runs", "brick")),
        P(("runs", "brick")),
        P(),
        P(),
        P(),
    )
    out_specs = P(None, ("runs", "brick"))
    return jax.shard_map(shards, mesh=mesh, in_specs=in_specs, out_specs=out_specs, check_vma=False)
```

```python
import functools

import jax
import jax.numpy as jnp
from jax import lax
from jax.experimental import pallas as pl
from jax.experimental.pallas import tpu as pltpu
from jax.sharding import PartitionSpec as P

BS = 64
LANES = 128
HALF = LANES // 2
SUB = 8
STEPS = 4
TEAM = 4
BESIDE = 2
MESH = pl.DeviceIdType.MESH
NT = ((1,), (1,))
PLANE = BS * BS // LANES


def iota(shape, dim):
    return lax.broadcasted_iota(jnp.int32, shape, dim)


def pieces(x, count=3):
    out = []
    for _ in range(count):
        high = x.astype(jnp.bfloat16)
        out.append(high)
        x = x - high.astype(jnp.float32)
    return out


def mxu(a, b, contract=((1,), (0,))):
    return lax.dot_general(a, b, (contract, ((), ())), preferred_element_type=jnp.float32)


def wide(x):
    high, low = pieces(x, 2)
    return jnp.concatenate([high, high, low], axis=1)


def tall(x):
    high, low = pieces(x, 2)
    return jnp.concatenate([high, low, high], axis=0)


def hat(x):
    return jnp.maximum(1.0 - jnp.abs(x), 0.0)


def quotient(x, d):
    return lax.div(x, d)


def remainder(x, d):
    return lax.rem(x, d)


def device(chip, e, core, flip):
    return {"brick": 2 * (chip + sum(f for b, f in enumerate(flip) if e >> b & 1)) + core}


def fused(
    n, cap,
    owner_hbm, coords_hbm, fracs_hbm, cells_hbm, counts_hbm, dist_hbm, kernel_hbm, redist_hbm, shatter_hbm,
    out_ref,
    owner_ref, coords_ref, fracs_ref, counts_ref, dist_ref, mats_ref, cells,
    send, relay, recv, index_v, wa_ref, wb_ref, rsend, rrecv,
    relay_sem, recv_sem, rrecv_sem, local_sem,
):
    me = lax.axis_index("brick")
    rows = cells_hbm.shape[0]
    f32, bf16 = jnp.float32, jnp.bfloat16
    chips, chip, core = n // 2, quotient(me, 2), remainder(me, 2)
    layers, layer, side = n // 4, quotient(me, 4), remainder(quotient(me, 2), 2)
    flip = [(1 - 2 * remainder(quotient(chip, bit), 2)) * bit for bit in (1 << b for b in range(chips.bit_length() - 1))]
    lower = 1 - quotient(2 * layer, layers)
    gives = lower * remainder(layer + quotient(layer, 2) + 1, 2)
    passes = lower * (1 - gives) * core
    senders = [at for at in range(layers) if 2 * at >= layers or (at + at // 2) % 2]

    def spot(e, c):
        return 4 * (e // 2) + 2 * c + e % 2

    def arrival(source, e, c):
        first = 1 - jnp.minimum(source, 1)
        return first * (2 * (e % 2) + c) + (1 - first) * (3 + source)

    def load(source, target, i):
        return pltpu.make_async_copy(source, target, local_sem.at[i])

    first = [
        load(owner_hbm, owner_ref, 0),
        load(coords_hbm, coords_ref, 1),
        load(fracs_hbm, fracs_ref, 2),
    ]
    grid = [
        load(cells_hbm, cells.at[:, pl.ds(0, 3), :], 3),
        load(cells_hbm.at[pl.ds(PLANE, rows - PLANE)], cells.at[pl.ds(0, rows - PLANE), pl.ds(4, 3), :], 4),
    ]
    for copy in first:
        copy.start()
    barrier = pltpu.get_barrier_semaphore()

    def enter(device_id):
        pl.semaphore_signal(barrier, inc=1, device_id=device_id, device_id_type=MESH)

    @pl.when(passes == 1)
    def _():
        enter(device(chip, BESIDE, 0, flip))
        enter(device(chip, BESIDE, 1, flip))

    @pl.when(gives == 1)
    def _():
        enter(device(chip, 0, 1 - core, flip))
        enter(device(chip, 1, 0, flip))
        enter(device(chip, 1, 1, flip))

    for at in senders:
        for c in (1, 0):
            for d in (4 * at + c, 4 * at + 2 + c):
                pl.when(me != d)(functools.partial(enter, {"brick": d}))

    for copy in grid:
        copy.start()
    cells[rows - PLANE, 4:8, :] = jnp.zeros((4, LANES), f32)
    for copy in first:
        copy.wait()
    load(dist_hbm, dist_ref, 0).start()
    for i, matrix in enumerate((kernel_hbm, shatter_hbm, redist_hbm)):
        load(matrix, mats_ref.at[i], 1).start()
    load(counts_hbm, counts_ref, 2).start()

    tracers = owner_ref.shape[1]
    blocks = tracers // LANES
    owner = owner_ref[...]
    apart = (owner >> 1) ^ chip
    rel = 4 * (apart >> 1) + 2 * (owner & 1) + (apart & 1)
    onehot = jnp.where(iota((n, tracers), 0) == rel, 1.0, 0.0)
    upto = jnp.where(iota((LANES, LANES), 0) <= iota((LANES, LANES), 1), 1.0, 0.0).astype(bf16)
    stacked = jnp.concatenate([onehot[:, b * LANES : (b + 1) * LANES] for b in range(blocks)], axis=0)
    counted = mxu(stacked.astype(bf16), upto)
    running = jnp.zeros((n, 1), f32)
    ranks = []
    for b in range(blocks):
        part = counted[b * n : (b + 1) * n]
        ranks.append(jnp.sum(onehot[:, b * LANES : (b + 1) * LANES] * (part + running), axis=0, keepdims=True))
        running = running + part[:, LANES - 1 :]
    rank = jnp.concatenate(ranks, axis=1).astype(jnp.int32) - 1
    placed = jnp.where(iota((LANES, tracers), 0) == rank, 1.0, 0.0).astype(bf16)
    slot = jnp.clip(rank, 0, LANES - 1)

    blank = jnp.zeros((1, tracers), f32)
    coords = coords_ref[...].astype(f32)
    fracs = fracs_ref[...]
    high, middle, low = [p.astype(f32) for p in pieces(fracs)]
    main = jnp.concatenate([coords, blank, high, blank], axis=0)
    rest = jnp.concatenate([middle, blank, low, blank], axis=0)
    left = [jnp.where(rel == d, x, 0.0) for x in (main, rest) for d in range(n)]
    packed = mxu(jnp.concatenate(left, axis=0).astype(bf16), placed, NT)
    top = iota((SUB, LANES), 0) < 4
    for d in range(n):
        x = packed[SUB * d : SUB * (d + 1)]
        y = packed[SUB * (n + d) : SUB * (n + d + 1)]
        x = x + jnp.where(top, 0.0, y + pltpu.roll(y, 4, 0))
        send[d] = x

    pltpu.make_async_copy(send.at[2 * core], recv.at[2 * core], recv_sem.at[arrival(layer, 0, core)]).start()

    def pass_on(source, target, e, c, i, sem):
        pltpu.make_async_remote_copy(
            src_ref=source, dst_ref=target, send_sem=local_sem.at[5 + i], recv_sem=sem,
            device_id=device(chip, e, c, flip), device_id_type=MESH,
        ).start()

    most = 3 * layers // 4
    spans = ((most, layers), (1, most))

    def give():
        for i, (a, b) in enumerate(spans):
            size = 4 * (b - a)
            pass_on(
                send.at[pl.ds(4 * a, size)], relay.at[pl.ds(n * core + 4 * a, size)], BESIDE, 1, 0,
                relay_sem.at[2 * core + i],
            )
        pass_on(
            send.at[spot(BESIDE, 1)], recv.at[spot(BESIDE, core)], BESIDE, 1, 1,
            recv_sem.at[arrival(layer, BESIDE, core)],
        )
        for e, c in ((1, 0), (1, 1), (0, 1 - core)):
            pass_on(send.at[spot(e, c)], recv.at[spot(e, core)], e, c, 1, recv_sem.at[arrival(layer, e, core)])

    def mine():
        for e in reversed(range(chips)):
            for c in (0, 1) if e else (1 - core,):
                pass_on(send.at[spot(e, c)], recv.at[spot(e, core)], e, c, 0, recv_sem.at[arrival(layer, e, core)])

    def theirs():
        client = layer + flip[1] // 2
        for i, (a, b) in enumerate(spans):
            for k in (0, 1):
                part = relay.at[pl.ds(n * k + 4 * a, 4 * (b - a))]
                pltpu.make_async_copy(part, part, relay_sem.at[2 * k + i]).wait()
                for e in reversed(range(2 * a, 2 * b)):
                    for c in (0, 1):
                        if (e, c) != (BESIDE, 1):
                            pass_on(
                                relay.at[n * k + spot(e, c)], recv.at[spot(e, k)], BESIDE ^ e, c, 1,
                                recv_sem.at[arrival(client, e, k)],
                            )

    @pl.when(gives == 1)
    def _():
        pl.semaphore_wait(barrier, 4)
        give()

    @pl.when(gives == 0)
    def _():
        pl.semaphore_wait(barrier, n - 1)
        pl.when(passes == 1)(theirs)
        mine()

    load(dist_hbm, dist_ref, 0).wait()
    pltpu.make_async_copy(mats_ref, mats_ref, local_sem.at[1]).wait()
    load(counts_hbm, counts_ref, 2).wait()
    steps = counts_ref[...]
    h = 1.0 / jnp.maximum(steps, 1).astype(f32)
    dist = dist_ref[...]
    bins = dist.shape[0]
    both = wide(jnp.concatenate([mats_ref[0], mats_ref[1]], axis=0))
    moved = wide(mats_ref[2])

    out = mxu(both, tall(dist))
    dot, broken = out[:bins], out[bins:]
    back = mxu(moved, tall(dist * dot))

    for copy in grid:
        copy.wait()

    row = iota((SUB, LANES), 0)
    lanes = iota((SUB, LANES), 1)
    lane = iota((cap, LANES), 1)
    within = (lane % HALF).astype(f32)
    half = (lane // HALF).astype(f32)

    def answer(source, which):
        team = len(which)
        apart = sum(
            remainder(quotient(layer, bit) + quotient(source, bit), 2) * bit
            for bit in (1 << b for b in range(layers.bit_length() - 1))
        )
        slots = [4 * apart + 2 * kind + across for across, kind in which]
        here = recv.at[pl.ds(slots[0], team)]
        pltpu.make_async_copy(here, here, recv_sem.at[arrival(source, *which[0])]).wait()
        spots = []
        for slot_u in slots:
            x = recv[slot_u]
            whole = x.astype(jnp.int32)
            spread = jnp.where(row == 0, whole * PLANE, whole >> 1)
            index = (spread + pltpu.roll(spread, SUB - 1, 0)).astype(f32)
            base = jnp.where(row == 1, (whole & 1).astype(f32), x)
            spots.append(jnp.where(row == 0, index, base + pltpu.roll(x, 4, 0)))
        columns = jnp.concatenate(spots, axis=0).T
        whole = jnp.clip(columns[:cap].astype(jnp.int32), 0, rows - PLANE - 1)
        for u in range(team):
            index_v[u] = whole[:, SUB * u : SUB * (u + 1)]
        for u in range(team):
            y = columns[:cap, SUB * u + 1 : SUB * u + 2]
            z = columns[:cap, SUB * u + 2 : SUB * u + 3]
            w = hat(within - z)
            across = half - y
            wa_ref[u] = w * hat(across)
            wb_ref[u] = w * hat(across + 2.0)
        for u in range(team):
            acc = jnp.zeros((SUB, LANES), f32)
            for c in range(cap):
                r = index_v[u, c, 0]
                p = cells[r] * wa_ref[u, pl.ds(c, 1), :] + cells[r + 1] * wb_ref[u, pl.ds(c, 1), :]
                acc = jnp.where(lanes == c, jnp.sum(p, axis=1, keepdims=True), acc)
            rsend[slots[u]] = acc
        for u, (across, kind) in enumerate(which):
            at = side + across * (1 - 2 * side)
            remote = pltpu.make_async_remote_copy(
                src_ref=rsend.at[slots[u]], dst_ref=rrecv.at[4 * apart + 2 * core + across],
                send_sem=local_sem.at[0], recv_sem=rrecv_sem.at[quotient(apart, most)],
                device_id={"brick": 4 * source + 2 * at + kind}, device_id_type=MESH,
            )
            itself = 4 * source + 2 * at + kind == me
            pl.when(jnp.logical_not(itself))(remote.start)

            @pl.when(itself)
            def _():
                pltpu.make_async_copy(rsend.at[2 * core], rrecv.at[2 * core], rrecv_sem.at[0]).start()

    def one(i, carry):
        answer(0, [(quotient(i, 2), remainder(i, 2))])
        return carry

    def four(source, carry):
        answer(source, [(0, 0), (1, 0), (0, 1), (1, 1)])
        return carry

    lax.fori_loop(0, 4, one, 0)
    lax.fori_loop(1, layers, four, 0)

    near, far = rrecv.at[pl.ds(0, 4 * most)], rrecv.at[pl.ds(4 * most, n - 4 * most)]
    pltpu.make_async_copy(near, near, rrecv_sem.at[0]).wait()
    answers = jnp.concatenate(pieces(near[...].reshape(4 * most * SUB, LANES), 2), axis=1)
    found = mxu(answers, jnp.concatenate([placed, placed], axis=0))
    both_ends = jnp.zeros((SUB, tracers), f32)
    for i in range(4 * most):
        both_ends = jnp.where(rel == i, found[SUB * i : SUB * (i + 1)], both_ends)
    pltpu.make_async_copy(far, far, rrecv_sem.at[1]).wait()
    parts = []
    for b in range(blocks):
        block = slice(b * LANES, (b + 1) * LANES)
        part, place = both_ends[:, block], jnp.broadcast_to(slot[:, block], (SUB, LANES))
        for i in range(4 * most, n):
            one = jnp.take_along_axis(rrecv[i], place, axis=1, mode="promise_in_bounds")
            part = jnp.where(rel[:, block] == i, one, part)
        parts.append(part)
    both_ends = jnp.concatenate(parts, axis=1)
    f0 = fracs[0:1]
    sampled = [both_ends[f : f + 1] * (1.0 - f0) + both_ends[4 + f : 5 + f] * f0 for f in range(3)]
    coag = h * sampled[0] * jnp.sqrt(sampled[1])
    shat = h * sampled[2] * sampled[1]
    for section in range(STEPS):
        if section:
            out = mxu(both, tall(dist))
            dot, broken = out[:bins], out[bins:]
            back = mxu(moved, tall(dist * dot))
        active = steps >= section + 1
        c, s = jnp.where(active, coag, 0.0), jnp.where(active, shat, 0.0)
        dist = ((dist + s * broken) + c * back) * (1.0 / ((1.0 + s) + c * dot))
    out_ref[...] = dist
    some = rsend.at[pl.ds(1, n - 1)]
    pltpu.make_async_copy(some, some, local_sem.at[0]).wait()

    @pl.when(gives == 1)
    def _():
        handed, own = send.at[pl.ds(4, n - 4)], send.at[pl.ds(0, 4)]
        pltpu.make_async_copy(handed, handed, local_sem.at[5]).wait()
        pltpu.make_async_copy(own, own, local_sem.at[6]).wait()

    @pl.when(gives == 0)
    def _():
        own = send.at[pl.ds(1, n - 1)]
        pltpu.make_async_copy(own, own, local_sem.at[5]).wait()

    @pl.when(passes == 1)
    def _():
        others = relay.at[pl.ds(0, 2 * (n - 5))]
        pltpu.make_async_copy(others, others, local_sem.at[6]).wait()


def shards(grid, distribution, owner_ids, coords, fracs, counts, kernel, redist, shatter):
    n = lax.axis_size("brick")
    bins, tracers = distribution.shape
    cap = 2 * tracers // n
    assert cap <= HALF and n >= 16 and n & (n - 1) == 0 and tracers % LANES == 0
    f32, i32 = jnp.float32, jnp.int32
    cells = jnp.swapaxes(grid.reshape(grid.shape[0], -1, LANES), 0, 1)
    operands = (
        owner_ids.reshape(1, tracers), coords, fracs, cells, counts.reshape(1, tracers),
        distribution, kernel, redist, shatter,
    )
    dma = pltpu.SemaphoreType.DMA
    return pl.pallas_call(
        lambda *refs: pl.run_scoped(functools.partial(fused, n, cap, *refs), dma((7,))),
        out_shape=jax.ShapeDtypeStruct((bins, tracers), f32),
        in_specs=[pl.BlockSpec(memory_space=pltpu.HBM)] * len(operands),
        out_specs=pl.BlockSpec(memory_space=pltpu.VMEM),
        scratch_shapes=[
            pltpu.VMEM((1, tracers), i32),
            pltpu.VMEM(coords.shape, i32),
            pltpu.VMEM(fracs.shape, f32),
            pltpu.VMEM((1, tracers), i32),
            pltpu.VMEM(distribution.shape, f32),
            pltpu.VMEM((3, *kernel.shape), f32),
            pltpu.VMEM((cells.shape[0], SUB, LANES), f32),
            pltpu.VMEM((n, SUB, LANES), f32),
            pltpu.VMEM((2 * n, SUB, LANES), f32),
            pltpu.VMEM((n, SUB, LANES), f32),
            pltpu.VMEM((TEAM, cap, SUB), i32),
            pltpu.VMEM((TEAM, cap, LANES), f32),
            pltpu.VMEM((TEAM, cap, LANES), f32),
            pltpu.VMEM((n, SUB, LANES), f32),
            pltpu.VMEM((n, SUB, LANES), f32),
            dma((4,)), dma((n // 4 + 3,)), dma((2,)),
        ],
        compiler_params=pltpu.CompilerParams(
            collective_id=0, has_side_effects=True, vmem_limit_bytes=32 * 1024 * 1024
        ),
        name="fused",
    )(*[pltpu.with_memory_space_constraint(x, pltpu.HBM) for x in operands])


def solution(mesh):
    in_specs = (
        P(None, ("runs", "brick")),
        P(None, ("runs", "brick")),
        P(("runs", "brick"), None),
        P(None, ("runs", "brick")),
        P(None, ("runs", "brick")),
        P(("runs", "brick")),
        P(),
        P(),
        P(),
    )
    out_specs = P(None, ("runs", "brick"))
    return jax.shard_map(shards, mesh=mesh, in_specs=in_specs, out_specs=out_specs, check_vma=False)
```

```python
import functools

import jax
import jax.numpy as jnp
from jax import lax
from jax.experimental import pallas as pl
from jax.experimental.pallas import tpu as pltpu
from jax.sharding import PartitionSpec as P

BS = 64
LANES = 128
HALF = LANES // 2
SUB = 8
STEPS = 4
TEAM = 2
BESIDE = 2
MESH = pl.DeviceIdType.MESH
NT = ((1,), (1,))
PLANE = BS * BS // LANES


def iota(shape, dim):
    return lax.broadcasted_iota(jnp.int32, shape, dim)


def pieces(x, count=3):
    out = []
    for _ in range(count):
        high = x.astype(jnp.bfloat16)
        out.append(high)
        x = x - high.astype(jnp.float32)
    return out


def mxu(a, b, contract=((1,), (0,))):
    return lax.dot_general(a, b, (contract, ((), ())), preferred_element_type=jnp.float32)


def wide(x):
    high, low = pieces(x, 2)
    return jnp.concatenate([high, high, low], axis=1)


def tall(x):
    high, low = pieces(x, 2)
    return jnp.concatenate([high, low, high], axis=0)


def hat(x):
    return jnp.maximum(1.0 - jnp.abs(x), 0.0)


def quotient(x, d):
    return lax.div(x, d)


def remainder(x, d):
    return lax.rem(x, d)


def device(chip, e, core, flip):
    return {"brick": 2 * (chip + sum(f for b, f in enumerate(flip) if e >> b & 1)) + core}


def fused(
    n, cap,
    owner_hbm, coords_hbm, fracs_hbm, cells_hbm, counts_hbm, dist_hbm, kernel_hbm, redist_hbm, shatter_hbm,
    out_ref,
    owner_ref, coords_ref, fracs_ref, counts_ref, dist_ref, mats_ref, cells,
    send, relay, across_ref, recv, index_v, wa_ref, wb_ref, rsend, rrecv,
    relay_sem, recv_sem, rrecv_sem, local_sem,
):
    me = lax.axis_index("brick")
    rows = cells_hbm.shape[0]
    f32, bf16 = jnp.float32, jnp.bfloat16
    chips, chip, core = n // 2, quotient(me, 2), remainder(me, 2)
    layers, layer, side = n // 4, quotient(me, 4), remainder(quotient(me, 2), 2)
    flip = [(1 - 2 * remainder(quotient(chip, bit), 2)) * bit for bit in (1 << b for b in range(chips.bit_length() - 1))]
    lower = 1 - quotient(2 * layer, layers)
    gives = lower * remainder(layer + quotient(layer, 2) + 1, 2)
    passes = lower * (1 - gives) * core
    senders = [at for at in range(layers) if 2 * at >= layers or (at + at // 2) % 2]

    def spot(e, c):
        return 4 * (e // 2) + 2 * c + e % 2

    def load(source, target, i):
        return pltpu.make_async_copy(source, target, local_sem.at[i])

    first = [
        load(owner_hbm, owner_ref, 0),
        load(coords_hbm, coords_ref, 1),
        load(fracs_hbm, fracs_ref, 2),
    ]
    grid = [
        load(cells_hbm, cells.at[:, pl.ds(0, 3), :], 3),
        load(cells_hbm.at[pl.ds(PLANE, rows - PLANE)], cells.at[pl.ds(0, rows - PLANE), pl.ds(4, 3), :], 4),
    ]
    for copy in first:
        copy.start()
    barrier = pltpu.get_barrier_semaphore()

    def enter(device_id):
        pl.semaphore_signal(barrier, inc=1, device_id=device_id, device_id_type=MESH)

    @pl.when(passes == 1)
    def _():
        enter(device(chip, BESIDE, 1, flip))
        enter(device(chip, BESIDE ^ 1, 1, flip))

    @pl.when(gives == 1)
    def _():
        enter(device(chip, 0, 1 - core, flip))
        enter(device(chip, 1, 1, flip))

    for at in senders:
        for c in (1, 0):
            for d in (4 * at + c, 4 * at + 2 + c):
                pl.when(me != d)(functools.partial(enter, {"brick": d}))

    for copy in grid:
        copy.start()
    cells[rows - PLANE, 4:8, :] = jnp.zeros((4, LANES), f32)
    for copy in first:
        copy.wait()
    load(dist_hbm, dist_ref, 0).start()
    for i, matrix in enumerate((kernel_hbm, shatter_hbm, redist_hbm)):
        load(matrix, mats_ref.at[i], 1).start()
    load(counts_hbm, counts_ref, 2).start()

    tracers = owner_ref.shape[1]
    blocks = tracers // LANES
    owner = owner_ref[...]
    apart = (owner >> 1) ^ chip
    rel = 4 * (apart >> 1) + 2 * (owner & 1) + (apart & 1)
    onehot = jnp.where(iota((n, tracers), 0) == rel, 1.0, 0.0)
    upto = jnp.where(iota((LANES, LANES), 0) <= iota((LANES, LANES), 1), 1.0, 0.0).astype(bf16)
    stacked = jnp.concatenate([onehot[:, b * LANES : (b + 1) * LANES] for b in range(blocks)], axis=0)
    counted = mxu(stacked.astype(bf16), upto)
    running = jnp.zeros((n, 1), f32)
    ranks = []
    for b in range(blocks):
        part = counted[b * n : (b + 1) * n]
        ranks.append(jnp.sum(onehot[:, b * LANES : (b + 1) * LANES] * (part + running), axis=0, keepdims=True))
        running = running + part[:, LANES - 1 :]
    rank = jnp.concatenate(ranks, axis=1).astype(jnp.int32) - 1
    placed = jnp.where(iota((LANES, tracers), 0) == rank, 1.0, 0.0).astype(bf16)
    slot = jnp.clip(rank, 0, LANES - 1)

    blank = jnp.zeros((1, tracers), f32)
    coords = coords_ref[...].astype(f32)
    fracs = fracs_ref[...]
    high, middle, low = [p.astype(f32) for p in pieces(fracs)]
    main = jnp.concatenate([coords, blank, high, blank], axis=0)
    rest = jnp.concatenate([middle, blank, low, blank], axis=0)
    left = [jnp.where(rel == d, x, 0.0) for x in (main, rest) for d in range(n)]
    packed = mxu(jnp.concatenate(left, axis=0).astype(bf16), placed, NT)
    top = iota((SUB, LANES), 0) < 4
    for d in range(n):
        x = packed[SUB * d : SUB * (d + 1)]
        y = packed[SUB * (n + d) : SUB * (n + d + 1)]
        x = x + jnp.where(top, 0.0, y + pltpu.roll(y, 4, 0))
        send[d] = x

    pltpu.make_async_copy(send.at[2 * core], recv.at[2 * core], recv_sem.at[core]).start()

    def pass_on(source, target, e, c, i, sem):
        pltpu.make_async_remote_copy(
            src_ref=source, dst_ref=target, send_sem=local_sem.at[5 + i], recv_sem=sem,
            device_id=device(chip, e, c, flip), device_id_type=MESH,
        ).start()

    most = 3 * layers // 4
    spans = ((most, layers), (1, most))

    crossing = 2 * (layers - most)

    def entrust():
        pass_on(send, relay.at[pl.ds(0, n)], 0, 1, 0, relay_sem.at[0])
        pass_on(send.at[spot(0, 1)], recv.at[spot(0, 0)], 0, 1, 1, recv_sem.at[0])

    def give():
        other = relay.at[pl.ds(0, n)]
        pltpu.make_async_copy(other, other, relay_sem.at[0]).wait()
        both_cores = ((0, relay, 1), (1, send, 0))
        for k, held, sem in both_cores:
            for g in range(most, layers):
                for c in (0, 1):
                    pass_on(
                        held.at[spot(2 * g + 1, c)], across_ref.at[crossing * k + 2 * (g - most) + c],
                        BESIDE ^ 1, 1, sem, relay_sem.at[4],
                    )
        for i, (a, b) in enumerate(spans):
            for k, held, sem in both_cores:
                size = 4 * (b - a)
                pass_on(
                    held.at[pl.ds(4 * a, size)], relay.at[pl.ds(n * k + 4 * a, size)], BESIDE, 1, sem,
                    relay_sem.at[2 * k + i],
                )
        for k, held, sem in both_cores:
            pass_on(
                held.at[spot(BESIDE, 1)], recv.at[spot(BESIDE, k)], BESIDE, 1, sem, recv_sem.at[2 * (BESIDE // 2) + k]
            )
            for c in (0, 1):
                pass_on(held.at[spot(1, c)], recv.at[spot(1, k)], 1, c, sem, recv_sem.at[k])
        pass_on(send.at[spot(0, 0)], recv.at[spot(0, 1)], 0, 0, 0, recv_sem.at[1])

    def mine():
        for e in reversed(range(chips)):
            for c in (0, 1) if e else (1 - core,):
                pass_on(send.at[spot(e, c)], recv.at[spot(e, core)], e, c, 0, recv_sem.at[2 * (e // 2) + core])

    def theirs():
        pltpu.make_async_copy(across_ref, across_ref, relay_sem.at[4]).wait()
        for k in (0, 1):
            for g in range(most, layers):
                for c in (0, 1):
                    e = 2 * g + 1
                    pass_on(
                        across_ref.at[crossing * k + 2 * (g - most) + c], recv.at[spot(e, k)], BESIDE ^ 1 ^ e, c, 1,
                        recv_sem.at[2 * g + k],
                    )
        for i, (a, b) in enumerate(spans):
            for k in (0, 1):
                part = relay.at[pl.ds(n * k + 4 * a, 4 * (b - a))]
                pltpu.make_async_copy(part, part, relay_sem.at[2 * k + i]).wait()
                for e in reversed(range(2 * a, 2 * b)):
                    for c in (0, 1):
                        if (e, c) != (BESIDE, 1) and (i or e % 2 == 0):
                            pass_on(
                                relay.at[n * k + spot(e, c)], recv.at[spot(e, k)], BESIDE ^ e, c, 1,
                                recv_sem.at[2 * (e // 2) + k],
                            )

    @pl.when(gives == 1)
    def _():
        @pl.when(core == 0)
        def _():
            pl.semaphore_wait(barrier, 1)
            entrust()

        @pl.when(core == 1)
        def _():
            pl.semaphore_wait(barrier, 5)
            give()

    @pl.when(gives == 0)
    def _():
        pl.semaphore_wait(barrier, n - 1)
        pl.when(passes == 1)(theirs)
        mine()

    load(dist_hbm, dist_ref, 0).wait()
    pltpu.make_async_copy(mats_ref, mats_ref, local_sem.at[1]).wait()
    load(counts_hbm, counts_ref, 2).wait()
    steps = counts_ref[...]
    h = 1.0 / jnp.maximum(steps, 1).astype(f32)
    dist = dist_ref[...]
    bins = dist.shape[0]
    both = wide(jnp.concatenate([mats_ref[0], mats_ref[1]], axis=0))
    moved = wide(mats_ref[2])

    out = mxu(both, tall(dist))
    dot, broken = out[:bins], out[bins:]
    back = mxu(moved, tall(dist * dot))

    for copy in grid:
        copy.wait()

    row = iota((SUB, LANES), 0)
    lanes = iota((SUB, LANES), 1)
    lane = iota((cap, LANES), 1)
    within = (lane % HALF).astype(f32)
    half = (lane // HALF).astype(f32)

    def answer(turn, carry):
        source, kind = quotient(turn, 2), remainder(turn, 2)
        apart = sum(
            remainder(quotient(layer, bit) + quotient(source, bit), 2) * bit
            for bit in (1 << b for b in range(layers.bit_length() - 1))
        )
        team = 2 * apart + kind
        start = team * TEAM
        here = recv.at[pl.ds(start, TEAM)]
        pltpu.make_async_copy(here, here, recv_sem.at[team]).wait()
        spots = []
        for u in range(TEAM):
            x = recv[start + u]
            whole = x.astype(jnp.int32)
            spread = jnp.where(row == 0, whole * PLANE, whole >> 1)
            index = (spread + pltpu.roll(spread, SUB - 1, 0)).astype(f32)
            base = jnp.where(row == 1, (whole & 1).astype(f32), x)
            spots.append(jnp.where(row == 0, index, base + pltpu.roll(x, 4, 0)))
        columns = jnp.concatenate(spots, axis=0).T
        whole = jnp.clip(columns[:cap].astype(jnp.int32), 0, rows - PLANE - 1)
        for u in range(TEAM):
            index_v[u] = whole[:, SUB * u : SUB * (u + 1)]
        for u in range(TEAM):
            y = columns[:cap, SUB * u + 1 : SUB * u + 2]
            z = columns[:cap, SUB * u + 2 : SUB * u + 3]
            w = hat(within - z)
            across = half - y
            wa_ref[u] = w * hat(across)
            wb_ref[u] = w * hat(across + 2.0)
        for u in range(TEAM):
            acc = jnp.zeros((SUB, LANES), f32)
            for c in range(cap):
                r = index_v[u, c, 0]
                p = cells[r] * wa_ref[u, pl.ds(c, 1), :] + cells[r + 1] * wb_ref[u, pl.ds(c, 1), :]
                acc = jnp.where(lanes == c, jnp.sum(p, axis=1, keepdims=True), acc)
            rsend[start + u] = acc
        for u in reversed(range(TEAM)):
            at = side if u == 0 else 1 - side
            remote = pltpu.make_async_remote_copy(
                src_ref=rsend.at[start + u], dst_ref=rrecv.at[4 * apart + 2 * core + u],
                send_sem=local_sem.at[0], recv_sem=rrecv_sem.at[quotient(apart, most)],
                device_id={"brick": 4 * source + 2 * at + kind}, device_id_type=MESH,
            )
            if u:
                remote.start()
            else:
                pl.when(team != core)(remote.start)

                @pl.when(team == core)
                def _():
                    pltpu.make_async_copy(rsend.at[2 * core], rrecv.at[2 * core], rrecv_sem.at[0]).start()
        return carry

    lax.fori_loop(0, n // TEAM, answer, 0)

    near, far = rrecv.at[pl.ds(0, 4 * most)], rrecv.at[pl.ds(4 * most, n - 4 * most)]
    pltpu.make_async_copy(near, near, rrecv_sem.at[0]).wait()
    answers = jnp.concatenate(pieces(near[...].reshape(4 * most * SUB, LANES), 2), axis=1)
    found = mxu(answers, jnp.concatenate([placed, placed], axis=0))
    both_ends = jnp.zeros((SUB, tracers), f32)
    for i in range(4 * most):
        both_ends = jnp.where(rel == i, found[SUB * i : SUB * (i + 1)], both_ends)
    pltpu.make_async_copy(far, far, rrecv_sem.at[1]).wait()
    parts = []
    for b in range(blocks):
        block = slice(b * LANES, (b + 1) * LANES)
        part, place = both_ends[:, block], jnp.broadcast_to(slot[:, block], (SUB, LANES))
        for i in range(4 * most, n):
            one = jnp.take_along_axis(rrecv[i], place, axis=1, mode="promise_in_bounds")
            part = jnp.where(rel[:, block] == i, one, part)
        parts.append(part)
    both_ends = jnp.concatenate(parts, axis=1)
    f0 = fracs[0:1]
    sampled = [both_ends[f : f + 1] * (1.0 - f0) + both_ends[4 + f : 5 + f] * f0 for f in range(3)]
    coag = h * sampled[0] * jnp.sqrt(sampled[1])
    shat = h * sampled[2] * sampled[1]
    for section in range(STEPS):
        if section:
            out = mxu(both, tall(dist))
            dot, broken = out[:bins], out[bins:]
            back = mxu(moved, tall(dist * dot))
        active = steps >= section + 1
        c, s = jnp.where(active, coag, 0.0), jnp.where(active, shat, 0.0)
        dist = ((dist + s * broken) + c * back) * (1.0 / ((1.0 + s) + c * dot))
    out_ref[...] = dist
    some = rsend.at[pl.ds(1, n - 1)]
    pltpu.make_async_copy(some, some, local_sem.at[0]).wait()

    @pl.when(gives == 1)
    def _():
        @pl.when(core == 0)
        def _():
            pltpu.make_async_copy(send, send, local_sem.at[5]).wait()
            pltpu.make_async_copy(send.at[0], send.at[0], local_sem.at[6]).wait()

        @pl.when(core == 1)
        def _():
            for extra, i in ((0, 5), (1, 6)):
                handed = relay.at[pl.ds(0, n + crossing - extra)]
                pltpu.make_async_copy(handed, handed, local_sem.at[i]).wait()

    @pl.when(gives == 0)
    def _():
        own = send.at[pl.ds(1, n - 1)]
        pltpu.make_async_copy(own, own, local_sem.at[5]).wait()

    @pl.when(passes == 1)
    def _():
        others = relay.at[pl.ds(0, 4 * crossing + 8 * (most - 1) - 2)]
        pltpu.make_async_copy(others, others, local_sem.at[6]).wait()


def shards(grid, distribution, owner_ids, coords, fracs, counts, kernel, redist, shatter):
    n = lax.axis_size("brick")
    bins, tracers = distribution.shape
    cap = 2 * tracers // n
    assert cap <= HALF and n >= 16 and n & (n - 1) == 0 and tracers % LANES == 0
    f32, i32 = jnp.float32, jnp.int32
    cells = jnp.swapaxes(grid.reshape(grid.shape[0], -1, LANES), 0, 1)
    operands = (
        owner_ids.reshape(1, tracers), coords, fracs, cells, counts.reshape(1, tracers),
        distribution, kernel, redist, shatter,
    )
    dma = pltpu.SemaphoreType.DMA
    return pl.pallas_call(
        lambda *refs: pl.run_scoped(functools.partial(fused, n, cap, *refs), dma((7,))),
        out_shape=jax.ShapeDtypeStruct((bins, tracers), f32),
        in_specs=[pl.BlockSpec(memory_space=pltpu.HBM)] * len(operands),
        out_specs=pl.BlockSpec(memory_space=pltpu.VMEM),
        scratch_shapes=[
            pltpu.VMEM((1, tracers), i32),
            pltpu.VMEM(coords.shape, i32),
            pltpu.VMEM(fracs.shape, f32),
            pltpu.VMEM((1, tracers), i32),
            pltpu.VMEM(distribution.shape, f32),
            pltpu.VMEM((3, *kernel.shape), f32),
            pltpu.VMEM((cells.shape[0], SUB, LANES), f32),
            pltpu.VMEM((n, SUB, LANES), f32),
            pltpu.VMEM((2 * n, SUB, LANES), f32),
            pltpu.VMEM((4 * (n // 4 - 3 * (n // 4) // 4), SUB, LANES), f32),
            pltpu.VMEM((n, SUB, LANES), f32),
            pltpu.VMEM((TEAM, cap, SUB), i32),
            pltpu.VMEM((TEAM, cap, LANES), f32),
            pltpu.VMEM((TEAM, cap, LANES), f32),
            pltpu.VMEM((n, SUB, LANES), f32),
            pltpu.VMEM((n, SUB, LANES), f32),
            dma((5,)), dma((n // TEAM,)), dma((2,)),
        ],
        compiler_params=pltpu.CompilerParams(
            collective_id=0, has_side_effects=True, vmem_limit_bytes=32 * 1024 * 1024
        ),
        name="fused",
    )(*[pltpu.with_memory_space_constraint(x, pltpu.HBM) for x in operands])


def solution(mesh):
    in_specs = (
        P(None, ("runs", "brick")),
        P(None, ("runs", "brick")),
        P(("runs", "brick"), None),
        P(None, ("runs", "brick")),
        P(None, ("runs", "brick")),
        P(("runs", "brick")),
        P(),
        P(),
        P(),
    )
    out_specs = P(None, ("runs", "brick"))
    return jax.shard_map(shards, mesh=mesh, in_specs=in_specs, out_specs=out_specs, check_vma=False)
```

```python
import functools

import jax
import jax.numpy as jnp
from jax import lax
from jax.experimental import pallas as pl
from jax.experimental.pallas import tpu as pltpu
from jax.sharding import PartitionSpec as P

BS = 64
LANES = 128
HALF = LANES // 2
SUB = 8
STEPS = 4
TEAM = 4
BESIDE = 2
MESH = pl.DeviceIdType.MESH
NT = ((1,), (1,))
PLANE = BS * BS // LANES


def iota(shape, dim):
    return lax.broadcasted_iota(jnp.int32, shape, dim)


def pieces(x, count=3):
    out = []
    for _ in range(count):
        high = x.astype(jnp.bfloat16)
        out.append(high)
        x = x - high.astype(jnp.float32)
    return out


def mxu(a, b, contract=((1,), (0,))):
    return lax.dot_general(a, b, (contract, ((), ())), preferred_element_type=jnp.float32)


def wide(x):
    high, low = pieces(x, 2)
    return jnp.concatenate([high, high, low], axis=1)


def tall(x):
    high, low = pieces(x, 2)
    return jnp.concatenate([high, low, high], axis=0)


def hat(x):
    return jnp.maximum(1.0 - jnp.abs(x), 0.0)


def quotient(x, d):
    return lax.div(x, d)


def remainder(x, d):
    return lax.rem(x, d)


def device(chip, e, core, flip):
    return {"brick": 2 * (chip + sum(f for b, f in enumerate(flip) if e >> b & 1)) + core}


def fused(
    n, cap,
    owner_hbm, coords_hbm, fracs_hbm, cells_hbm, counts_hbm, dist_hbm, kernel_hbm, redist_hbm, shatter_hbm,
    out_ref,
    owner_ref, coords_ref, fracs_ref, counts_ref, dist_ref, mats_ref, cells,
    send, relay, recv, index_v, wa_ref, wb_ref, rsend, rrecv,
    relay_sem, recv_sem, rrecv_sem, local_sem,
):
    me = lax.axis_index("brick")
    rows = cells_hbm.shape[0]
    f32, bf16 = jnp.float32, jnp.bfloat16
    chips, chip, core = n // 2, quotient(me, 2), remainder(me, 2)
    layers, layer, side = n // 4, quotient(me, 4), remainder(quotient(me, 2), 2)
    flip = [(1 - 2 * remainder(quotient(chip, bit), 2)) * bit for bit in (1 << b for b in range(chips.bit_length() - 1))]
    lower = 1 - quotient(2 * layer, layers)
    gives = lower * remainder(layer + quotient(layer, 2) + 1, 2)
    passes = lower * (1 - gives) * core
    senders = [at for at in range(layers) if 2 * at >= layers or (at + at // 2) % 2]

    def spot(e, c):
        return 4 * (e // 2) + 2 * c + e % 2

    def arrival(source, c):
        first = 1 - jnp.minimum(source, 1)
        return first * c + (1 - first) * (1 + source)

    def load(source, target, i):
        return pltpu.make_async_copy(source, target, local_sem.at[i])

    first = [
        load(owner_hbm, owner_ref, 0),
        load(coords_hbm, coords_ref, 1),
        load(fracs_hbm, fracs_ref, 2),
    ]
    grid = [
        load(cells_hbm, cells.at[:, pl.ds(0, 3), :], 3),
        load(cells_hbm.at[pl.ds(PLANE, rows - PLANE)], cells.at[pl.ds(0, rows - PLANE), pl.ds(4, 3), :], 4),
    ]
    for copy in first:
        copy.start()
    barrier = pltpu.get_barrier_semaphore()

    def enter(device_id):
        pl.semaphore_signal(barrier, inc=1, device_id=device_id, device_id_type=MESH)

    @pl.when(passes == 1)
    def _():
        enter(device(chip, BESIDE, 0, flip))
        enter(device(chip, BESIDE, 1, flip))

    @pl.when(gives == 1)
    def _():
        enter(device(chip, 0, 1 - core, flip))
        enter(device(chip, 1, 0, flip))
        enter(device(chip, 1, 1, flip))

    for at in senders:
        for c in (1, 0):
            for d in (4 * at + c, 4 * at + 2 + c):
                pl.when(me != d)(functools.partial(enter, {"brick": d}))

    for copy in grid:
        copy.start()
    cells[rows - PLANE, 4:8, :] = jnp.zeros((4, LANES), f32)
    for copy in first:
        copy.wait()
    load(dist_hbm, dist_ref, 0).start()
    for i, matrix in enumerate((kernel_hbm, shatter_hbm, redist_hbm)):
        load(matrix, mats_ref.at[i], 1).start()
    load(counts_hbm, counts_ref, 2).start()

    tracers = owner_ref.shape[1]
    blocks = tracers // LANES
    owner = owner_ref[...]
    apart = (owner >> 1) ^ chip
    rel = 4 * (apart >> 1) + 2 * (owner & 1) + (apart & 1)
    onehot = jnp.where(iota((n, tracers), 0) == rel, 1.0, 0.0)
    upto = jnp.where(iota((LANES, LANES), 0) <= iota((LANES, LANES), 1), 1.0, 0.0).astype(bf16)
    stacked = jnp.concatenate([onehot[:, b * LANES : (b + 1) * LANES] for b in range(blocks)], axis=0)
    counted = mxu(stacked.astype(bf16), upto)
    running = jnp.zeros((n, 1), f32)
    ranks = []
    for b in range(blocks):
        part = counted[b * n : (b + 1) * n]
        ranks.append(jnp.sum(onehot[:, b * LANES : (b + 1) * LANES] * (part + running), axis=0, keepdims=True))
        running = running + part[:, LANES - 1 :]
    rank = jnp.concatenate(ranks, axis=1).astype(jnp.int32) - 1
    placed = jnp.where(iota((LANES, tracers), 0) == rank, 1.0, 0.0).astype(bf16)
    slot = jnp.clip(rank, 0, LANES - 1)

    blank = jnp.zeros((1, tracers), f32)
    coords = coords_ref[...].astype(f32)
    fracs = fracs_ref[...]
    high, middle, low = [p.astype(f32) for p in pieces(fracs)]
    main = jnp.concatenate([coords, blank, high, blank], axis=0)
    rest = jnp.concatenate([middle, blank, low, blank], axis=0)
    left = [jnp.where(rel == d, x, 0.0) for x in (main, rest) for d in range(n)]
    packed = mxu(jnp.concatenate(left, axis=0).astype(bf16), placed, NT)
    top = iota((SUB, LANES), 0) < 4
    for d in range(n):
        x = packed[SUB * d : SUB * (d + 1)]
        y = packed[SUB * (n + d) : SUB * (n + d + 1)]
        x = x + jnp.where(top, 0.0, y + pltpu.roll(y, 4, 0))
        send[d] = x

    pltpu.make_async_copy(send.at[2 * core], recv.at[2 * core], recv_sem.at[arrival(layer, core)]).start()

    def pass_on(source, target, e, c, i, sem):
        pltpu.make_async_remote_copy(
            src_ref=source, dst_ref=target, send_sem=local_sem.at[5 + i], recv_sem=sem,
            device_id=device(chip, e, c, flip), device_id_type=MESH,
        ).start()

    most = 3 * layers // 4
    spans = ((most, layers), (1, most))

    def give():
        for i, (a, b) in enumerate(spans):
            size = 4 * (b - a)
            pass_on(
                send.at[pl.ds(4 * a, size)], relay.at[pl.ds(n * core + 4 * a, size)], BESIDE, 1, 0,
                relay_sem.at[2 * core + i],
            )
        pass_on(
            send.at[spot(BESIDE, 1)], recv.at[spot(BESIDE, core)], BESIDE, 1, 1,
            recv_sem.at[arrival(layer, core)],
        )
        for e, c in ((1, 0), (1, 1), (0, 1 - core)):
            pass_on(send.at[spot(e, c)], recv.at[spot(e, core)], e, c, 1, recv_sem.at[arrival(layer, core)])

    def mine():
        for e in reversed(range(chips)):
            for c in (0, 1) if e else (1 - core,):
                pass_on(send.at[spot(e, c)], recv.at[spot(e, core)], e, c, 0, recv_sem.at[arrival(layer, core)])

    def theirs():
        client = layer + flip[1] // 2
        for i, (a, b) in enumerate(spans):
            for k in (0, 1):
                part = relay.at[pl.ds(n * k + 4 * a, 4 * (b - a))]
                pltpu.make_async_copy(part, part, relay_sem.at[2 * k + i]).wait()
                for e in reversed(range(2 * a, 2 * b)):
                    for c in (0, 1):
                        if (e, c) != (BESIDE, 1):
                            pass_on(
                                relay.at[n * k + spot(e, c)], recv.at[spot(e, k)], BESIDE ^ e, c, 1,
                                recv_sem.at[arrival(client, k)],
                            )

    @pl.when(gives == 1)
    def _():
        pl.semaphore_wait(barrier, 4)
        give()

    @pl.when(gives == 0)
    def _():
        pl.semaphore_wait(barrier, n - 1)
        pl.when(passes == 1)(theirs)
        mine()

    load(dist_hbm, dist_ref, 0).wait()
    pltpu.make_async_copy(mats_ref, mats_ref, local_sem.at[1]).wait()
    load(counts_hbm, counts_ref, 2).wait()
    steps = counts_ref[...]
    h = 1.0 / jnp.maximum(steps, 1).astype(f32)
    dist = dist_ref[...]
    bins = dist.shape[0]
    both = wide(jnp.concatenate([mats_ref[0], mats_ref[1]], axis=0))
    moved = wide(mats_ref[2])

    out = mxu(both, tall(dist))
    dot, broken = out[:bins], out[bins:]
    back = mxu(moved, tall(dist * dot))

    for copy in grid:
        copy.wait()

    row = iota((SUB, LANES), 0)
    lanes = iota((SUB, LANES), 1)
    lane = iota((cap, LANES), 1)
    within = (lane % HALF).astype(f32)
    half = (lane // HALF).astype(f32)

    def answer(source, which):
        team = len(which)
        apart = sum(
            remainder(quotient(layer, bit) + quotient(source, bit), 2) * bit
            for bit in (1 << b for b in range(layers.bit_length() - 1))
        )
        slots = [4 * apart + 2 * kind + across for across, kind in which]
        here = recv.at[pl.ds(slots[0], team)]
        pltpu.make_async_copy(here, here, recv_sem.at[arrival(source, which[0][1])]).wait()
        spots = []
        for slot_u in slots:
            x = recv[slot_u]
            whole = x.astype(jnp.int32)
            spread = jnp.where(row == 0, whole * PLANE, whole >> 1)
            index = (spread + pltpu.roll(spread, SUB - 1, 0)).astype(f32)
            base = jnp.where(row == 1, (whole & 1).astype(f32), x)
            spots.append(jnp.where(row == 0, index, base + pltpu.roll(x, 4, 0)))
        columns = jnp.concatenate(spots, axis=0).T
        whole = jnp.clip(columns[:cap].astype(jnp.int32), 0, rows - PLANE - 1)
        for u in range(team):
            index_v[u] = whole[:, SUB * u : SUB * (u + 1)]
        for u in range(team):
            y = columns[:cap, SUB * u + 1 : SUB * u + 2]
            z = columns[:cap, SUB * u + 2 : SUB * u + 3]
            w = hat(within - z)
            across = half - y
            wa_ref[u] = w * hat(across)
            wb_ref[u] = w * hat(across + 2.0)
        for u in range(team):
            acc = jnp.zeros((SUB, LANES), f32)
            for c in range(cap):
                r = index_v[u, c, 0]
                p = cells[r] * wa_ref[u, pl.ds(c, 1), :] + cells[r + 1] * wb_ref[u, pl.ds(c, 1), :]
                acc = jnp.where(lanes == c, jnp.sum(p, axis=1, keepdims=True), acc)
            rsend[slots[u]] = acc
        for u, (across, kind) in enumerate(which):
            at = side + across * (1 - 2 * side)
            remote = pltpu.make_async_remote_copy(
                src_ref=rsend.at[slots[u]], dst_ref=rrecv.at[4 * apart + 2 * core + across],
                send_sem=local_sem.at[0], recv_sem=rrecv_sem.at[quotient(apart, most)],
                device_id={"brick": 4 * source + 2 * at + kind}, device_id_type=MESH,
            )
            itself = 4 * source + 2 * at + kind == me
            pl.when(jnp.logical_not(itself))(remote.start)

            @pl.when(itself)
            def _():
                pltpu.make_async_copy(rsend.at[2 * core], rrecv.at[2 * core], rrecv_sem.at[0]).start()

    def two(kind, carry):
        answer(0, [(0, kind), (1, kind)])
        return carry

    def four(source, carry):
        answer(source, [(0, 0), (1, 0), (0, 1), (1, 1)])
        return carry

    lax.fori_loop(0, 2, two, 0)
    lax.fori_loop(1, layers, four, 0)

    near, far = rrecv.at[pl.ds(0, 4 * most)], rrecv.at[pl.ds(4 * most, n - 4 * most)]
    pltpu.make_async_copy(near, near, rrecv_sem.at[0]).wait()
    answers = jnp.concatenate(pieces(near[...].reshape(4 * most * SUB, LANES), 2), axis=1)
    found = mxu(answers, jnp.concatenate([placed, placed], axis=0))
    both_ends = jnp.zeros((SUB, tracers), f32)
    for i in range(4 * most):
        both_ends = jnp.where(rel == i, found[SUB * i : SUB * (i + 1)], both_ends)
    pltpu.make_async_copy(far, far, rrecv_sem.at[1]).wait()
    parts = []
    for b in range(blocks):
        block = slice(b * LANES, (b + 1) * LANES)
        part, place = both_ends[:, block], jnp.broadcast_to(slot[:, block], (SUB, LANES))
        for i in range(4 * most, n):
            one = jnp.take_along_axis(rrecv[i], place, axis=1, mode="promise_in_bounds")
            part = jnp.where(rel[:, block] == i, one, part)
        parts.append(part)
    both_ends = jnp.concatenate(parts, axis=1)
    f0 = fracs[0:1]
    sampled = [both_ends[f : f + 1] * (1.0 - f0) + both_ends[4 + f : 5 + f] * f0 for f in range(3)]
    coag = h * sampled[0] * jnp.sqrt(sampled[1])
    shat = h * sampled[2] * sampled[1]
    for section in range(STEPS):
        if section:
            out = mxu(both, tall(dist))
            dot, broken = out[:bins], out[bins:]
            back = mxu(moved, tall(dist * dot))
        active = steps >= section + 1
        c, s = jnp.where(active, coag, 0.0), jnp.where(active, shat, 0.0)
        dist = ((dist + s * broken) + c * back) * (1.0 / ((1.0 + s) + c * dot))
    out_ref[...] = dist
    some = rsend.at[pl.ds(1, n - 1)]
    pltpu.make_async_copy(some, some, local_sem.at[0]).wait()

    @pl.when(gives == 1)
    def _():
        handed, own = send.at[pl.ds(4, n - 4)], send.at[pl.ds(0, 4)]
        pltpu.make_async_copy(handed, handed, local_sem.at[5]).wait()
        pltpu.make_async_copy(own, own, local_sem.at[6]).wait()

    @pl.when(gives == 0)
    def _():
        own = send.at[pl.ds(1, n - 1)]
        pltpu.make_async_copy(own, own, local_sem.at[5]).wait()

    @pl.when(passes == 1)
    def _():
        others = relay.at[pl.ds(0, 2 * (n - 5))]
        pltpu.make_async_copy(others, others, local_sem.at[6]).wait()


def shards(grid, distribution, owner_ids, coords, fracs, counts, kernel, redist, shatter):
    n = lax.axis_size("brick")
    bins, tracers = distribution.shape
    cap = 2 * tracers // n
    assert cap <= HALF and n >= 16 and n & (n - 1) == 0 and tracers % LANES == 0
    f32, i32 = jnp.float32, jnp.int32
    cells = jnp.swapaxes(grid.reshape(grid.shape[0], -1, LANES), 0, 1)
    operands = (
        owner_ids.reshape(1, tracers), coords, fracs, cells, counts.reshape(1, tracers),
        distribution, kernel, redist, shatter,
    )
    dma = pltpu.SemaphoreType.DMA
    return pl.pallas_call(
        lambda *refs: pl.run_scoped(functools.partial(fused, n, cap, *refs), dma((7,))),
        out_shape=jax.ShapeDtypeStruct((bins, tracers), f32),
        in_specs=[pl.BlockSpec(memory_space=pltpu.HBM)] * len(operands),
        out_specs=pl.BlockSpec(memory_space=pltpu.VMEM),
        scratch_shapes=[
            pltpu.VMEM((1, tracers), i32),
            pltpu.VMEM(coords.shape, i32),
            pltpu.VMEM(fracs.shape, f32),
            pltpu.VMEM((1, tracers), i32),
            pltpu.VMEM(distribution.shape, f32),
            pltpu.VMEM((3, *kernel.shape), f32),
            pltpu.VMEM((cells.shape[0], SUB, LANES), f32),
            pltpu.VMEM((n, SUB, LANES), f32),
            pltpu.VMEM((2 * n, SUB, LANES), f32),
            pltpu.VMEM((n, SUB, LANES), f32),
            pltpu.VMEM((TEAM, cap, SUB), i32),
            pltpu.VMEM((TEAM, cap, LANES), f32),
            pltpu.VMEM((TEAM, cap, LANES), f32),
            pltpu.VMEM((n, SUB, LANES), f32),
            pltpu.VMEM((n, SUB, LANES), f32),
            dma((4,)), dma((n // 4 + 1,)), dma((2,)),
        ],
        compiler_params=pltpu.CompilerParams(
            collective_id=0, has_side_effects=True, vmem_limit_bytes=32 * 1024 * 1024
        ),
        name="fused",
    )(*[pltpu.with_memory_space_constraint(x, pltpu.HBM) for x in operands])


def solution(mesh):
    in_specs = (
        P(None, ("runs", "brick")),
        P(None, ("runs", "brick")),
        P(("runs", "brick"), None),
        P(None, ("runs", "brick")),
        P(None, ("runs", "brick")),
        P(("runs", "brick")),
        P(),
        P(),
        P(),
    )
    out_specs = P(None, ("runs", "brick"))
    return jax.shard_map(shards, mesh=mesh, in_specs=in_specs, out_specs=out_specs, check_vma=False)
```

```python
import functools

import jax
import jax.numpy as jnp
from jax import lax
from jax.experimental import pallas as pl
from jax.experimental.pallas import tpu as pltpu
from jax.sharding import PartitionSpec as P

BS = 64
LANES = 128
HALF = LANES // 2
SUB = 8
STEPS = 4
TEAM = 2
BESIDE = 2
MESH = pl.DeviceIdType.MESH
NT = ((1,), (1,))
PLANE = BS * BS // LANES


def iota(shape, dim):
    return lax.broadcasted_iota(jnp.int32, shape, dim)


def pieces(x, count=3):
    out = []
    for _ in range(count):
        high = x.astype(jnp.bfloat16)
        out.append(high)
        x = x - high.astype(jnp.float32)
    return out


def mxu(a, b, contract=((1,), (0,))):
    return lax.dot_general(a, b, (contract, ((), ())), preferred_element_type=jnp.float32)


def wide(x):
    high, low = pieces(x, 2)
    return jnp.concatenate([high, high, low], axis=1)


def tall(x):
    high, low = pieces(x, 2)
    return jnp.concatenate([high, low, high], axis=0)


def hat(x):
    return jnp.maximum(1.0 - jnp.abs(x), 0.0)


def quotient(x, d):
    return lax.div(x, d)


def remainder(x, d):
    return lax.rem(x, d)


def device(chip, e, core, flip):
    return {"brick": 2 * (chip + sum(f for b, f in enumerate(flip) if e >> b & 1)) + core}


def fused(
    n, cap,
    owner_hbm, coords_hbm, fracs_hbm, cells_hbm, counts_hbm, dist_hbm, kernel_hbm, redist_hbm, shatter_hbm,
    out_ref,
    owner_ref, coords_ref, fracs_ref, counts_ref, dist_ref, mats_ref, cells,
    send, relay, recv, index_v, wa_ref, wb_ref, rsend, rrecv,
    relay_sem, recv_sem, rrecv_sem, local_sem,
):
    me = lax.axis_index("brick")
    barrier = pltpu.get_barrier_semaphore()

    def enter(device_id):
        pl.semaphore_signal(barrier, inc=1, device_id=device_id, device_id_type=MESH)

    senders = [at for at in range(n // 4) if 8 * at >= n or (at + at // 2) % 2]
    relays = [4 * at + d for at in senders if 8 * at < n for d in (1, 3)]
    others = [4 * at + d for at in senders for d in (1, 3, 0, 2) if 4 * at + d not in relays]
    for d in relays:
        pl.when(me != d)(functools.partial(enter, {"brick": d}))

    rows = cells_hbm.shape[0]
    f32, bf16 = jnp.float32, jnp.bfloat16
    chips, chip, core = n // 2, quotient(me, 2), remainder(me, 2)
    layers, layer, side = n // 4, quotient(me, 4), remainder(quotient(me, 2), 2)
    flip = [(1 - 2 * remainder(quotient(chip, bit), 2)) * bit for bit in (1 << b for b in range(chips.bit_length() - 1))]
    lower = 1 - quotient(2 * layer, layers)
    gives = lower * remainder(layer + quotient(layer, 2) + 1, 2)
    passes = lower * (1 - gives) * core

    def spot(e, c):
        return 4 * (e // 2) + 2 * c + e % 2

    def load(source, target, i):
        return pltpu.make_async_copy(source, target, local_sem.at[i])

    first = [
        load(owner_hbm, owner_ref, 0),
        load(coords_hbm, coords_ref, 1),
        load(fracs_hbm, fracs_ref, 2),
    ]
    grid = [
        load(cells_hbm, cells.at[:, pl.ds(0, 3), :], 3),
        load(cells_hbm.at[pl.ds(PLANE, rows - PLANE)], cells.at[pl.ds(0, rows - PLANE), pl.ds(4, 3), :], 4),
    ]
    for copy in first:
        copy.start()
    @pl.when(passes == 1)
    def _():
        enter(device(chip, BESIDE, 0, flip))
        enter(device(chip, BESIDE, 1, flip))

    @pl.when(gives == 1)
    def _():
        enter(device(chip, 0, 1 - core, flip))
        enter(device(chip, 1, 0, flip))
        enter(device(chip, 1, 1, flip))

    for d in others:
        pl.when(me != d)(functools.partial(enter, {"brick": d}))

    for copy in grid:
        copy.start()
    cells[rows - PLANE, 4:8, :] = jnp.zeros((4, LANES), f32)
    for copy in first:
        copy.wait()
    load(dist_hbm, dist_ref, 0).start()
    for i, matrix in enumerate((kernel_hbm, shatter_hbm, redist_hbm)):
        load(matrix, mats_ref.at[i], 1).start()
    load(counts_hbm, counts_ref, 2).start()

    tracers = owner_ref.shape[1]
    blocks = tracers // LANES
    owner = owner_ref[...]
    apart = (owner >> 1) ^ chip
    rel = 4 * (apart >> 1) + 2 * (owner & 1) + (apart & 1)
    onehot = jnp.where(iota((n, tracers), 0) == rel, 1.0, 0.0)
    upto = jnp.where(iota((LANES, LANES), 0) <= iota((LANES, LANES), 1), 1.0, 0.0).astype(bf16)
    stacked = jnp.concatenate([onehot[:, b * LANES : (b + 1) * LANES] for b in range(blocks)], axis=0)
    counted = mxu(stacked.astype(bf16), upto)
    running = jnp.zeros((n, 1), f32)
    ranks = []
    for b in range(blocks):
        part = counted[b * n : (b + 1) * n]
        ranks.append(jnp.sum(onehot[:, b * LANES : (b + 1) * LANES] * (part + running), axis=0, keepdims=True))
        running = running + part[:, LANES - 1 :]
    rank = jnp.concatenate(ranks, axis=1).astype(jnp.int32) - 1
    placed = jnp.where(iota((LANES, tracers), 0) == rank, 1.0, 0.0).astype(bf16)
    slot = jnp.clip(rank, 0, LANES - 1)

    blank = jnp.zeros((1, tracers), f32)
    coords = coords_ref[...].astype(f32)
    fracs = fracs_ref[...]
    high, middle, low = [p.astype(f32) for p in pieces(fracs)]
    main = jnp.concatenate([coords, blank, high, blank], axis=0)
    rest = jnp.concatenate([middle, blank, low, blank], axis=0)
    left = [jnp.where(rel == d, x, 0.0) for x in (main, rest) for d in range(n)]
    packed = mxu(jnp.concatenate(left, axis=0).astype(bf16), placed, NT)
    top = iota((SUB, LANES), 0) < 4
    for d in range(n):
        x = packed[SUB * d : SUB * (d + 1)]
        y = packed[SUB * (n + d) : SUB * (n + d + 1)]
        x = x + jnp.where(top, 0.0, y + pltpu.roll(y, 4, 0))
        send[d] = x

    pltpu.make_async_copy(send.at[2 * core], recv.at[2 * core], recv_sem.at[core]).start()

    def pass_on(source, target, e, c, i, sem):
        pltpu.make_async_remote_copy(
            src_ref=source, dst_ref=target, send_sem=local_sem.at[5 + i], recv_sem=sem,
            device_id=device(chip, e, c, flip), device_id_type=MESH,
        ).start()

    most = 3 * layers // 4
    spans = ((most, layers), (1, most))

    def give():
        for i, (a, b) in enumerate(spans):
            size = 4 * (b - a)
            pass_on(
                send.at[pl.ds(4 * a, size)], relay.at[pl.ds(n * core + 4 * a, size)], BESIDE, 1, 0,
                relay_sem.at[2 * core + i],
            )
        pass_on(
            send.at[spot(BESIDE, 1)], recv.at[spot(BESIDE, core)], BESIDE, 1, 1, recv_sem.at[2 * (BESIDE // 2) + core]
        )
        for e, c in ((1, 0), (1, 1), (0, 1 - core)):
            pass_on(send.at[spot(e, c)], recv.at[spot(e, core)], e, c, 1, recv_sem.at[core])

    def mine():
        for e in reversed(range(chips)):
            for c in (0, 1) if e else (1 - core,):
                pass_on(send.at[spot(e, c)], recv.at[spot(e, core)], e, c, 0, recv_sem.at[2 * (e // 2) + core])

    def theirs():
        for i, (a, b) in enumerate(spans):
            for k in (0, 1):
                part = relay.at[pl.ds(n * k + 4 * a, 4 * (b - a))]
                pltpu.make_async_copy(part, part, relay_sem.at[2 * k + i]).wait()
                for e in reversed(range(2 * a, 2 * b)):
                    for c in (0, 1):
                        if (e, c) != (BESIDE, 1):
                            pass_on(
                                relay.at[n * k + spot(e, c)], recv.at[spot(e, k)], BESIDE ^ e, c, 1,
                                recv_sem.at[2 * (e // 2) + k],
                            )

    @pl.when(gives == 1)
    def _():
        pl.semaphore_wait(barrier, 4)
        give()

    @pl.when(gives == 0)
    def _():
        pl.semaphore_wait(barrier, n - 1)
        pl.when(passes == 1)(theirs)
        mine()

    load(dist_hbm, dist_ref, 0).wait()
    pltpu.make_async_copy(mats_ref, mats_ref, local_sem.at[1]).wait()
    load(counts_hbm, counts_ref, 2).wait()
    steps = counts_ref[...]
    h = 1.0 / jnp.maximum(steps, 1).astype(f32)
    dist = dist_ref[...]
    bins = dist.shape[0]
    both = wide(jnp.concatenate([mats_ref[0], mats_ref[1]], axis=0))
    moved = wide(mats_ref[2])

    out = mxu(both, tall(dist))
    dot, broken = out[:bins], out[bins:]
    back = mxu(moved, tall(dist * dot))

    for copy in grid:
        copy.wait()

    row = iota((SUB, LANES), 0)
    lanes = iota((SUB, LANES), 1)
    lane = iota((cap, LANES), 1)
    within = (lane % HALF).astype(f32)
    half = (lane // HALF).astype(f32)

    def answer(turn, carry):
        source, kind = quotient(turn, 2), remainder(turn, 2)
        apart = sum(
            remainder(quotient(layer, bit) + quotient(source, bit), 2) * bit
            for bit in (1 << b for b in range(layers.bit_length() - 1))
        )
        team = 2 * apart + kind
        start = team * TEAM
        here = recv.at[pl.ds(start, TEAM)]
        pltpu.make_async_copy(here, here, recv_sem.at[team]).wait()
        spots = []
        for u in range(TEAM):
            x = recv[start + u]
            whole = x.astype(jnp.int32)
            spread = jnp.where(row == 0, whole * PLANE, whole >> 1)
            index = (spread + pltpu.roll(spread, SUB - 1, 0)).astype(f32)
            base = jnp.where(row == 1, (whole & 1).astype(f32), x)
            spots.append(jnp.where(row == 0, index, base + pltpu.roll(x, 4, 0)))
        columns = jnp.concatenate(spots, axis=0).T
        whole = jnp.clip(columns[:cap].astype(jnp.int32), 0, rows - PLANE - 1)
        for u in range(TEAM):
            index_v[u] = whole[:, SUB * u : SUB * (u + 1)]
        for u in range(TEAM):
            y = columns[:cap, SUB * u + 1 : SUB * u + 2]
            z = columns[:cap, SUB * u + 2 : SUB * u + 3]
            w = hat(within - z)
            across = half - y
            wa_ref[u] = w * hat(across)
            wb_ref[u] = w * hat(across + 2.0)
        for u in range(TEAM):
            acc = jnp.zeros((SUB, LANES), f32)
            for c in range(cap):
                r = index_v[u, c, 0]
                p = cells[r] * wa_ref[u, pl.ds(c, 1), :] + cells[r + 1] * wb_ref[u, pl.ds(c, 1), :]
                acc = jnp.where(lanes == c, jnp.sum(p, axis=1, keepdims=True), acc)
            rsend[start + u] = acc
        for u in reversed(range(TEAM)):
            at = side if u == 0 else 1 - side
            remote = pltpu.make_async_remote_copy(
                src_ref=rsend.at[start + u], dst_ref=rrecv.at[4 * apart + 2 * core + u],
                send_sem=local_sem.at[0], recv_sem=rrecv_sem.at[quotient(apart, most)],
                device_id={"brick": 4 * source + 2 * at + kind}, device_id_type=MESH,
            )
            if u:
                remote.start()
            else:
                pl.when(team != core)(remote.start)

                @pl.when(team == core)
                def _():
                    pltpu.make_async_copy(rsend.at[2 * core], rrecv.at[2 * core], rrecv_sem.at[0]).start()
        return carry

    lax.fori_loop(0, n // TEAM, answer, 0)

    near, far = rrecv.at[pl.ds(0, 4 * most)], rrecv.at[pl.ds(4 * most, n - 4 * most)]
    pltpu.make_async_copy(near, near, rrecv_sem.at[0]).wait()
    answers = jnp.concatenate(pieces(near[...].reshape(4 * most * SUB, LANES), 2), axis=1)
    found = mxu(answers, jnp.concatenate([placed, placed], axis=0))
    both_ends = jnp.zeros((SUB, tracers), f32)
    for i in range(4 * most):
        both_ends = jnp.where(rel == i, found[SUB * i : SUB * (i + 1)], both_ends)
    pltpu.make_async_copy(far, far, rrecv_sem.at[1]).wait()
    parts = []
    for b in range(blocks):
        block = slice(b * LANES, (b + 1) * LANES)
        part, place = both_ends[:, block], jnp.broadcast_to(slot[:, block], (SUB, LANES))
        for i in range(4 * most, n):
            one = jnp.take_along_axis(rrecv[i], place, axis=1, mode="promise_in_bounds")
            part = jnp.where(rel[:, block] == i, one, part)
        parts.append(part)
    both_ends = jnp.concatenate(parts, axis=1)
    f0 = fracs[0:1]
    sampled = [both_ends[f : f + 1] * (1.0 - f0) + both_ends[4 + f : 5 + f] * f0 for f in range(3)]
    coag = h * sampled[0] * jnp.sqrt(sampled[1])
    shat = h * sampled[2] * sampled[1]
    for section in range(STEPS):
        if section:
            out = mxu(both, tall(dist))
            dot, broken = out[:bins], out[bins:]
            back = mxu(moved, tall(dist * dot))
        active = steps >= section + 1
        c, s = jnp.where(active, coag, 0.0), jnp.where(active, shat, 0.0)
        dist = ((dist + s * broken) + c * back) * (1.0 / ((1.0 + s) + c * dot))
    out_ref[...] = dist
    some = rsend.at[pl.ds(1, n - 1)]
    pltpu.make_async_copy(some, some, local_sem.at[0]).wait()

    @pl.when(gives == 1)
    def _():
        handed, own = send.at[pl.ds(4, n - 4)], send.at[pl.ds(0, 4)]
        pltpu.make_async_copy(handed, handed, local_sem.at[5]).wait()
        pltpu.make_async_copy(own, own, local_sem.at[6]).wait()

    @pl.when(gives == 0)
    def _():
        own = send.at[pl.ds(1, n - 1)]
        pltpu.make_async_copy(own, own, local_sem.at[5]).wait()

    @pl.when(passes == 1)
    def _():
        others = relay.at[pl.ds(0, 2 * (n - 5))]
        pltpu.make_async_copy(others, others, local_sem.at[6]).wait()


def shards(grid, distribution, owner_ids, coords, fracs, counts, kernel, redist, shatter):
    n = lax.axis_size("brick")
    bins, tracers = distribution.shape
    cap = 2 * tracers // n
    assert cap <= HALF and n >= 16 and n & (n - 1) == 0 and tracers % LANES == 0
    f32, i32 = jnp.float32, jnp.int32
    cells = jnp.swapaxes(grid.reshape(grid.shape[0], -1, LANES), 0, 1)
    operands = (
        owner_ids.reshape(1, tracers), coords, fracs, cells, counts.reshape(1, tracers),
        distribution, kernel, redist, shatter,
    )
    dma = pltpu.SemaphoreType.DMA
    return pl.pallas_call(
        lambda *refs: pl.run_scoped(functools.partial(fused, n, cap, *refs), dma((7,))),
        out_shape=jax.ShapeDtypeStruct((bins, tracers), f32),
        in_specs=[pl.BlockSpec(memory_space=pltpu.HBM)] * len(operands),
        out_specs=pl.BlockSpec(memory_space=pltpu.VMEM),
        scratch_shapes=[
            pltpu.VMEM((1, tracers), i32),
            pltpu.VMEM(coords.shape, i32),
            pltpu.VMEM(fracs.shape, f32),
            pltpu.VMEM((1, tracers), i32),
            pltpu.VMEM(distribution.shape, f32),
            pltpu.VMEM((3, *kernel.shape), f32),
            pltpu.VMEM((cells.shape[0], SUB, LANES), f32),
            pltpu.VMEM((n, SUB, LANES), f32),
            pltpu.VMEM((2 * n, SUB, LANES), f32),
            pltpu.VMEM((n, SUB, LANES), f32),
            pltpu.VMEM((TEAM, cap, SUB), i32),
            pltpu.VMEM((TEAM, cap, LANES), f32),
            pltpu.VMEM((TEAM, cap, LANES), f32),
            pltpu.VMEM((n, SUB, LANES), f32),
            pltpu.VMEM((n, SUB, LANES), f32),
            dma((4,)), dma((n // TEAM,)), dma((2,)),
        ],
        compiler_params=pltpu.CompilerParams(
            collective_id=0, has_side_effects=True, vmem_limit_bytes=32 * 1024 * 1024
        ),
        name="fused",
    )(*[pltpu.with_memory_space_constraint(x, pltpu.HBM) for x in operands])


def solution(mesh):
    in_specs = (
        P(None, ("runs", "brick")),
        P(None, ("runs", "brick")),
        P(("runs", "brick"), None),
        P(None, ("runs", "brick")),
        P(None, ("runs", "brick")),
        P(("runs", "brick")),
        P(),
        P(),
        P(),
    )
    out_specs = P(None, ("runs", "brick"))
    return jax.shard_map(shards, mesh=mesh, in_specs=in_specs, out_specs=out_specs, check_vma=False)
```

```python
import functools

import jax
import jax.numpy as jnp
from jax import lax
from jax.experimental import pallas as pl
from jax.experimental.pallas import tpu as pltpu
from jax.sharding import PartitionSpec as P

BS = 64
LANES = 128
HALF = LANES // 2
SUB = 8
STEPS = 4
TEAM = 4
BESIDE = 2
MESH = pl.DeviceIdType.MESH
NT = ((1,), (1,))
PLANE = BS * BS // LANES


def iota(shape, dim):
    return lax.broadcasted_iota(jnp.int32, shape, dim)


def pieces(x, count=3):
    out = []
    for _ in range(count):
        high = x.astype(jnp.bfloat16)
        out.append(high)
        x = x - high.astype(jnp.float32)
    return out


def mxu(a, b, contract=((1,), (0,))):
    return lax.dot_general(a, b, (contract, ((), ())), preferred_element_type=jnp.float32)


def wide(x):
    high, low = pieces(x, 2)
    return jnp.concatenate([high, high, low], axis=1)


def tall(x):
    high, low = pieces(x, 2)
    return jnp.concatenate([high, low, high], axis=0)


def hat(x):
    return jnp.maximum(1.0 - jnp.abs(x), 0.0)


def quotient(x, d):
    return lax.div(x, d)


def remainder(x, d):
    return lax.rem(x, d)


def device(chip, e, core, flip):
    return {"brick": 2 * (chip + sum(f for b, f in enumerate(flip) if e >> b & 1)) + core}


def fused(
    n, cap,
    owner_hbm, coords_hbm, fracs_hbm, cells_hbm, counts_hbm, dist_hbm, kernel_hbm, redist_hbm, shatter_hbm,
    out_ref,
    owner_ref, coords_ref, fracs_ref, counts_ref, dist_ref, mats_ref, cells,
    send, relay, recv, index_v, wa_ref, wb_ref, rsend, rrecv,
    relay_sem, recv_sem, rrecv_sem, local_sem,
):
    me = lax.axis_index("brick")
    rows = cells_hbm.shape[0]
    f32, bf16 = jnp.float32, jnp.bfloat16
    chips, chip, core = n // 2, quotient(me, 2), remainder(me, 2)
    layers, layer, side = n // 4, quotient(me, 4), remainder(quotient(me, 2), 2)
    flip = [(1 - 2 * remainder(quotient(chip, bit), 2)) * bit for bit in (1 << b for b in range(chips.bit_length() - 1))]
    lower = 1 - quotient(2 * layer, layers)
    gives = lower * remainder(layer + quotient(layer, 2) + 1, 2)
    passes = lower * (1 - gives) * core
    senders = [at for at in range(layers) if 2 * at >= layers or (at + at // 2) % 2]

    def spot(e, c):
        return 4 * (e // 2) + 2 * c + e % 2

    def arrival(source, c):
        first = 1 - jnp.minimum(source, 1)
        return first * c + (1 - first) * (1 + source)

    def load(source, target, i):
        return pltpu.make_async_copy(source, target, local_sem.at[i])

    first = [
        load(owner_hbm, owner_ref, 0),
        load(coords_hbm, coords_ref, 1),
        load(fracs_hbm, fracs_ref, 2),
    ]
    grid = [
        load(cells_hbm, cells.at[:, pl.ds(0, 3), :], 3),
        load(cells_hbm.at[pl.ds(PLANE, rows - PLANE)], cells.at[pl.ds(0, rows - PLANE), pl.ds(4, 3), :], 4),
    ]
    for copy in first:
        copy.start()
    barrier = pltpu.get_barrier_semaphore()

    def enter(device_id):
        pl.semaphore_signal(barrier, inc=1, device_id=device_id, device_id_type=MESH)

    @pl.when(passes == 1)
    def _():
        enter(device(chip, BESIDE, 0, flip))
        enter(device(chip, BESIDE, 1, flip))

    @pl.when(gives == 1)
    def _():
        enter(device(chip, 0, 1 - core, flip))
        enter(device(chip, 1, 0, flip))
        enter(device(chip, 1, 1, flip))

    for at in senders:
        for c in (1, 0):
            for d in (4 * at + c, 4 * at + 2 + c):
                pl.when(me != d)(functools.partial(enter, {"brick": d}))

    for copy in grid:
        copy.start()
    cells[rows - PLANE, 4:8, :] = jnp.zeros((4, LANES), f32)
    for copy in first:
        copy.wait()
    load(dist_hbm, dist_ref, 0).start()
    for i, matrix in enumerate((kernel_hbm, shatter_hbm, redist_hbm)):
        load(matrix, mats_ref.at[i], 1).start()
    load(counts_hbm, counts_ref, 2).start()

    tracers = owner_ref.shape[1]
    blocks = tracers // LANES
    owner = owner_ref[...]
    apart = (owner >> 1) ^ chip
    rel = 4 * (apart >> 1) + 2 * (owner & 1) + (apart & 1)
    onehot = jnp.where(iota((n, tracers), 0) == rel, 1.0, 0.0)
    upto = jnp.where(iota((LANES, LANES), 0) <= iota((LANES, LANES), 1), 1.0, 0.0).astype(bf16)
    stacked = jnp.concatenate([onehot[:, b * LANES : (b + 1) * LANES] for b in range(blocks)], axis=0)
    counted = mxu(stacked.astype(bf16), upto)
    running = jnp.zeros((n, 1), f32)
    ranks = []
    for b in range(blocks):
        part = counted[b * n : (b + 1) * n]
        ranks.append(jnp.sum(onehot[:, b * LANES : (b + 1) * LANES] * (part + running), axis=0, keepdims=True))
        running = running + part[:, LANES - 1 :]
    rank = jnp.concatenate(ranks, axis=1).astype(jnp.int32) - 1
    placed = jnp.where(iota((LANES, tracers), 0) == rank, 1.0, 0.0).astype(bf16)
    slot = jnp.clip(rank, 0, LANES - 1)

    blank = jnp.zeros((1, tracers), f32)
    coords = coords_ref[...].astype(f32)
    fracs = fracs_ref[...]
    high, middle, low = [p.astype(f32) for p in pieces(fracs)]
    main = jnp.concatenate([coords, blank, high, blank], axis=0)
    rest = jnp.concatenate([middle, blank, low, blank], axis=0)
    left = [jnp.where(rel == d, x, 0.0) for x in (main, rest) for d in range(n)]
    packed = mxu(jnp.concatenate(left, axis=0).astype(bf16), placed, NT)
    top = iota((SUB, LANES), 0) < 4
    for d in range(n):
        x = packed[SUB * d : SUB * (d + 1)]
        y = packed[SUB * (n + d) : SUB * (n + d + 1)]
        x = x + jnp.where(top, 0.0, y + pltpu.roll(y, 4, 0))
        send[d] = x

    pltpu.make_async_copy(send.at[2 * core], recv.at[2 * core], recv_sem.at[arrival(layer, core)]).start()

    def pass_on(source, target, e, c, i, sem):
        pltpu.make_async_remote_copy(
            src_ref=source, dst_ref=target, send_sem=local_sem.at[5 + i], recv_sem=sem,
            device_id=device(chip, e, c, flip), device_id_type=MESH,
        ).start()

    most = 3 * layers // 4
    spans = ((most, layers), (1, most))

    def give():
        for i, (a, b) in enumerate(spans):
            size = 4 * (b - a)
            pass_on(
                send.at[pl.ds(4 * a, size)], relay.at[pl.ds(n * core + 4 * a, size)], BESIDE, 1, 0,
                relay_sem.at[2 * core + i],
            )
        pass_on(
            send.at[spot(BESIDE, 1)], recv.at[spot(BESIDE, core)], BESIDE, 1, 1,
            recv_sem.at[arrival(layer, core)],
        )
        for e, c in ((1, 0), (1, 1), (0, 1 - core)):
            pass_on(send.at[spot(e, c)], recv.at[spot(e, core)], e, c, 1, recv_sem.at[arrival(layer, core)])

    def mine():
        for e in reversed(range(chips)):
            for c in (0, 1) if e else (1 - core,):
                pass_on(send.at[spot(e, c)], recv.at[spot(e, core)], e, c, 0, recv_sem.at[arrival(layer, core)])

    def theirs():
        client = layer + flip[1] // 2
        for i, (a, b) in enumerate(spans):
            for k in (0, 1):
                part = relay.at[pl.ds(n * k + 4 * a, 4 * (b - a))]
                pltpu.make_async_copy(part, part, relay_sem.at[2 * k + i]).wait()
                for e in reversed(range(2 * a, 2 * b)):
                    for c in (0, 1):
                        if (e, c) != (BESIDE, 1):
                            pass_on(
                                relay.at[n * k + spot(e, c)], recv.at[spot(e, k)], BESIDE ^ e, c, 1,
                                recv_sem.at[arrival(client, k)],
                            )

    @pl.when(gives == 1)
    def _():
        pl.semaphore_wait(barrier, 4)
        give()

    @pl.when(gives == 0)
    def _():
        pl.semaphore_wait(barrier, n - 1)
        pl.when(passes == 1)(theirs)
        mine()

    load(dist_hbm, dist_ref, 0).wait()
    pltpu.make_async_copy(mats_ref, mats_ref, local_sem.at[1]).wait()
    load(counts_hbm, counts_ref, 2).wait()
    steps = counts_ref[...]
    h = 1.0 / jnp.maximum(steps, 1).astype(f32)
    dist = dist_ref[...]
    bins = dist.shape[0]
    both = wide(jnp.concatenate([mats_ref[0], mats_ref[1]], axis=0))
    moved = wide(mats_ref[2])

    out = mxu(both, tall(dist))
    dot, broken = out[:bins], out[bins:]
    back = mxu(moved, tall(dist * dot))

    for copy in grid:
        copy.wait()

    row = iota((SUB, LANES), 0)
    lanes = iota((SUB, LANES), 1)
    lane = iota((cap, LANES), 1)
    within = (lane % HALF).astype(f32)
    half = (lane // HALF).astype(f32)

    def answer(source, which):
        team = len(which)
        apart = sum(
            remainder(quotient(layer, bit) + quotient(source, bit), 2) * bit
            for bit in (1 << b for b in range(layers.bit_length() - 1))
        )
        slots = [4 * apart + 2 * kind + across for across, kind in which]
        here = recv.at[pl.ds(slots[0], team)]
        pltpu.make_async_copy(here, here, recv_sem.at[arrival(source, which[0][1])]).wait()
        spots = []
        for slot_u in slots:
            x = recv[slot_u]
            whole = x.astype(jnp.int32)
            spread = jnp.where(row == 0, whole * PLANE, whole >> 1)
            index = (spread + pltpu.roll(spread, SUB - 1, 0)).astype(f32)
            base = jnp.where(row == 1, (whole & 1).astype(f32), x)
            spots.append(jnp.where(row == 0, index, base + pltpu.roll(x, 4, 0)))
        columns = jnp.concatenate(spots, axis=0).T
        whole = jnp.clip(columns[:cap].astype(jnp.int32), 0, rows - PLANE - 1)
        for u in range(team):
            index_v[u] = whole[:, SUB * u : SUB * (u + 1)]
        for u in range(team):
            y = columns[:cap, SUB * u + 1 : SUB * u + 2]
            z = columns[:cap, SUB * u + 2 : SUB * u + 3]
            w = hat(within - z)
            across = half - y
            wa_ref[u] = w * hat(across)
            wb_ref[u] = w * hat(across + 2.0)
        for u in range(team):
            acc = jnp.zeros((SUB, LANES), f32)
            for c in range(cap):
                r = index_v[u, c, 0]
                p = cells[r] * wa_ref[u, pl.ds(c, 1), :] + cells[r + 1] * wb_ref[u, pl.ds(c, 1), :]
                acc = jnp.where(lanes == c, jnp.sum(p, axis=1, keepdims=True), acc)
            rsend[slots[u]] = acc
        for u, (across, kind) in reversed(list(enumerate(which))):
            at = side + across * (1 - 2 * side)
            remote = pltpu.make_async_remote_copy(
                src_ref=rsend.at[slots[u]], dst_ref=rrecv.at[4 * apart + 2 * core + across],
                send_sem=local_sem.at[0], recv_sem=rrecv_sem.at[quotient(apart, most)],
                device_id={"brick": 4 * source + 2 * at + kind}, device_id_type=MESH,
            )
            itself = 4 * source + 2 * at + kind == me
            pl.when(jnp.logical_not(itself))(remote.start)

            @pl.when(itself)
            def _():
                pltpu.make_async_copy(rsend.at[2 * core], rrecv.at[2 * core], rrecv_sem.at[0]).start()

    def two(kind, carry):
        answer(0, [(0, kind), (1, kind)])
        return carry

    def four(source, carry):
        answer(source, [(0, 0), (1, 0), (0, 1), (1, 1)])
        return carry

    lax.fori_loop(0, 2, two, 0)
    lax.fori_loop(1, layers, four, 0)

    near, far = rrecv.at[pl.ds(0, 4 * most)], rrecv.at[pl.ds(4 * most, n - 4 * most)]
    pltpu.make_async_copy(near, near, rrecv_sem.at[0]).wait()
    answers = jnp.concatenate(pieces(near[...].reshape(4 * most * SUB, LANES), 2), axis=1)
    found = mxu(answers, jnp.concatenate([placed, placed], axis=0))
    both_ends = jnp.zeros((SUB, tracers), f32)
    for i in range(4 * most):
        both_ends = jnp.where(rel == i, found[SUB * i : SUB * (i + 1)], both_ends)
    pltpu.make_async_copy(far, far, rrecv_sem.at[1]).wait()
    parts = []
    for b in range(blocks):
        block = slice(b * LANES, (b + 1) * LANES)
        part, place = both_ends[:, block], jnp.broadcast_to(slot[:, block], (SUB, LANES))
        for i in range(4 * most, n):
            one = jnp.take_along_axis(rrecv[i], place, axis=1, mode="promise_in_bounds")
            part = jnp.where(rel[:, block] == i, one, part)
        parts.append(part)
    both_ends = jnp.concatenate(parts, axis=1)
    f0 = fracs[0:1]
    sampled = [both_ends[f : f + 1] * (1.0 - f0) + both_ends[4 + f : 5 + f] * f0 for f in range(3)]
    coag = h * sampled[0] * jnp.sqrt(sampled[1])
    shat = h * sampled[2] * sampled[1]
    for section in range(STEPS):
        if section:
            out = mxu(both, tall(dist))
            dot, broken = out[:bins], out[bins:]
            back = mxu(moved, tall(dist * dot))
        active = steps >= section + 1
        c, s = jnp.where(active, coag, 0.0), jnp.where(active, shat, 0.0)
        dist = ((dist + s * broken) + c * back) * (1.0 / ((1.0 + s) + c * dot))
    out_ref[...] = dist
    some = rsend.at[pl.ds(1, n - 1)]
    pltpu.make_async_copy(some, some, local_sem.at[0]).wait()

    @pl.when(gives == 1)
    def _():
        handed, own = send.at[pl.ds(4, n - 4)], send.at[pl.ds(0, 4)]
        pltpu.make_async_copy(handed, handed, local_sem.at[5]).wait()
        pltpu.make_async_copy(own, own, local_sem.at[6]).wait()

    @pl.when(gives == 0)
    def _():
        own = send.at[pl.ds(1, n - 1)]
        pltpu.make_async_copy(own, own, local_sem.at[5]).wait()

    @pl.when(passes == 1)
    def _():
        others = relay.at[pl.ds(0, 2 * (n - 5))]
        pltpu.make_async_copy(others, others, local_sem.at[6]).wait()


def shards(grid, distribution, owner_ids, coords, fracs, counts, kernel, redist, shatter):
    n = lax.axis_size("brick")
    bins, tracers = distribution.shape
    cap = 2 * tracers // n
    assert cap <= HALF and n >= 16 and n & (n - 1) == 0 and tracers % LANES == 0
    f32, i32 = jnp.float32, jnp.int32
    cells = jnp.swapaxes(grid.reshape(grid.shape[0], -1, LANES), 0, 1)
    operands = (
        owner_ids.reshape(1, tracers), coords, fracs, cells, counts.reshape(1, tracers),
        distribution, kernel, redist, shatter,
    )
    dma = pltpu.SemaphoreType.DMA
    return pl.pallas_call(
        lambda *refs: pl.run_scoped(functools.partial(fused, n, cap, *refs), dma((7,))),
        out_shape=jax.ShapeDtypeStruct((bins, tracers), f32),
        in_specs=[pl.BlockSpec(memory_space=pltpu.HBM)] * len(operands),
        out_specs=pl.BlockSpec(memory_space=pltpu.VMEM),
        scratch_shapes=[
            pltpu.VMEM((1, tracers), i32),
            pltpu.VMEM(coords.shape, i32),
            pltpu.VMEM(fracs.shape, f32),
            pltpu.VMEM((1, tracers), i32),
            pltpu.VMEM(distribution.shape, f32),
            pltpu.VMEM((3, *kernel.shape), f32),
            pltpu.VMEM((cells.shape[0], SUB, LANES), f32),
            pltpu.VMEM((n, SUB, LANES), f32),
            pltpu.VMEM((2 * n, SUB, LANES), f32),
            pltpu.VMEM((n, SUB, LANES), f32),
            pltpu.VMEM((TEAM, cap, SUB), i32),
            pltpu.VMEM((TEAM, cap, LANES), f32),
            pltpu.VMEM((TEAM, cap, LANES), f32),
            pltpu.VMEM((n, SUB, LANES), f32),
            pltpu.VMEM((n, SUB, LANES), f32),
            dma((4,)), dma((n // 4 + 1,)), dma((2,)),
        ],
        compiler_params=pltpu.CompilerParams(
            collective_id=0, has_side_effects=True, vmem_limit_bytes=32 * 1024 * 1024
        ),
        name="fused",
    )(*[pltpu.with_memory_space_constraint(x, pltpu.HBM) for x in operands])


def solution(mesh):
    in_specs = (
        P(None, ("runs", "brick")),
        P(None, ("runs", "brick")),
        P(("runs", "brick"), None),
        P(None, ("runs", "brick")),
        P(None, ("runs", "brick")),
        P(("runs", "brick")),
        P(),
        P(),
        P(),
    )
    out_specs = P(None, ("runs", "brick"))
    return jax.shard_map(shards, mesh=mesh, in_specs=in_specs, out_specs=out_specs, check_vma=False)
```
